32 devices in a mesh: flow: 8 (over z, x), grad: 4 (over y, core).
Axes of the slice: x: 2, y: 2, z: 4, core: 2. Of those that a mesh axis runs over, the one named last changes fastest.
Arguments:
- populations: float32 [19, 64, 32, 128], P(None, 'flow', 'grad'), may hold values from 0.008 to 1.01, as said below
- le_offset: int32 [1], replicated, may hold values from 0 to 63
- sphere_velocity: float32 [3, 8, 4, 64], P(None, 'flow', 'grad'), may hold values from -0.4 to 0.4
- link_cell: int32 [8, 4, 16384], P('flow', 'grad'), may hold values from 0 to 8191, as said below
- link_dir: int32 [8, 4, 16384], P('flow', 'grad'), may hold values from 1 to 18, as said below
- link_sphere: int32 [8, 4, 16384], P('flow', 'grad'), may hold values from 0 to 575
- link_count: int32 [8, 4], P('flow', 'grad'), may hold values from 4096 to 16384, as said below
- pair_first: int32 [8, 4, 256], P('flow', 'grad'), may hold values from 0 to 63
- pair_second: int32 [8, 4, 256], P('flow', 'grad'), may hold values from 0 to 575
- pair_count: int32 [8, 4], P('flow', 'grad'), may hold values from 64 to 256, as said below
- pair_gap: float32 [8, 4, 256], P('flow', 'grad'), may hold values from 0.02 to 1
- pair_normal: float32 [3, 8, 4, 256], P(None, 'flow', 'grad'), may hold values from -1 to 1
Outputs:
- populations_next: float32 [19, 64, 32, 128], P(None, 'flow', 'grad')
- sphere_force: float32 [3, 8, 4, 64], P(None, 'flow', 'grad')
- velocity_next: float32 [3, 8, 4, 64], P(None, 'flow', 'grad')
The draws below stay inside these ranges and needn't reach their ends.
Inputs may be any that keep to these rules, and one draw needn't show every extreme that they name: `populations`: each population lies between 0.3 and 3 times its direction's lattice weight. `link_cell`: local cell numbers (x_local * 8 + y_local) * 128 + z; within one tile no two link slots name the same cell and direction, and a cell may carry several links. `link_dir`: within one tile no two link slots name the same cell and direction. Live links of a tile are its first link_count slots; in every draw some tile has all 16384 slots live. Live pairs of a tile are its first pair_count slots; in every draw some tile has all 256 slots live.
All inputs are finite; a program needn't handle non-finite values.
Results may differ from the reference program's by a relative error of at most 0.0003.
Values sent between devices are 32-bit elements; how exact they have to be, the bound alone decides.
No kernel may reach another device: no remote copies, remote signals or barrier semaphores. Data moves between devices by JAX's collectives and lax.ppermute only.
A program may use at most 64 MiB of HBM per device.

```python
import math
import jax
import jax.numpy as jnp
from jax import lax

CX = 8
CY = 8
NZ = 128
LINKS_DEV = 16384
SPH_DEV = 64
PAIRS_DEV = 256
NX = 64
NY = 32
N_FLOW = 8
N_GRAD = 4


LATTICE_WEIGHTS = [1.0 / 3.0] + [1.0 / 18.0] * 6 + [1.0 / 36.0] * 12


def draw_populations(key, part):
    shape = (19, NX, NY, NZ)
    weights = jnp.asarray(LATTICE_WEIGHTS, jnp.float32).reshape(19, 1, 1, 1)
    factor = jnp.exp(jax.random.uniform(key, shape, jnp.float32, math.log(0.3), math.log(3.0)))
    return weights * factor


def link_codes(key):
    tiles = N_FLOW * N_GRAD
    keys = jax.random.split(jax.random.fold_in(key, 11), tiles)

    def one_tile(single):
        return jax.random.permutation(single, 18 * CX * CY * NZ)[:LINKS_DEV]
    picked_codes = lax.map(one_tile, keys)
    return picked_codes.reshape(N_FLOW, N_GRAD, LINKS_DEV).astype(jnp.int32)


def draw_link_cell(key, part):
    return link_codes(key) // 18


def draw_link_dir(key, part):
    return link_codes(key) % 18 + 1


def full_counts(key, largest):
    tiles = N_FLOW * N_GRAD
    counts = jax.random.randint(key, (tiles,), largest // 4, largest + 1, jnp.int32)
    chosen = jax.random.randint(jax.random.fold_in(key, 7), (), 0, tiles)
    return counts.at[chosen].set(largest).reshape(N_FLOW, N_GRAD)


def draw_link_count(key, part):
    return full_counts(jax.random.fold_in(key, 21), LINKS_DEV)


def draw_pair_count(key, part):
    return full_counts(jax.random.fold_in(key, 31), PAIRS_DEV)


def draw_pair_normal(key, part):
    shape = (N_FLOW, N_GRAD, PAIRS_DEV)
    polar = jnp.arccos(jax.random.uniform(jax.random.fold_in(key, 41), shape, jnp.float32, -1.0, 1.0))
    azimuth = jax.random.uniform(jax.random.fold_in(key, 42), shape, jnp.float32, -math.pi, math.pi)
    return jnp.stack([jnp.sin(polar) * jnp.cos(azimuth), jnp.sin(polar) * jnp.sin(azimuth), jnp.cos(polar)])


def plant(entries, own_key, least, high):
    dims = entries.shape
    place = [jax.random.randint(jax.random.fold_in(own_key, axis), (), 0, dims[axis]) for axis in range(len(dims))]
    entries = entries.at[tuple(place)].set(least)
    longest = dims.index(max(dims))
    place[longest] = (place[longest] + 1) % dims[longest]
    return entries.at[tuple(place)].set(high)


def shard_levels(own_key, extent, shards, smallest, high):
    def one(position, shards_of):
        steps = jax.random.uniform(jax.random.fold_in(jax.random.fold_in(own_key, 6), position), (shards_of,), jnp.float32, smallest / len(shards), high / len(shards))
        return jnp.repeat(jnp.exp(steps), extent[position] // shards_of).reshape((-1,) + (1,) * (len(extent) - position - 1))

    loudness = one(*shards[0])
    for cut in shards[1:]:
        loudness = loudness * one(*cut)
    return loudness


def bell_draw(rng, extent, scale, bound, cuts=(), held_as=jnp.bfloat16):
    drawn = scale * jax.random.normal(rng, extent, jnp.float32)
    if cuts:
        drawn = drawn * shard_levels(rng, extent, cuts, -0.22, 0.18)
    return jnp.clip(drawn, -bound, bound).astype(held_as)


def setup_inputs(seed: int = 0) -> dict:
    arg_keys = jax.random.split(jax.random.key(seed), 13)
    return {
        "populations": draw_populations(jax.random.fold_in(arg_keys[12], 71), 0),
        "le_offset": jax.random.randint(arg_keys[1], (1,), 0, NX).astype(jnp.int32),
        "sphere_velocity": bell_draw(arg_keys[2], (3, N_FLOW, N_GRAD, SPH_DEV), 0.1, 0.4, ((1, 8), (2, 4)), jnp.float32),
        "link_cell": draw_link_cell(jax.random.fold_in(arg_keys[12], 71), 0),
        "link_dir": draw_link_dir(jax.random.fold_in(arg_keys[12], 71), 0),
        "link_sphere": plant(jax.random.randint(arg_keys[5], (N_FLOW, N_GRAD, LINKS_DEV), 0, 9 * SPH_DEV), jax.random.fold_in(arg_keys[5], 1), 0, (9 * SPH_DEV) - 1).astype(jnp.int32),
        "link_count": draw_link_count(jax.random.fold_in(arg_keys[12], 71), 0),
        "pair_first": plant(jax.random.randint(arg_keys[7], (N_FLOW, N_GRAD, PAIRS_DEV), 0, SPH_DEV), jax.random.fold_in(arg_keys[7], 1), 0, SPH_DEV - 1).astype(jnp.int32),
        "pair_second": plant(jax.random.randint(arg_keys[8], (N_FLOW, N_GRAD, PAIRS_DEV), 0, 9 * SPH_DEV), jax.random.fold_in(arg_keys[8], 1), 0, (9 * SPH_DEV) - 1).astype(jnp.int32),
        "pair_count": draw_pair_count(jax.random.fold_in(arg_keys[12], 71), 0),
        "pair_gap": jnp.clip(0.02 + 0.98 * jax.random.uniform(arg_keys[10], (N_FLOW, N_GRAD, PAIRS_DEV), jnp.float32) ** shard_levels(arg_keys[10], (N_FLOW, N_GRAD, PAIRS_DEV), ((0, 8), (1, 4)), -0.2, 0.2), 0.02, 1.0),
        "pair_normal": draw_pair_normal(jax.random.fold_in(arg_keys[12], 71), 0),
    }


VELOCITIES = [(0, 0, 0), (1, 0, 0), (-1, 0, 0), (0, 1, 0), (0, -1, 0), (0, 0, 1), (0, 0, -1), (1, 1, 0), (-1, -1, 0), (1, -1, 0), (-1, 1, 0), (1, 0, 1), (-1, 0, -1), (1, 0, -1), (-1, 0, 1), (0, 1, 1), (0, -1, -1), (0, 1, -1), (0, -1, 1)]
WEIGHTS = [1.0 / 3.0] + [1.0 / 18.0] * 6 + [1.0 / 36.0] * 12
RELAX_TIME = 0.8
SHEAR_SPEED = 0.1
LUB_COEF = 0.5
GAP_FLOOR = 0.1
GAP_CUTOFF = 1.0
INV_MASS = 1.0 / 523.6


def collide(populations):
    density = jnp.sum(populations, axis=0)
    speeds = []
    for axis_id in range(3):
        running = None
        for direction, vector in enumerate(VELOCITIES):
            if vector[axis_id] != 0:
                addend = vector[axis_id] * populations[direction]
                running = addend if running is None else running + addend
        speeds.append(running / density)
    speed_sq = speeds[0] * speeds[0] + speeds[1] * speeds[1] + speeds[2] * speeds[2]
    relaxed = []
    for direction, vector in enumerate(VELOCITIES):
        c_dot = None
        for axis_id in range(3):
            if vector[axis_id] != 0:
                addend = vector[axis_id] * speeds[axis_id]
                c_dot = addend if c_dot is None else c_dot + addend
        if c_dot is None:
            equil = WEIGHTS[direction] * density * (1.0 - 1.5 * speed_sq)
        else:
            equil = WEIGHTS[direction] * density * (1.0 + 3.0 * c_dot + 4.5 * c_dot * c_dot - 1.5 * speed_sq)
        current = populations[direction]
        relaxed.append(current - (current - equil) / RELAX_TIME)
    return relaxed, density


def tile_links(relaxed, density, propagated, near_speed, link_cell, link_dir, link_sphere, link_count, pair_first, pair_second, pair_count, pair_gap, pair_normal):
    n_cells = relaxed.shape[1]
    slot_count = near_speed.shape[1] // 9
    onehot = (link_dir[None, :] == lax.iota(jnp.int32, 19)[:, None]).astype(relaxed.dtype)
    lookup = jnp.asarray([[vector[k] for vector in VELOCITIES] for k in range(3)] + [WEIGHTS], relaxed.dtype)
    picked = jnp.dot(lookup, onehot, precision=lax.Precision.HIGHEST)
    leaving = jnp.sum(onehot * relaxed[:, link_cell], axis=0)
    wall_speed = near_speed[:, link_sphere]
    c_dot_u = jnp.sum(picked[:3] * wall_speed, axis=0)
    bounced = leaving - 6.0 * picked[3] * density[link_cell] * c_dot_u
    is_live = lax.iota(jnp.int32, link_dir.shape[0]) < link_count
    opposite = jnp.where(link_dir % 2 == 1, link_dir + 1, link_dir - 1)
    target = jnp.where(is_live, opposite * n_cells + link_cell, 19 * n_cells)
    updated = propagated.reshape(-1).at[target].set(bounced, mode="drop").reshape(19, n_cells)
    link_force = picked[:3] * (leaving + bounced) * is_live.astype(relaxed.dtype)
    pair_live = (lax.iota(jnp.int32, pair_first.shape[0]) < pair_count).astype(relaxed.dtype)
    first_ref = pair_first + 4 * slot_count
    first_speed = near_speed[:, first_ref]
    second_speed = near_speed[:, pair_second]
    normal_rate = jnp.sum((first_speed - second_speed) * pair_normal, axis=0)
    resist = LUB_COEF * (1.0 / jnp.maximum(pair_gap, GAP_FLOOR) - 1.0 / GAP_CUTOFF)
    lubrication = -resist * normal_rate * pair_normal * pair_live
    sphere_refs = jnp.concatenate([link_sphere, first_ref, pair_second])
    values = jnp.concatenate([link_force, lubrication, -lubrication], axis=1)
    partial_value = jax.ops.segment_sum(values.T, sphere_refs, num_segments=9 * slot_count).T
    return updated, partial_value


def reference(populations, le_offset, sphere_velocity, link_cell, link_dir, link_sphere, link_count, pair_first, pair_second, pair_count, pair_gap, pair_normal):
    relaxed, density = collide(populations)
    offset_cells = le_offset[0]
    moved = []
    for direction, vector in enumerate(VELOCITIES):
        layer = relaxed[direction]
        boost = 6.0 * WEIGHTS[direction] * vector[0] * SHEAR_SPEED
        below = jnp.roll(layer[:, NY - 1, :], -offset_cells, axis=0) - boost
        above = jnp.roll(layer[:, 0, :], offset_cells, axis=0) + boost
        padded = jnp.concatenate([below[:, None, :], layer, above[:, None, :]], axis=1)
        rows_kept = padded[:, 1 - vector[1]:1 - vector[1] + NY, :]
        moved.append(jnp.roll(rows_kept, (vector[0], vector[2]), axis=(0, 2)))
    tiles = N_FLOW * N_GRAD
    cells_tile = CX * CY * NZ

    def to_tiles(field, count):
        return field.reshape(count, N_FLOW, CX, N_GRAD, CY, NZ).transpose(1, 3, 0, 2, 4, 5).reshape(tiles, count, cells_tile)

    relaxed_tiles = to_tiles(jnp.stack(relaxed), 19)
    moved_tiles = to_tiles(jnp.stack(moved), 19)
    density_tiles = to_tiles(density[None], 1)[:, 0]
    rolled = []
    for code in range(9):
        rolled.append(jnp.roll(sphere_velocity, (1 - code // 3, 1 - code % 3), axis=(1, 2)))
    near_speed = jnp.stack(rolled).transpose(2, 3, 1, 0, 4).reshape(tiles, 3, 9 * SPH_DEV)
    inputs = (relaxed_tiles, density_tiles, moved_tiles, near_speed,
              link_cell.reshape(tiles, LINKS_DEV), link_dir.reshape(tiles, LINKS_DEV),
              link_sphere.reshape(tiles, LINKS_DEV), link_count.reshape(tiles),
              pair_first.reshape(tiles, PAIRS_DEV), pair_second.reshape(tiles, PAIRS_DEV),
              pair_count.reshape(tiles), pair_gap.reshape(tiles, PAIRS_DEV),
              pair_normal.transpose(1, 2, 0, 3).reshape(tiles, 3, PAIRS_DEV))
    updated, partials = lax.map(lambda pieces: tile_links(*pieces), inputs)
    populations_next = updated.reshape(N_FLOW, N_GRAD, 19, CX, CY, NZ).transpose(2, 0, 3, 1, 4, 5).reshape(19, NX, NY, NZ)
    partials = partials.reshape(N_FLOW, N_GRAD, 3, 9, SPH_DEV)
    accumulated = None
    for code in range(9):
        addend = jnp.roll(partials[:, :, :, code], (code // 3 - 1, code % 3 - 1), axis=(0, 1))
        accumulated = addend if accumulated is None else accumulated + addend
    sphere_force = accumulated.transpose(2, 0, 1, 3)
    velocity_next = sphere_velocity + INV_MASS * sphere_force
    return populations_next, sphere_force, velocity_next
```

```python
import functools

import jax
import jax.numpy as jnp
from jax import lax
from jax.experimental import pallas as pl
from jax.experimental.pallas import tpu as pltpu
from jax.sharding import PartitionSpec as P

VELOCITIES = [
    (0, 0, 0),
    (1, 0, 0),
    (-1, 0, 0),
    (0, 1, 0),
    (0, -1, 0),
    (0, 0, 1),
    (0, 0, -1),
    (1, 1, 0),
    (-1, -1, 0),
    (1, -1, 0),
    (-1, 1, 0),
    (1, 0, 1),
    (-1, 0, -1),
    (1, 0, -1),
    (-1, 0, 1),
    (0, 1, 1),
    (0, -1, -1),
    (0, 1, -1),
    (0, -1, 1),
]
WEIGHTS = [1.0 / 3.0] + [1.0 / 18.0] * 6 + [1.0 / 36.0] * 12
UPWARD = [3, 7, 10, 15, 17]
DOWNWARD = [4, 8, 9, 16, 18]
RIGHTWARD = [1, 7, 9, 11, 13]
LEFTWARD = [2, 8, 10, 12, 14]
RELAX_TIME = 0.8
SHEAR_SPEED = 0.1
LUB_COEF = 0.5
GAP_FLOOR = 0.1
GAP_CUTOFF = 1.0
INV_MASS = 1.0 / 523.6
LANES = 128
SUBS = 8
NEAR = 9
NO_LINK = 1e30
BF16 = jnp.bfloat16
F32 = jnp.float32
NT = (((1,), (1,)), ((), ()))

VMEM = pl.BlockSpec(memory_space=pltpu.VMEM)
SMEM = pl.BlockSpec(memory_space=pltpu.SMEM)


def collide_kernel(pops, speed, relaxed, density, right_msg, left_msg):
    width_x, width_y = pops.shape[1], pops.shape[2]
    slots = speed.shape[3]
    for x in range(width_x):
        current = [pops[d, x] for d in range(19)]
        total = functools.reduce(lambda p, q: p + q, current)
        density[x] = total
        inverse = 1.0 / total
        speeds = []
        for axis_id in range(3):
            running = None
            for direction, vector in enumerate(VELOCITIES):
                if vector[axis_id] == 0:
                    continue
                if running is None:
                    running = current[direction]
                elif vector[axis_id] > 0:
                    running = running + current[direction]
                else:
                    running = running - current[direction]
            speeds.append(running * inverse)
        base = 1.0 - 1.5 * (
            speeds[0] * speeds[0] + speeds[1] * speeds[1] + speeds[2] * speeds[2]
        )
        for direction, vector in enumerate(VELOCITIES):
            c_dot = None
            for axis_id in range(3):
                if vector[axis_id] != 0:
                    addend = vector[axis_id] * speeds[axis_id]
                    c_dot = addend if c_dot is None else c_dot + addend
            shape = base if c_dot is None else base + c_dot * (3.0 + 4.5 * c_dot)
            equil = WEIGHTS[direction] * total * shape
            value = current[direction] - (current[direction] - equil) * (1.0 / RELAX_TIME)
            relaxed[direction, x] = value
            if x == width_x - 1 and direction in RIGHTWARD:
                right_msg[RIGHTWARD.index(direction)] = value
            if x == 0 and direction in LEFTWARD:
                left_msg[LEFTWARD.index(direction)] = value
            if direction in UPWARD:
                left_msg[5 + UPWARD.index(direction), x : x + 1, :] = value[width_y - 1 :, :]
            if direction in DOWNWARD:
                right_msg[5 + DOWNWARD.index(direction), x : x + 1, :] = value[:1, :]
    right_msg[10] = jnp.zeros((SUBS, LANES), F32)
    left_msg[10] = jnp.zeros((SUBS, LANES), F32)
    for k in range(3):
        row = speed[k, 0]
        twice = jnp.concatenate([row] * (LANES // slots), axis=1)
        right_msg[10, k : k + 1, :] = twice
        left_msg[10, k : k + 1, :] = twice


def prepare_kernel(shift, own_right, own_left, from_left, from_right, up_msg, down_msg, own_speed, rows):
    width_x = own_right.shape[1]
    up_rest, down_rest = shift[0], shift[1]
    top_edge, bottom_edge = shift[2], shift[3]
    for j, direction in enumerate(UPWARD):
        step = VELOCITIES[direction][0]
        boost = 6.0 * WEIGHTS[direction] * step * SHEAR_SPEED
        rows[j, SUBS : 2 * SUBS] = own_left[5 + j]
        rows[j, 2 * SUBS : 3 * SUBS] = from_right[5 + j]
        if step > 0:
            slab = from_left[RIGHTWARD.index(direction)]
            rows[j, SUBS - 1 : SUBS] = slab[SUBS - 1 :, :]
        moved = rows[j, pl.ds(SUBS - step + up_rest, width_x), :]
        if step != 0:
            moved = moved - boost * top_edge.astype(F32)
        up_msg[j] = moved
    for j, direction in enumerate(DOWNWARD):
        step = VELOCITIES[direction][0]
        boost = 6.0 * WEIGHTS[direction] * step * SHEAR_SPEED
        rows[5 + j, :SUBS] = from_left[5 + j]
        rows[5 + j, SUBS : 2 * SUBS] = own_right[5 + j]
        if step < 0:
            slab = from_right[LEFTWARD.index(direction)]
            rows[5 + j, 2 * SUBS : 2 * SUBS + 1] = slab[:1, :]
        moved = rows[5 + j, pl.ds(SUBS - step - down_rest, width_x), :]
        if step != 0:
            moved = moved + boost * bottom_edge.astype(F32)
        down_msg[j] = moved
    three = [from_left[10], own_right[10], from_right[10]]
    for out, first in ((up_msg, 5), (down_msg, 5), (own_speed, 0)):
        for f in range(3):
            for k in range(3):
                row = 3 * f + k
                out[first + row // SUBS, row % SUBS : row % SUBS + 1, :] = three[f][k : k + 1, :]


def to_bf16(value):
    return value.astype(F32).astype(BF16)


def mark_kernel(count, cell, direction, sphere, marks):
    step = pl.program_id(0)
    width = cell.shape[2]
    half_rows = marks.shape[0]
    q = cell[0]
    ref = sphere[0]
    row = (direction[0] - 1) * (2 * half_rows // 18) + q // LANES
    z = q % LANES
    half = (row >= half_rows).astype(jnp.int32)
    row = row - half * half_rows
    number = step * width + lax.broadcasted_iota(jnp.int32, (1, width), 1)
    level = ref // LANES
    scale = jnp.where(level == 0, 1.0, 0.0)
    for t in range(1, 5):
        scale = jnp.where(level == t, 2.0 ** (8 * t), scale)
    code = jnp.where(number < count[0, 0], (LANES + ref % LANES).astype(F32) * scale, 0.0)
    block = half_rows // 3
    parts = []
    for first in range(0, half_rows, block):
        local = row - first
        local = to_bf16(jnp.where((local >= 0) & (local < block), local, 255))
        index = to_bf16(lax.broadcasted_iota(jnp.int32, (block, width), 0))
        parts.append(
            jnp.where(
                index == jnp.broadcast_to(local, (block, width)), jnp.ones((), BF16), jnp.zeros((), BF16)
            )
        )
    rows_hot = jnp.concatenate(parts, axis=0)
    column = to_bf16(z + LANES * half)
    index = to_bf16(lax.broadcasted_iota(jnp.int32, (2 * LANES, width), 0))
    columns = jnp.where(
        index == jnp.broadcast_to(column, (2 * LANES, width)),
        jnp.broadcast_to(code.astype(BF16), (2 * LANES, width)),
        jnp.zeros((), BF16),
    )
    part = lax.dot_general(rows_hot, columns, NT, preferred_element_type=F32)

    @pl.when(step == 0)
    def _():
        marks[...] = part

    @pl.when(step > 0)
    def _():
        marks[...] += part


def split(value):
    high = value.astype(BF16)
    return high, (value - high.astype(F32)).astype(BF16)


def force_kernel(
    pair_count,
    relaxed,
    density,
    marks,
    own_speed,
    below_speed,
    above_speed,
    pair_first,
    pair_second,
    pair_gap,
    pair_normal,
    bounced,
    parts,
    link_table,
    first_of,
    second_of,
    value_of,
    sums,
):
    width_x = relaxed.shape[1]
    slots = LANES // 2
    half_rows = marks.shape[0]
    lane = lax.broadcasted_iota(jnp.int32, (1, LANES), 1)
    sources = [below_speed, own_speed, above_speed]

    def speed_row(code, k):
        row = 3 * (code // 3) + k
        source = sources[code % 3]
        first = 0 if source is own_speed else 5
        return source[first + row // SUBS, row % SUBS : row % SUBS + 1, :]

    tables = []
    for k in range(3):
        rows = []
        for t in range(5):
            low = speed_row(2 * t, k)
            high = speed_row(min(2 * t + 1, NEAR - 1), k)
            rows.append(jnp.where(lane < slots, low, high))
        tables.append(rows)
    for direction in range(1, 19):
        for t in range(5):
            total = None
            for k in range(3):
                if VELOCITIES[direction][k] != 0:
                    addend = VELOCITIES[direction][k] * tables[k][t]
                    total = addend if total is None else total + addend
            link_table[direction - 1, t : t + 1, :] = total

    index_a = to_bf16(lax.broadcasted_iota(jnp.int32, (48, LANES), 0))
    index_b = to_bf16(lax.broadcasted_iota(jnp.int32, (16, LANES), 0))
    one = jnp.ones((), BF16)
    zero = jnp.zeros((), BF16)

    def hot_rows(first_row, second_row, values):
        a = jnp.broadcast_to(to_bf16(first_row), (48, LANES))
        b = jnp.broadcast_to(to_bf16(second_row), (16, LANES))
        left = jnp.where(index_a == a, one, zero)
        mask = index_b == b
        right = []
        for value in values:
            high, low = split(value)
            right.append(
                jnp.concatenate(
                    [
                        jnp.where(mask, jnp.broadcast_to(high, (16, LANES)), zero),
                        jnp.where(mask, jnp.broadcast_to(low, (16, LANES)), zero),
                    ],
                    axis=0,
                )
            )
        return left, right

    def group(g, carry):
        for side in range(2):
            index = 2 * g + side
            half = index // 9
            first_row = (index - 9 * half) * (2 * half_rows // 18)
            weight6 = jnp.where(index < 6, 6.0 * WEIGHTS[1], 6.0 * WEIGHTS[7]).astype(F32)
            lookup = [
                jnp.broadcast_to(link_table[index, t : t + 1, :], (SUBS, LANES)) for t in range(5)
            ]
            for x in range(width_x):
                mark = marks[
                    pl.ds(pl.multiple_of(first_row + SUBS * x, SUBS), SUBS),
                    pl.ds(pl.multiple_of(half * LANES, LANES), LANES),
                ]
                live = mark > 0.0
                scaled = mark
                level = jnp.zeros((SUBS, LANES), F32)
                for t in range(1, 5):
                    above = mark > 2.0 ** (8 * t + 6)
                    scaled = jnp.where(above, mark * 2.0 ** (-8 * t), scaled)
                    level = jnp.where(above, float(t), level)
                place = jnp.where(live, scaled - float(LANES), 0.0).astype(jnp.int32)
                speed = jnp.take_along_axis(lookup[0], place, axis=1)
                for t in range(1, 5):
                    found = jnp.take_along_axis(lookup[t], place, axis=1)
                    speed = jnp.where(level == float(t), found, speed)
                leaving = relaxed[index + 1, x]
                back = leaving - weight6 * density[x] * speed
                bounced[index, x] = jnp.where(live, back, NO_LINK)
                force = leaving + back
                if side == 1:
                    force = -force
                high_part = place // 16
                first = jnp.where(live, level * 8.0 + high_part.astype(F32), -1.0)
                second = (place - 16 * high_part).astype(F32)
                where = side * width_x * SUBS + SUBS * x
                first_of[where : where + SUBS] = first
                second_of[where : where + SUBS] = second
                value_of[where : where + SUBS] = jnp.where(live, force, 0.0)
        lefts, rights = [], []
        for r in range(2 * width_x * SUBS):
            left, right = hot_rows(
                first_of[r : r + 1], second_of[r : r + 1], [value_of[r : r + 1]]
            )
            lefts.append(left)
            rights.append(right[0])
        sums[g] = lax.dot_general(
            jnp.concatenate(lefts, axis=1),
            jnp.concatenate(rights, axis=1),
            NT,
            preferred_element_type=F32,
        )
        return carry

    lax.fori_loop(0, 9, group, 0)

    totals = []
    for k in range(3):
        total = None
        for g in range(9):
            c = VELOCITIES[2 * g + 1][k]
            if c == 0:
                continue
            if total is None:
                total = sums[g] if c > 0 else -sums[g]
            else:
                total = total + sums[g] if c > 0 else total - sums[g]
        totals.append(total)

    pairs = pair_first.shape[2]
    lefts = []
    rights = [[], [], []]
    for start in range(0, pairs, LANES):
        here = slice(start, start + LANES)
        first = pair_first[0, :, here]
        second = pair_second[0, :, here]
        first_wide = jnp.broadcast_to(first, (SUBS, LANES))
        place = jnp.broadcast_to(second % LANES, (SUBS, LANES))
        level = second // LANES
        gap = pair_gap[0, :, here]
        rate = None
        for k in range(3):
            table = jnp.broadcast_to(tables[k][2], (SUBS, LANES))
            first_speed = jnp.take_along_axis(table, first_wide, axis=1)[:1]
            second_speed = None
            for t in range(5):
                table = jnp.broadcast_to(tables[k][t], (SUBS, LANES))
                found = jnp.take_along_axis(table, place, axis=1)[:1]
                second_speed = found if t == 0 else jnp.where(level == t, found, second_speed)
            addend = (first_speed - second_speed) * pair_normal[k, 0, :, here]
            rate = addend if rate is None else rate + addend
        resist = LUB_COEF * (1.0 / jnp.maximum(gap, GAP_FLOOR) - 1.0 / GAP_CUTOFF)
        number = start + lane
        factor = jnp.where(number < pair_count[0, 0], -resist * rate, 0.0)
        values = [factor * pair_normal[k, 0, :, here] for k in range(3)]
        first = first + 4 * slots
        for ref, these in ((first, values), (second, [-v for v in values])):
            left, right = hot_rows(ref // 16, ref % 16, these)
            lefts.append(left)
            for k in range(3):
                rights[k].append(right[k])
    left = jnp.concatenate(lefts, axis=1)
    for k in range(3):
        total = totals[k] + lax.dot_general(
            left, jnp.concatenate(rights[k], axis=1), NT, preferred_element_type=F32
        )
        value = total[:, :16] + total[:, 16:32]
        first_of[0:48] = jnp.concatenate([value, jnp.zeros((48, LANES - 16), F32)], axis=1)
        line = None
        for s in range(4):
            piece = first_of[pl.ds(s, NEAR, stride=4), :]
            if s:
                piece = pltpu.roll(piece, 16 * s, axis=1)
            line = piece if line is None else line + piece
        for code in range(NEAR):
            row = 3 * (code % 3) + k
            parts[code // 3, row : row + 1, :] = line[code : code + 1]


def stream_kernel(relaxed, bounced, from_left, from_right, below, above, out):
    width_x, width_y = relaxed.shape[1], relaxed.shape[2]
    for direction, (cx, cy, cz) in enumerate(VELOCITIES):
        for x in range(width_x):
            source = x - cx
            if source < 0:
                tile = from_left[RIGHTWARD.index(direction)]
            elif source >= width_x:
                tile = from_right[LEFTWARD.index(direction)]
            else:
                tile = relaxed[direction, source]
            if cy != 0:
                tile = pltpu.roll(tile, cy % width_y, axis=0)
                row = lax.broadcasted_iota(jnp.int32, tile.shape, 0)
                if cy > 0:
                    ghost = below[UPWARD.index(direction), x : x + 1, :]
                    tile = jnp.where(row == 0, jnp.broadcast_to(ghost, tile.shape), tile)
                else:
                    ghost = above[DOWNWARD.index(direction), x : x + 1, :]
                    tile = jnp.where(row == width_y - 1, jnp.broadcast_to(ghost, tile.shape), tile)
            if cz != 0:
                tile = pltpu.roll(tile, cz % LANES, axis=1)
            if direction > 0:
                opposite = direction + 1 if direction % 2 == 1 else direction - 1
                back = bounced[opposite - 1, x]
                tile = jnp.where(back < 0.5 * NO_LINK, back, tile)
            out[direction, x] = tile


def send(block, axis, distance):
    count = lax.axis_size(axis)
    return lax.ppermute(block, axis, [(i, (i + distance) % count) for i in range(count)])


def shape_of(*dims):
    return jax.ShapeDtypeStruct(dims, F32)


def per_device(
    populations,
    le_offset,
    sphere_velocity,
    link_cell,
    link_dir,
    link_sphere,
    link_count,
    pair_first,
    pair_second,
    pair_count,
    pair_gap,
    pair_normal,
):
    width_x, width_y, depth = populations.shape[1:]
    slots = sphere_velocity.shape[3]
    links = link_cell.shape[2]
    flow_count = lax.axis_size("flow")
    grad_count = lax.axis_size("grad")
    grad_index = lax.axis_index("grad")
    assert depth == LANES and width_y == SUBS and width_x == SUBS and 2 * slots == LANES

    relaxed, density, right_msg, left_msg = pl.pallas_call(
        collide_kernel,
        name="collide",
        in_specs=[VMEM, VMEM],
        out_specs=[VMEM] * 4,
        out_shape=[
            shape_of(19, width_x, width_y, depth),
            shape_of(width_x, width_y, depth),
            shape_of(11, SUBS, LANES),
            shape_of(11, SUBS, LANES),
        ],
    )(populations, sphere_velocity)

    from_left = send(right_msg, "flow", 1)
    from_right = send(left_msg, "flow", -1)

    half_rows = 9 * width_x * width_y
    width = links // 4
    link_spec = pl.BlockSpec((1, 1, width), lambda i: (0, 0, i))
    marks = pl.pallas_call(
        mark_kernel,
        name="mark",
        grid=(links // width,),
        in_specs=[SMEM, link_spec, link_spec, link_spec],
        out_specs=pl.BlockSpec((half_rows, 2 * LANES), lambda i: (0, 0)),
        out_shape=shape_of(half_rows, 2 * LANES),
    )(link_count, link_cell, link_dir, link_sphere)

    offset = le_offset[0]
    rest = offset % width_x
    at_top = (grad_index == grad_count - 1).astype(jnp.int32)
    at_bottom = (grad_index == 0).astype(jnp.int32)
    shift = jnp.stack([rest * at_top, rest * at_bottom, at_top, at_bottom])
    up_msg, down_msg, own_speed = pl.pallas_call(
        prepare_kernel,
        name="prepare",
        in_specs=[SMEM] + [VMEM] * 4,
        out_specs=[VMEM] * 3,
        out_shape=[shape_of(7, SUBS, LANES), shape_of(7, SUBS, LANES), shape_of(2, SUBS, LANES)],
        scratch_shapes=[pltpu.VMEM((10, 3 * SUBS, LANES), F32)],
    )(shift, right_msg, left_msg, from_left, from_right)

    below = send(up_msg, "grad", 1)
    above = send(down_msg, "grad", -1)

    hops = offset // width_x
    edge = jnp.where(at_bottom == 1, below[:5], above[:5])
    for level in range(max(flow_count - 1, 1).bit_length()):
        route = []
        for a in range(flow_count):
            far = 1 << level
            route.append((a * grad_count, (a - far) % flow_count * grad_count))
            route.append(
                (a * grad_count + grad_count - 1, (a + far) % flow_count * grad_count + grad_count - 1)
            )
        arrived = lax.ppermute(edge, ("flow", "grad"), route)
        edge = jnp.where(hops // (1 << level) % 2 == 1, arrived, edge)
    below_rows = jnp.where(at_bottom == 1, edge, below[:5])
    above_rows = jnp.where(at_top == 1, edge, above[:5])

    bounced, parts = pl.pallas_call(
        force_kernel,
        name="force",
        in_specs=[SMEM] + [VMEM] * 10,
        out_specs=[VMEM] * 2,
        out_shape=[shape_of(18, width_x, width_y, depth), shape_of(3, 2 * SUBS, LANES)],
        scratch_shapes=[
            pltpu.VMEM((18, SUBS, LANES), F32),
            pltpu.VMEM((2 * width_x * SUBS, LANES), F32),
            pltpu.VMEM((2 * width_x * SUBS, LANES), F32),
            pltpu.VMEM((2 * width_x * SUBS, LANES), F32),
            pltpu.VMEM((9, 48, 32), F32),
        ],
    )(
        pair_count,
        relaxed,
        density,
        marks,
        own_speed,
        below,
        above,
        pair_first,
        pair_second,
        pair_gap,
        pair_normal,
    )

    column = parts[1] + send(parts[0], "flow", -1) + send(parts[2], "flow", 1)
    column = column[:9].reshape(3, 3, LANES)
    own_force = column[1] + send(column[0], "grad", -1) + send(column[2], "grad", 1)
    sphere_force = own_force[:, None, None, :slots]
    velocity_next = sphere_velocity + INV_MASS * sphere_force

    updated = pl.pallas_call(
        stream_kernel,
        name="stream",
        in_specs=[VMEM] * 6,
        out_specs=VMEM,
        out_shape=shape_of(19, width_x, width_y, depth),
    )(relaxed, bounced, from_left, from_right, below_rows, above_rows)
    return updated, sphere_force, velocity_next


def solution(mesh):
    in_specs = (
        P(None, "flow", "grad", None),
        P(),
        P(None, "flow", "grad", None),
        P("flow", "grad", None),
        P("flow", "grad", None),
        P("flow", "grad", None),
        P("flow", "grad"),
        P("flow", "grad", None),
        P("flow", "grad", None),
        P("flow", "grad"),
        P("flow", "grad", None),
        P(None, "flow", "grad", None),
    )
    out_specs = (
        P(None, "flow", "grad", None),
        P(None, "flow", "grad", None),
        P(None, "flow", "grad", None),
    )
    return jax.shard_map(
        per_device, mesh=mesh, in_specs=in_specs, out_specs=out_specs, check_vma=False
    )
```

```python
import functools

import jax
import jax.numpy as jnp
from jax import lax
from jax.experimental import pallas as pl
from jax.experimental.pallas import tpu as pltpu
from jax.sharding import PartitionSpec as P

VELOCITIES = [
    (0, 0, 0),
    (1, 0, 0),
    (-1, 0, 0),
    (0, 1, 0),
    (0, -1, 0),
    (0, 0, 1),
    (0, 0, -1),
    (1, 1, 0),
    (-1, -1, 0),
    (1, -1, 0),
    (-1, 1, 0),
    (1, 0, 1),
    (-1, 0, -1),
    (1, 0, -1),
    (-1, 0, 1),
    (0, 1, 1),
    (0, -1, -1),
    (0, 1, -1),
    (0, -1, 1),
]
WEIGHTS = [1.0 / 3.0] + [1.0 / 18.0] * 6 + [1.0 / 36.0] * 12
UPWARD = [3, 7, 10, 15, 17]
DOWNWARD = [4, 8, 9, 16, 18]
RIGHTWARD = [1, 7, 9, 11, 13]
LEFTWARD = [2, 8, 10, 12, 14]
RELAX_TIME = 0.8
SHEAR_SPEED = 0.1
LUB_COEF = 0.5
GAP_FLOOR = 0.1
GAP_CUTOFF = 1.0
INV_MASS = 1.0 / 523.6
LANES = 128
SUBS = 8
NEAR = 9
NO_LINK = 1e30
BF16 = jnp.bfloat16
F32 = jnp.float32
NT = (((1,), (1,)), ((), ()))

VMEM = pl.BlockSpec(memory_space=pltpu.VMEM)


def collide_kernel(pops, speed, relaxed, density, right_msg, left_msg):
    width_x, width_y = pops.shape[1], pops.shape[2]
    slots = speed.shape[3]
    for x in range(width_x):
        current = [pops[d, x] for d in range(19)]
        total = functools.reduce(lambda p, q: p + q, current)
        density[x] = total
        inverse = 1.0 / total
        speeds = []
        for axis_id in range(3):
            running = None
            for direction, vector in enumerate(VELOCITIES):
                if vector[axis_id] == 0:
                    continue
                if running is None:
                    running = current[direction]
                elif vector[axis_id] > 0:
                    running = running + current[direction]
                else:
                    running = running - current[direction]
            speeds.append(running * inverse)
        base = 1.0 - 1.5 * (
            speeds[0] * speeds[0] + speeds[1] * speeds[1] + speeds[2] * speeds[2]
        )
        for direction, vector in enumerate(VELOCITIES):
            c_dot = None
            for axis_id in range(3):
                if vector[axis_id] != 0:
                    addend = vector[axis_id] * speeds[axis_id]
                    c_dot = addend if c_dot is None else c_dot + addend
            shape = base if c_dot is None else base + c_dot * (3.0 + 4.5 * c_dot)
            equil = WEIGHTS[direction] * total * shape
            value = current[direction] - (current[direction] - equil) * (1.0 / RELAX_TIME)
            relaxed[direction, x] = value
            if x == width_x - 1 and direction in RIGHTWARD:
                right_msg[RIGHTWARD.index(direction)] = value
            if x == 0 and direction in LEFTWARD:
                left_msg[LEFTWARD.index(direction)] = value
            if direction in UPWARD:
                left_msg[5 + UPWARD.index(direction), x : x + 1, :] = value[width_y - 1 :, :]
            if direction in DOWNWARD:
                right_msg[5 + DOWNWARD.index(direction), x : x + 1, :] = value[:1, :]
    right_msg[10] = jnp.zeros((SUBS, LANES), F32)
    left_msg[10] = jnp.zeros((SUBS, LANES), F32)
    for k in range(3):
        row = speed[k, 0]
        twice = jnp.concatenate([row] * (LANES // slots), axis=1)
        right_msg[10, k : k + 1, :] = twice
        left_msg[10, k : k + 1, :] = twice


def prepare_kernel(
    offset, own_right, own_left, from_left, from_right, up_msg, down_msg, edge_msg, own_speed, rows
):
    width_x = own_right.shape[1]
    grad_index = lax.axis_index("grad")
    at_top = grad_index == lax.axis_size("grad") - 1
    at_bottom = grad_index == 0
    rest = jnp.broadcast_to(lax.rem(offset[...], width_x), (width_x, LANES))
    up_rest = jnp.where(at_top, rest, 0)
    down_rest = jnp.where(at_bottom, rest, 0)
    top_boost = jnp.where(at_top, 1.0, 0.0)
    bottom_boost = jnp.where(at_bottom, 1.0, 0.0)

    def window(j, start, sign, amount):
        moved = rows[j, start : start + width_x, :]
        for r in range(1, width_x):
            first = start + sign * r
            moved = jnp.where(amount == r, rows[j, first : first + width_x, :], moved)
        return moved

    for j, direction in enumerate(UPWARD):
        step = VELOCITIES[direction][0]
        boost = 6.0 * WEIGHTS[direction] * step * SHEAR_SPEED
        rows[j, SUBS : 2 * SUBS] = own_left[5 + j]
        rows[j, 2 * SUBS : 3 * SUBS] = from_right[5 + j]
        if step > 0:
            slab = from_left[RIGHTWARD.index(direction)]
            rows[j, SUBS - 1 : SUBS] = slab[SUBS - 1 :, :]
        moved = window(j, SUBS - step, 1, up_rest)
        if step != 0:
            moved = moved - boost * top_boost
        up_msg[j] = moved
        edge_msg[j] = moved
    for j, direction in enumerate(DOWNWARD):
        step = VELOCITIES[direction][0]
        boost = 6.0 * WEIGHTS[direction] * step * SHEAR_SPEED
        rows[5 + j, :SUBS] = from_left[5 + j]
        rows[5 + j, SUBS : 2 * SUBS] = own_right[5 + j]
        if step < 0:
            slab = from_right[LEFTWARD.index(direction)]
            rows[5 + j, 2 * SUBS : 2 * SUBS + 1] = slab[:1, :]
        moved = window(5 + j, SUBS - step, -1, down_rest)
        if step != 0:
            moved = moved + boost * bottom_boost
        down_msg[j] = moved
        edge_msg[j] = jnp.where(at_bottom, moved, edge_msg[j])
    three = [from_left[10], own_right[10], from_right[10]]
    for out, first in ((up_msg, 5), (down_msg, 5), (own_speed, 0)):
        for f in range(3):
            for k in range(3):
                row = 3 * f + k
                out[first + row // SUBS, row % SUBS : row % SUBS + 1, :] = three[f][k : k + 1, :]


def to_bf16(value):
    return value.astype(F32).astype(BF16)


def mark_kernel(first_step, count, cell, direction, sphere, *refs):
    marks = refs[-1]
    step = pl.program_id(0)
    width = cell.shape[2]
    half_rows = marks.shape[0]
    q = cell[0]
    ref = sphere[0]
    row = (direction[0] - 1) * (2 * half_rows // 18) + q // LANES
    z = q % LANES
    half = (row >= half_rows).astype(jnp.int32)
    row = row - half * half_rows
    number = (first_step + step) * width + lax.broadcasted_iota(jnp.int32, (1, width), 1)
    level = ref // LANES
    scale = jnp.where(level == 0, 1.0, 0.0)
    for t in range(1, 5):
        scale = jnp.where(level == t, 2.0 ** (8 * t), scale)
    code = jnp.where(number < count[...], (LANES + ref % LANES).astype(F32) * scale, 0.0)
    block = half_rows // 3
    parts = []
    for first in range(0, half_rows, block):
        local = row - first
        local = to_bf16(jnp.where((local >= 0) & (local < block), local, 255))
        index = to_bf16(lax.broadcasted_iota(jnp.int32, (block, width), 0))
        parts.append(
            jnp.where(
                index == jnp.broadcast_to(local, (block, width)), jnp.ones((), BF16), jnp.zeros((), BF16)
            )
        )
    rows_hot = jnp.concatenate(parts, axis=0)
    column = to_bf16(z + LANES * half)
    index = to_bf16(lax.broadcasted_iota(jnp.int32, (2 * LANES, width), 0))
    columns = jnp.where(
        index == jnp.broadcast_to(column, (2 * LANES, width)),
        jnp.broadcast_to(code.astype(BF16), (2 * LANES, width)),
        jnp.zeros((), BF16),
    )
    part = lax.dot_general(rows_hot, columns, NT, preferred_element_type=F32)

    @pl.when(step == 0)
    def _():
        marks[...] = refs[0][...] + part if len(refs) == 2 else part

    @pl.when(step > 0)
    def _():
        marks[...] += part


def split(value):
    high = value.astype(BF16)
    return high, (value - high.astype(F32)).astype(BF16)


def force_kernel(
    pair_count,
    relaxed,
    density,
    marks,
    own_speed,
    below_speed,
    above_speed,
    pair_first,
    pair_second,
    pair_gap,
    pair_normal,
    bounced,
    to_left,
    to_self,
    to_right,
    link_table,
    first_of,
    second_of,
    value_of,
    sums,
):
    width_x = relaxed.shape[1]
    slots = LANES // 2
    half_rows = marks.shape[0]
    lane = lax.broadcasted_iota(jnp.int32, (1, LANES), 1)
    sources = [below_speed, own_speed, above_speed]

    def speed_row(code, k):
        row = 3 * (code // 3) + k
        source = sources[code % 3]
        first = 0 if source is own_speed else 5
        return source[first + row // SUBS, row % SUBS : row % SUBS + 1, :]

    tables = []
    for k in range(3):
        rows = []
        for t in range(5):
            low = speed_row(2 * t, k)
            high = speed_row(min(2 * t + 1, NEAR - 1), k)
            rows.append(jnp.where(lane < slots, low, high))
        tables.append(rows)
    for direction in range(1, 19):
        for t in range(5):
            total = None
            for k in range(3):
                if VELOCITIES[direction][k] != 0:
                    addend = VELOCITIES[direction][k] * tables[k][t]
                    total = addend if total is None else total + addend
            link_table[direction - 1, t : t + 1, :] = total

    index_a = to_bf16(lax.broadcasted_iota(jnp.int32, (48, LANES), 0))
    index_b = to_bf16(lax.broadcasted_iota(jnp.int32, (16, LANES), 0))
    one = jnp.ones((), BF16)
    zero = jnp.zeros((), BF16)

    def hot_rows(first_row, second_row, values):
        a = jnp.broadcast_to(to_bf16(first_row), (48, LANES))
        b = jnp.broadcast_to(to_bf16(second_row), (16, LANES))
        left = jnp.where(index_a == a, one, zero)
        mask = index_b == b
        right = []
        for value in values:
            high, low = split(value)
            right.append(
                jnp.concatenate(
                    [
                        jnp.where(mask, jnp.broadcast_to(high, (16, LANES)), zero),
                        jnp.where(mask, jnp.broadcast_to(low, (16, LANES)), zero),
                    ],
                    axis=0,
                )
            )
        return left, right

    def group(g, carry):
        for side in range(2):
            index = 2 * g + side
            half = index // 9
            first_row = (index - 9 * half) * (2 * half_rows // 18)
            weight6 = jnp.where(index < 6, 6.0 * WEIGHTS[1], 6.0 * WEIGHTS[7]).astype(F32)
            lookup = [
                jnp.broadcast_to(link_table[index, t : t + 1, :], (SUBS, LANES)) for t in range(5)
            ]
            for x in range(width_x):
                mark = marks[
                    pl.ds(pl.multiple_of(first_row + SUBS * x, SUBS), SUBS),
                    pl.ds(pl.multiple_of(half * LANES, LANES), LANES),
                ]
                live = mark > 0.0
                scaled = mark
                level = jnp.zeros((SUBS, LANES), F32)
                for t in range(1, 5):
                    above = mark > 2.0 ** (8 * t + 6)
                    scaled = jnp.where(above, mark * 2.0 ** (-8 * t), scaled)
                    level = jnp.where(above, float(t), level)
                place = jnp.where(live, scaled - float(LANES), 0.0).astype(jnp.int32)
                speed = jnp.take_along_axis(lookup[0], place, axis=1)
                for t in range(1, 5):
                    found = jnp.take_along_axis(lookup[t], place, axis=1)
                    speed = jnp.where(level == float(t), found, speed)
                leaving = relaxed[index + 1, x]
                back = leaving - weight6 * density[x] * speed
                bounced[index, x] = jnp.where(live, back, NO_LINK)
                force = leaving + back
                if side == 1:
                    force = -force
                high_part = place // 16
                first = jnp.where(live, level * 8.0 + high_part.astype(F32), -1.0)
                second = (place - 16 * high_part).astype(F32)
                where = side * width_x * SUBS + SUBS * x
                first_of[where : where + SUBS] = first
                second_of[where : where + SUBS] = second
                value_of[where : where + SUBS] = jnp.where(live, force, 0.0)
        lefts, rights = [], []
        for r in range(2 * width_x * SUBS):
            left, right = hot_rows(
                first_of[r : r + 1], second_of[r : r + 1], [value_of[r : r + 1]]
            )
            lefts.append(left)
            rights.append(right[0])
        sums[g] = lax.dot_general(
            jnp.concatenate(lefts, axis=1),
            jnp.concatenate(rights, axis=1),
            NT,
            preferred_element_type=F32,
        )
        return carry

    lax.fori_loop(0, 9, group, 0)

    for out in (to_left, to_self, to_right):
        out[...] = jnp.zeros(out.shape, F32)
    totals = []
    for k in range(3):
        total = None
        for g in range(9):
            c = VELOCITIES[2 * g + 1][k]
            if c == 0:
                continue
            if total is None:
                total = sums[g] if c > 0 else -sums[g]
            else:
                total = total + sums[g] if c > 0 else total - sums[g]
        totals.append(total)

    pairs = pair_first.shape[2]
    lefts = []
    rights = [[], [], []]
    for start in range(0, pairs, LANES):
        here = slice(start, start + LANES)
        first = pair_first[0, :, here]
        second = pair_second[0, :, here]
        first_wide = jnp.broadcast_to(first, (SUBS, LANES))
        place = jnp.broadcast_to(second % LANES, (SUBS, LANES))
        level = second // LANES
        gap = pair_gap[0, :, here]
        rate = None
        for k in range(3):
            table = jnp.broadcast_to(tables[k][2], (SUBS, LANES))
            first_speed = jnp.take_along_axis(table, first_wide, axis=1)[:1]
            second_speed = None
            for t in range(5):
                table = jnp.broadcast_to(tables[k][t], (SUBS, LANES))
                found = jnp.take_along_axis(table, place, axis=1)[:1]
                second_speed = found if t == 0 else jnp.where(level == t, found, second_speed)
            addend = (first_speed - second_speed) * pair_normal[k, 0, :, here]
            rate = addend if rate is None else rate + addend
        resist = LUB_COEF * (1.0 / jnp.maximum(gap, GAP_FLOOR) - 1.0 / GAP_CUTOFF)
        number = start + lane
        factor = jnp.where(number < pair_count[...], -resist * rate, 0.0)
        values = [factor * pair_normal[k, 0, :, here] for k in range(3)]
        first = first + 4 * slots
        for ref, these in ((first, values), (second, [-v for v in values])):
            left, right = hot_rows(ref // 16, ref % 16, these)
            lefts.append(left)
            for k in range(3):
                rights[k].append(right[k])
    left = jnp.concatenate(lefts, axis=1)
    for k in range(3):
        total = totals[k] + lax.dot_general(
            left, jnp.concatenate(rights[k], axis=1), NT, preferred_element_type=F32
        )
        value = total[:, :16] + total[:, 16:32]
        first_of[0:48] = jnp.concatenate([value, jnp.zeros((48, LANES - 16), F32)], axis=1)
        line = None
        for s in range(4):
            piece = first_of[pl.ds(s, NEAR, stride=4), :]
            if s:
                piece = pltpu.roll(piece, 16 * s, axis=1)
            line = piece if line is None else line + piece
        for code in range(NEAR):
            row = SUBS * (code % 3) + k
            [to_left, to_self, to_right][code // 3][row : row + 1, :] = line[code : code + 1]


def stream_kernel(relaxed, bounced, from_left, from_right, below, above, edge, out):
    grad_index = lax.axis_index("grad")
    at_top = grad_index == lax.axis_size("grad") - 1
    at_bottom = grad_index == 0
    low_rows = [jnp.where(at_bottom, edge[j], below[j]) for j in range(5)]
    high_rows = [jnp.where(at_top, edge[j], above[j]) for j in range(5)]
    width_x, width_y = relaxed.shape[1], relaxed.shape[2]
    for direction, (cx, cy, cz) in enumerate(VELOCITIES):
        for x in range(width_x):
            source = x - cx
            if source < 0:
                tile = from_left[RIGHTWARD.index(direction)]
            elif source >= width_x:
                tile = from_right[LEFTWARD.index(direction)]
            else:
                tile = relaxed[direction, source]
            if cy != 0:
                tile = pltpu.roll(tile, cy % width_y, axis=0)
                row = lax.broadcasted_iota(jnp.int32, tile.shape, 0)
                if cy > 0:
                    ghost = low_rows[UPWARD.index(direction)][x : x + 1, :]
                    tile = jnp.where(row == 0, jnp.broadcast_to(ghost, tile.shape), tile)
                else:
                    ghost = high_rows[DOWNWARD.index(direction)][x : x + 1, :]
                    tile = jnp.where(row == width_y - 1, jnp.broadcast_to(ghost, tile.shape), tile)
            if cz != 0:
                tile = pltpu.roll(tile, cz % LANES, axis=1)
            if direction > 0:
                opposite = direction + 1 if direction % 2 == 1 else direction - 1
                back = bounced[opposite - 1, x]
                tile = jnp.where(back < 0.5 * NO_LINK, back, tile)
            out[direction, x] = tile


def finish_kernel(own, one, other, speed, force, moved):
    slots = speed.shape[3]
    total = own[...] + one[...] + other[...]
    for k in range(3):
        line = total[k : k + 1, :slots]
        force[k, 0] = line
        moved[k, 0] = speed[k, 0] + INV_MASS * line


def send(block, axis, distance):
    count = lax.axis_size(axis)
    return lax.ppermute(block, axis, [(i, (i + distance) % count) for i in range(count)])


def shape_of(*dims):
    return jax.ShapeDtypeStruct(dims, F32)


def local_of(*dims):
    return pltpu.VMEM(dims, F32)


def local(*arrays):
    return [pltpu.with_memory_space_constraint(array, pltpu.VMEM) for array in arrays]


def mark_links(first, steps, half_rows, count, link_arrays, *before):
    links = link_arrays[0].shape[2]
    width = links // 4
    link_spec = pl.BlockSpec((1, 1, width), lambda i: (0, 0, i + first))
    whole = pl.BlockSpec((half_rows, 2 * LANES), lambda i: (0, 0))
    one = pl.BlockSpec((1, 1), lambda i: (0, 0))
    return pl.pallas_call(
        functools.partial(mark_kernel, first),
        name="mark",
        grid=(steps,),
        in_specs=[one, link_spec, link_spec, link_spec] + [whole] * len(before),
        out_specs=whole,
        out_shape=local_of(half_rows, 2 * LANES),
    )(count, *link_arrays, *local(*before))


def per_device(
    populations,
    le_offset,
    sphere_velocity,
    link_cell,
    link_dir,
    link_sphere,
    link_count,
    pair_first,
    pair_second,
    pair_count,
    pair_gap,
    pair_normal,
):
    width_x, width_y, depth = populations.shape[1:]
    slots = sphere_velocity.shape[3]
    flow_count = lax.axis_size("flow")
    grad_count = lax.axis_size("grad")
    assert depth == LANES and width_y == SUBS and width_x == SUBS and 2 * slots == LANES

    relaxed, density, right_msg, left_msg = pl.pallas_call(
        collide_kernel,
        name="collide",
        in_specs=[VMEM, VMEM],
        out_specs=[VMEM] * 4,
        out_shape=[
            local_of(19, width_x, width_y, depth),
            local_of(width_x, width_y, depth),
            local_of(11, SUBS, LANES),
            local_of(11, SUBS, LANES),
        ],
    )(populations, sphere_velocity)

    from_left = send(right_msg, "flow", 1)
    from_right = send(left_msg, "flow", -1)

    half_rows = 9 * width_x * width_y
    link_arrays = [link_cell, link_dir, link_sphere]
    marks = mark_links(0, 2, half_rows, link_count, link_arrays)

    up_msg, down_msg, edge_msg, own_speed = pl.pallas_call(
        prepare_kernel,
        name="prepare",
        in_specs=[VMEM] * 5,
        out_specs=[VMEM] * 4,
        out_shape=[
            local_of(7, SUBS, LANES),
            local_of(7, SUBS, LANES),
            local_of(5, SUBS, LANES),
            local_of(2, SUBS, LANES),
        ],
        scratch_shapes=[pltpu.VMEM((10, 3 * SUBS, LANES), F32)],
    )(le_offset.reshape(1, 1), *local(right_msg, left_msg, from_left, from_right))

    def exchange(hops, up_msg, down_msg, edge_msg, marks, link_count, *link_arrays):
        below = send(up_msg, "grad", 1)
        above = send(down_msg, "grad", -1)
        route = []
        for a in range(flow_count):
            top = grad_count - 1
            route.append(((a + hops) % flow_count * grad_count + top, a * grad_count))
            route.append(((a - hops) % flow_count * grad_count, a * grad_count + top))
        edge = lax.ppermute(edge_msg, ("flow", "grad"), route)
        marks = mark_links(2, 2, half_rows, link_count, link_arrays, marks)
        return below, above, edge, marks

    below, above, edge, marks = lax.switch(
        lax.div(le_offset[0], width_x),
        [functools.partial(exchange, hops) for hops in range(flow_count)],
        up_msg,
        down_msg,
        edge_msg,
        marks,
        link_count,
        *link_arrays,
    )

    bounced, to_left, to_self, to_right = pl.pallas_call(
        force_kernel,
        name="force",
        in_specs=[VMEM] * 11,
        out_specs=[VMEM] * 4,
        out_shape=[local_of(18, width_x, width_y, depth)] + [local_of(3 * SUBS, LANES)] * 3,
        scratch_shapes=[
            pltpu.VMEM((18, SUBS, LANES), F32),
            pltpu.VMEM((2 * width_x * SUBS, LANES), F32),
            pltpu.VMEM((2 * width_x * SUBS, LANES), F32),
            pltpu.VMEM((2 * width_x * SUBS, LANES), F32),
            pltpu.VMEM((9, 48, 32), F32),
        ],
    )(
        pair_count,
        *local(relaxed, density, marks, own_speed, below, above),
        pair_first,
        pair_second,
        pair_gap,
        pair_normal,
    )

    column = to_self + send(to_left, "flow", -1) + send(to_right, "flow", 1)
    from_above = send(column[:SUBS], "grad", -1)
    from_below = send(column[2 * SUBS :], "grad", 1)
    line = shape_of(3, 1, 1, slots)
    sphere_force, velocity_next = pl.pallas_call(
        finish_kernel,
        name="finish",
        in_specs=[VMEM] * 4,
        out_specs=[VMEM] * 2,
        out_shape=[line, line],
    )(*local(column[SUBS : 2 * SUBS], from_above, from_below), sphere_velocity)

    updated = pl.pallas_call(
        stream_kernel,
        name="stream",
        in_specs=[VMEM] * 7,
        out_specs=VMEM,
        out_shape=shape_of(19, width_x, width_y, depth),
    )(*local(relaxed, bounced, from_left, from_right, below, above, edge))
    return updated, sphere_force, velocity_next


def solution(mesh):
    in_specs = (
        P(None, "flow", "grad", None),
        P(),
        P(None, "flow", "grad", None),
        P("flow", "grad", None),
        P("flow", "grad", None),
        P("flow", "grad", None),
        P("flow", "grad"),
        P("flow", "grad", None),
        P("flow", "grad", None),
        P("flow", "grad"),
        P("flow", "grad", None),
        P(None, "flow", "grad", None),
    )
    out_specs = (
        P(None, "flow", "grad", None),
        P(None, "flow", "grad", None),
        P(None, "flow", "grad", None),
    )
    return jax.shard_map(
        per_device, mesh=mesh, in_specs=in_specs, out_specs=out_specs, check_vma=False
    )
```

```python
import functools

import jax
import jax.numpy as jnp
from jax import lax
from jax.experimental import pallas as pl
from jax.experimental.pallas import tpu as pltpu
from jax.sharding import PartitionSpec as P

VELOCITIES = [
    (0, 0, 0),
    (1, 0, 0),
    (-1, 0, 0),
    (0, 1, 0),
    (0, -1, 0),
    (0, 0, 1),
    (0, 0, -1),
    (1, 1, 0),
    (-1, -1, 0),
    (1, -1, 0),
    (-1, 1, 0),
    (1, 0, 1),
    (-1, 0, -1),
    (1, 0, -1),
    (-1, 0, 1),
    (0, 1, 1),
    (0, -1, -1),
    (0, 1, -1),
    (0, -1, 1),
]
WEIGHTS = [1.0 / 3.0] + [1.0 / 18.0] * 6 + [1.0 / 36.0] * 12
UPWARD = [3, 7, 10, 15, 17]
DOWNWARD = [4, 8, 9, 16, 18]
RIGHTWARD = [1, 7, 9, 11, 13]
LEFTWARD = [2, 8, 10, 12, 14]
RELAX_TIME = 0.8
SHEAR_SPEED = 0.1
LUB_COEF = 0.5
GAP_FLOOR = 0.1
GAP_CUTOFF = 1.0
INV_MASS = 1.0 / 523.6
LANES = 128
SUBS = 8
NEAR = 9
NO_LINK = 1e30
BF16 = jnp.bfloat16
F32 = jnp.float32
NT = (((1,), (1,)), ((), ()))

VMEM = pl.BlockSpec(memory_space=pltpu.VMEM)


def collide_kernel(pops, speed, relaxed, density, right_msg, left_msg, own_line):
    width_x, width_y = pops.shape[1], pops.shape[2]
    slots = speed.shape[3]
    for x in range(width_x):
        current = [pops[d, x] for d in range(19)]
        total = functools.reduce(lambda p, q: p + q, current)
        density[x] = total
        inverse = 1.0 / total
        speeds = []
        for axis_id in range(3):
            running = None
            for direction, vector in enumerate(VELOCITIES):
                if vector[axis_id] == 0:
                    continue
                if running is None:
                    running = current[direction]
                elif vector[axis_id] > 0:
                    running = running + current[direction]
                else:
                    running = running - current[direction]
            speeds.append(running * inverse)
        base = 1.0 - 1.5 * (
            speeds[0] * speeds[0] + speeds[1] * speeds[1] + speeds[2] * speeds[2]
        )
        for direction, vector in enumerate(VELOCITIES):
            c_dot = None
            for axis_id in range(3):
                if vector[axis_id] != 0:
                    addend = vector[axis_id] * speeds[axis_id]
                    c_dot = addend if c_dot is None else c_dot + addend
            shape = base if c_dot is None else base + c_dot * (3.0 + 4.5 * c_dot)
            equil = WEIGHTS[direction] * total * shape
            value = current[direction] - (current[direction] - equil) * (1.0 / RELAX_TIME)
            relaxed[direction, x] = value
            if x == width_x - 1 and direction in RIGHTWARD:
                right_msg[RIGHTWARD.index(direction)] = value
            if x == 0 and direction in LEFTWARD:
                left_msg[LEFTWARD.index(direction)] = value
            if direction in UPWARD:
                left_msg[5 + UPWARD.index(direction), x : x + 1, :] = value[width_y - 1 :, :]
            if direction in DOWNWARD:
                right_msg[5 + DOWNWARD.index(direction), x : x + 1, :] = value[:1, :]
    right_msg[10] = jnp.zeros((SUBS, LANES), F32)
    left_msg[10] = jnp.zeros((SUBS, LANES), F32)
    for k in range(3):
        row = speed[k, 0]
        twice = jnp.concatenate([row] * (LANES // slots), axis=1)
        right_msg[10, k : k + 1, :] = twice
        left_msg[10, k : k + 1, :] = twice
        own_line[k : k + 1, :] = twice


def prepare_kernel(
    offset, own_right, own_left, from_left, from_right, up_msg, down_msg, edge_msg, own_speed, rows
):
    width_x = own_right.shape[1]
    grad_index = lax.axis_index("grad")
    at_top = grad_index == lax.axis_size("grad") - 1
    at_bottom = grad_index == 0
    rest = jnp.broadcast_to(lax.rem(offset[...], width_x), (width_x, LANES))
    up_rest = jnp.where(at_top, rest, 0)
    down_rest = jnp.where(at_bottom, rest, 0)
    top_boost = jnp.where(at_top, 1.0, 0.0)
    bottom_boost = jnp.where(at_bottom, 1.0, 0.0)

    def window(j, start, sign, amount):
        moved = rows[j, start : start + width_x, :]
        for r in range(1, width_x):
            first = start + sign * r
            moved = jnp.where(amount == r, rows[j, first : first + width_x, :], moved)
        return moved

    for j, direction in enumerate(UPWARD):
        step = VELOCITIES[direction][0]
        boost = 6.0 * WEIGHTS[direction] * step * SHEAR_SPEED
        rows[j, SUBS : 2 * SUBS] = own_left[5 + j]
        rows[j, 2 * SUBS : 3 * SUBS] = from_right[5 + j]
        if step > 0:
            slab = from_left[RIGHTWARD.index(direction)]
            rows[j, SUBS - 1 : SUBS] = slab[SUBS - 1 :, :]
        moved = window(j, SUBS - step, 1, up_rest)
        if step != 0:
            moved = moved - boost * top_boost
        up_msg[j] = moved
        edge_msg[j] = moved
    for j, direction in enumerate(DOWNWARD):
        step = VELOCITIES[direction][0]
        boost = 6.0 * WEIGHTS[direction] * step * SHEAR_SPEED
        rows[5 + j, :SUBS] = from_left[5 + j]
        rows[5 + j, SUBS : 2 * SUBS] = own_right[5 + j]
        if step < 0:
            slab = from_right[LEFTWARD.index(direction)]
            rows[5 + j, 2 * SUBS : 2 * SUBS + 1] = slab[:1, :]
        moved = window(5 + j, SUBS - step, -1, down_rest)
        if step != 0:
            moved = moved + boost * bottom_boost
        down_msg[j] = moved
        edge_msg[j] = jnp.where(at_bottom, moved, edge_msg[j])
    three = [from_left[10], own_right[10], from_right[10]]
    for out, first in ((up_msg, 5), (down_msg, 5), (own_speed, 0)):
        for f in range(3):
            for k in range(3):
                row = 3 * f + k
                out[first + row // SUBS, row % SUBS : row % SUBS + 1, :] = three[f][k : k + 1, :]


def to_bf16(value):
    return value.astype(F32).astype(BF16)


def mark_kernel(first_step, count, cell, direction, sphere, *refs):
    marks = refs[-1]
    step = pl.program_id(0)
    width = cell.shape[2]
    half_rows = marks.shape[0]
    q = cell[0]
    ref = sphere[0]
    row = (direction[0] - 1) * (2 * half_rows // 18) + q // LANES
    z = q % LANES
    half = (row >= half_rows).astype(jnp.int32)
    row = row - half * half_rows
    number = (first_step + step) * width + lax.broadcasted_iota(jnp.int32, (1, width), 1)
    level = ref // LANES
    scale = jnp.where(level == 0, 1.0, 0.0)
    for t in range(1, 5):
        scale = jnp.where(level == t, 2.0 ** (8 * t), scale)
    code = jnp.where(number < count[...], (LANES + ref % LANES).astype(F32) * scale, 0.0)
    block = half_rows // 3
    parts = []
    for first in range(0, half_rows, block):
        local = row - first
        local = to_bf16(jnp.where((local >= 0) & (local < block), local, 255))
        index = to_bf16(lax.broadcasted_iota(jnp.int32, (block, width), 0))
        parts.append(
            jnp.where(
                index == jnp.broadcast_to(local, (block, width)), jnp.ones((), BF16), jnp.zeros((), BF16)
            )
        )
    rows_hot = jnp.concatenate(parts, axis=0)
    column = to_bf16(z + LANES * half)
    index = to_bf16(lax.broadcasted_iota(jnp.int32, (2 * LANES, width), 0))
    columns = jnp.where(
        index == jnp.broadcast_to(column, (2 * LANES, width)),
        jnp.broadcast_to(code.astype(BF16), (2 * LANES, width)),
        jnp.zeros((), BF16),
    )
    part = lax.dot_general(rows_hot, columns, NT, preferred_element_type=F32)

    @pl.when(step == 0)
    def _():
        marks[...] = refs[0][...] + part if len(refs) == 2 else part

    @pl.when(step > 0)
    def _():
        marks[...] += part


def split(value):
    high = value.astype(BF16)
    return high, (value - high.astype(F32)).astype(BF16)


def force_kernel(
    pair_count,
    relaxed,
    density,
    marks,
    own_speed,
    below_speed,
    above_speed,
    pair_first,
    pair_second,
    pair_gap,
    pair_normal,
    bounced,
    to_left,
    to_self,
    to_right,
    link_table,
    first_of,
    second_of,
    value_of,
    rest_of,
    sums,
):
    width_x = relaxed.shape[1]
    slots = LANES // 2
    half_rows = marks.shape[0]
    lane = lax.broadcasted_iota(jnp.int32, (1, LANES), 1)
    sources = [below_speed, own_speed, above_speed]

    def speed_row(code, k):
        row = 3 * (code // 3) + k
        source = sources[code % 3]
        first = 0 if source is own_speed else 5
        return source[first + row // SUBS, row % SUBS : row % SUBS + 1, :]

    tables = []
    for k in range(3):
        rows = []
        for t in range(5):
            low = speed_row(2 * t, k)
            high = speed_row(min(2 * t + 1, NEAR - 1), k)
            rows.append(jnp.where(lane < slots, low, high))
        tables.append(rows)
    for direction in range(1, 19):
        for t in range(5):
            total = None
            for k in range(3):
                if VELOCITIES[direction][k] != 0:
                    addend = VELOCITIES[direction][k] * tables[k][t]
                    total = addend if total is None else total + addend
            link_table[direction - 1, t : t + 1, :] = total

    index_a = to_bf16(lax.broadcasted_iota(jnp.int32, (48, LANES), 0))
    index_b = to_bf16(lax.broadcasted_iota(jnp.int32, (16, LANES), 0))
    one = jnp.ones((), BF16)
    zero = jnp.zeros((), BF16)

    def spread(ref, r):
        row = ref[pl.ds(r, SUBS, stride=0), :]
        return jnp.concatenate([row, row], axis=0).astype(BF16)

    def slot_rows(r):
        a = spread(first_of, r)
        b = spread(second_of, r)
        high = spread(value_of, r)
        low = spread(rest_of, r)
        left = [jnp.where(index_a[16 * i : 16 * i + 16] == a, one, zero) for i in range(3)]
        mask = index_b == b
        right = [jnp.where(mask, high, zero), jnp.where(mask, low, zero)]
        return jnp.concatenate(left, axis=0), jnp.concatenate(right, axis=0)

    def hot_rows(first_row, second_row, values):
        a = jnp.broadcast_to(to_bf16(first_row), (48, LANES))
        b = jnp.broadcast_to(to_bf16(second_row), (16, LANES))
        left = jnp.where(index_a == a, one, zero)
        mask = index_b == b
        right = []
        for value in values:
            high, low = split(value)
            right.append(
                jnp.concatenate(
                    [
                        jnp.where(mask, jnp.broadcast_to(high, (16, LANES)), zero),
                        jnp.where(mask, jnp.broadcast_to(low, (16, LANES)), zero),
                    ],
                    axis=0,
                )
            )
        return left, right

    def group(g, carry):
        for side in range(2):
            index = 2 * g + side
            half = index // 9
            first_row = (index - 9 * half) * (2 * half_rows // 18)
            weight6 = jnp.where(index < 6, 6.0 * WEIGHTS[1], 6.0 * WEIGHTS[7]).astype(F32)
            lookup = [
                jnp.broadcast_to(link_table[index, t : t + 1, :], (SUBS, LANES)) for t in range(5)
            ]
            for x in range(width_x):
                mark = marks[
                    pl.ds(pl.multiple_of(first_row + SUBS * x, SUBS), SUBS),
                    pl.ds(pl.multiple_of(half * LANES, LANES), LANES),
                ]
                live = mark > 0.0
                scaled = mark
                level = jnp.zeros((SUBS, LANES), F32)
                for t in range(1, 5):
                    above = mark > 2.0 ** (8 * t + 6)
                    scaled = jnp.where(above, mark * 2.0 ** (-8 * t), scaled)
                    level = jnp.where(above, float(t), level)
                place = jnp.where(live, scaled - float(LANES), 0.0).astype(jnp.int32)
                speed = jnp.take_along_axis(lookup[0], place, axis=1)
                for t in range(1, 5):
                    found = jnp.take_along_axis(lookup[t], place, axis=1)
                    speed = jnp.where(level == float(t), found, speed)
                leaving = relaxed[index + 1, x]
                back = leaving - weight6 * density[x] * speed
                bounced[index, x] = jnp.where(live, back, NO_LINK)
                force = leaving + back
                if side == 1:
                    force = -force
                high_part = place // 16
                first = jnp.where(live, level * 8.0 + high_part.astype(F32), -1.0)
                second = (place - 16 * high_part).astype(F32)
                where = side * width_x * SUBS + SUBS * x
                first_of[where : where + SUBS] = first
                second_of[where : where + SUBS] = second
                force = jnp.where(live, force, 0.0)
                high = force.astype(BF16).astype(F32)
                value_of[where : where + SUBS] = high
                rest_of[where : where + SUBS] = force - high
        lefts, rights = [], []
        for r in range(2 * width_x * SUBS):
            left, right = slot_rows(r)
            lefts.append(left)
            rights.append(right)
        sums[g] = lax.dot_general(
            jnp.concatenate(lefts, axis=1),
            jnp.concatenate(rights, axis=1),
            NT,
            preferred_element_type=F32,
        )
        return carry

    lax.fori_loop(0, 9, group, 0)

    for out in (to_left, to_self, to_right):
        out[...] = jnp.zeros(out.shape, F32)
    totals = []
    for k in range(3):
        total = None
        for g in range(9):
            c = VELOCITIES[2 * g + 1][k]
            if c == 0:
                continue
            if total is None:
                total = sums[g] if c > 0 else -sums[g]
            else:
                total = total + sums[g] if c > 0 else total - sums[g]
        totals.append(total)

    pairs = pair_first.shape[2]
    lefts = []
    rights = [[], [], []]
    for start in range(0, pairs, LANES):
        here = slice(start, start + LANES)
        first = pair_first[0, :, here]
        second = pair_second[0, :, here]
        first_wide = jnp.broadcast_to(first, (SUBS, LANES))
        place = jnp.broadcast_to(second % LANES, (SUBS, LANES))
        level = second // LANES
        gap = pair_gap[0, :, here]
        rate = None
        for k in range(3):
            table = jnp.broadcast_to(tables[k][2], (SUBS, LANES))
            first_speed = jnp.take_along_axis(table, first_wide, axis=1)[:1]
            second_speed = None
            for t in range(5):
                table = jnp.broadcast_to(tables[k][t], (SUBS, LANES))
                found = jnp.take_along_axis(table, place, axis=1)[:1]
                second_speed = found if t == 0 else jnp.where(level == t, found, second_speed)
            addend = (first_speed - second_speed) * pair_normal[k, 0, :, here]
            rate = addend if rate is None else rate + addend
        resist = LUB_COEF * (1.0 / jnp.maximum(gap, GAP_FLOOR) - 1.0 / GAP_CUTOFF)
        number = start + lane
        factor = jnp.where(number < pair_count[...], -resist * rate, 0.0)
        values = [factor * pair_normal[k, 0, :, here] for k in range(3)]
        first = first + 4 * slots
        for ref, these in ((first, values), (second, [-v for v in values])):
            left, right = hot_rows(ref // 16, ref % 16, these)
            lefts.append(left)
            for k in range(3):
                rights[k].append(right[k])
    left = jnp.concatenate(lefts, axis=1)
    for k in range(3):
        total = totals[k] + lax.dot_general(
            left, jnp.concatenate(rights[k], axis=1), NT, preferred_element_type=F32
        )
        value = total[:, :16] + total[:, 16:32]
        first_of[0:48] = jnp.concatenate([value, jnp.zeros((48, LANES - 16), F32)], axis=1)
        line = None
        for s in range(4):
            piece = first_of[pl.ds(s, NEAR, stride=4), :]
            if s:
                piece = pltpu.roll(piece, 16 * s, axis=1)
            line = piece if line is None else line + piece
        for code in range(NEAR):
            row = SUBS * (code % 3) + k
            [to_left, to_self, to_right][code // 3][row : row + 1, :] = line[code : code + 1]


def stream_kernel(relaxed, bounced, from_left, from_right, below, above, edge, out):
    grad_index = lax.axis_index("grad")
    at_top = grad_index == lax.axis_size("grad") - 1
    at_bottom = grad_index == 0
    low_rows = [jnp.where(at_bottom, edge[j], below[j]) for j in range(5)]
    high_rows = [jnp.where(at_top, edge[j], above[j]) for j in range(5)]
    width_x, width_y = relaxed.shape[1], relaxed.shape[2]
    for direction, (cx, cy, cz) in enumerate(VELOCITIES):
        for x in range(width_x):
            source = x - cx
            if source < 0:
                tile = from_left[RIGHTWARD.index(direction)]
            elif source >= width_x:
                tile = from_right[LEFTWARD.index(direction)]
            else:
                tile = relaxed[direction, source]
            if cy != 0:
                tile = pltpu.roll(tile, cy % width_y, axis=0)
                row = lax.broadcasted_iota(jnp.int32, tile.shape, 0)
                if cy > 0:
                    ghost = low_rows[UPWARD.index(direction)][x : x + 1, :]
                    tile = jnp.where(row == 0, jnp.broadcast_to(ghost, tile.shape), tile)
                else:
                    ghost = high_rows[DOWNWARD.index(direction)][x : x + 1, :]
                    tile = jnp.where(row == width_y - 1, jnp.broadcast_to(ghost, tile.shape), tile)
            if cz != 0:
                tile = pltpu.roll(tile, cz % LANES, axis=1)
            if direction > 0:
                opposite = direction + 1 if direction % 2 == 1 else direction - 1
                back = bounced[opposite - 1, x]
                tile = jnp.where(back < 0.5 * NO_LINK, back, tile)
            out[direction, x] = tile


def finish_kernel(own, one, other, speed, force, moved):
    slots = force.shape[3]
    total = own[...] + one[...] + other[...]
    for k in range(3):
        line = total[k : k + 1, :slots]
        force[k, 0] = line
        moved[k, 0] = speed[k : k + 1, :slots] + INV_MASS * line


def send(block, axis, distance):
    count = lax.axis_size(axis)
    return lax.ppermute(block, axis, [(i, (i + distance) % count) for i in range(count)])


def shape_of(*dims):
    return jax.ShapeDtypeStruct(dims, F32)


def local_of(*dims):
    return pltpu.VMEM(dims, F32)


def local(*arrays):
    return [pltpu.with_memory_space_constraint(array, pltpu.VMEM) for array in arrays]


def mark_links(first, steps, half_rows, count, link_arrays, *before):
    links = link_arrays[0].shape[2]
    width = links // 2
    link_spec = pl.BlockSpec((1, 1, width), lambda i: (0, 0, i + first))
    whole = pl.BlockSpec((half_rows, 2 * LANES), lambda i: (0, 0))
    one = pl.BlockSpec((1, 1), lambda i: (0, 0))
    return pl.pallas_call(
        functools.partial(mark_kernel, first),
        name="mark",
        grid=(steps,),
        in_specs=[one, link_spec, link_spec, link_spec] + [whole] * len(before),
        out_specs=whole,
        out_shape=local_of(half_rows, 2 * LANES),
    )(count, *link_arrays, *local(*before))


def per_device(
    populations,
    le_offset,
    sphere_velocity,
    link_cell,
    link_dir,
    link_sphere,
    link_count,
    pair_first,
    pair_second,
    pair_count,
    pair_gap,
    pair_normal,
):
    width_x, width_y, depth = populations.shape[1:]
    slots = sphere_velocity.shape[3]
    flow_count = lax.axis_size("flow")
    grad_count = lax.axis_size("grad")
    assert depth == LANES and width_y == SUBS and width_x == SUBS and 2 * slots == LANES

    relaxed, density, right_msg, left_msg, own_line = pl.pallas_call(
        collide_kernel,
        name="collide",
        in_specs=[VMEM, VMEM],
        out_specs=[VMEM] * 5,
        out_shape=[
            local_of(19, width_x, width_y, depth),
            local_of(width_x, width_y, depth),
            local_of(11, SUBS, LANES),
            local_of(11, SUBS, LANES),
            local_of(3, LANES),
        ],
    )(populations, sphere_velocity)

    from_left = send(right_msg, "flow", 1)
    from_right = send(left_msg, "flow", -1)

    half_rows = 9 * width_x * width_y
    link_arrays = [link_cell, link_dir, link_sphere]
    marks = mark_links(0, 1, half_rows, link_count, link_arrays)

    up_msg, down_msg, edge_msg, own_speed = pl.pallas_call(
        prepare_kernel,
        name="prepare",
        in_specs=[VMEM] * 5,
        out_specs=[VMEM] * 4,
        out_shape=[
            local_of(7, SUBS, LANES),
            local_of(7, SUBS, LANES),
            local_of(5, SUBS, LANES),
            local_of(2, SUBS, LANES),
        ],
        scratch_shapes=[pltpu.VMEM((10, 3 * SUBS, LANES), F32)],
    )(le_offset.reshape(1, 1), *local(right_msg, left_msg, from_left, from_right))

    def exchange(hops, up_msg, down_msg, edge_msg, marks, link_count, *link_arrays):
        below = send(up_msg, "grad", 1)
        above = send(down_msg, "grad", -1)
        route = []
        for a in range(flow_count):
            top = grad_count - 1
            route.append(((a + hops) % flow_count * grad_count + top, a * grad_count))
            route.append(((a - hops) % flow_count * grad_count, a * grad_count + top))
        edge = lax.ppermute(edge_msg, ("flow", "grad"), route)
        marks = mark_links(1, 1, half_rows, link_count, link_arrays, marks)
        return below, above, edge, marks

    below, above, edge, marks = lax.switch(
        lax.div(le_offset[0], width_x),
        [functools.partial(exchange, hops) for hops in range(flow_count)],
        up_msg,
        down_msg,
        edge_msg,
        marks,
        link_count,
        *link_arrays,
    )

    bounced, to_left, to_self, to_right = pl.pallas_call(
        force_kernel,
        name="force",
        in_specs=[VMEM] * 11,
        out_specs=[VMEM] * 4,
        out_shape=[local_of(18, width_x, width_y, depth)] + [local_of(3 * SUBS, LANES)] * 3,
        scratch_shapes=[
            pltpu.VMEM((18, SUBS, LANES), F32),
            pltpu.VMEM((2 * width_x * SUBS, LANES), F32),
            pltpu.VMEM((2 * width_x * SUBS, LANES), F32),
            pltpu.VMEM((2 * width_x * SUBS, LANES), F32),
            pltpu.VMEM((2 * width_x * SUBS, LANES), F32),
            pltpu.VMEM((9, 48, 32), F32),
        ],
    )(
        pair_count,
        *local(relaxed, density, marks, own_speed, below, above),
        pair_first,
        pair_second,
        pair_gap,
        pair_normal,
    )

    updated = pl.pallas_call(
        stream_kernel,
        name="stream",
        in_specs=[VMEM] * 7,
        out_specs=VMEM,
        out_shape=shape_of(19, width_x, width_y, depth),
    )(*local(relaxed, bounced, from_left, from_right, below, above, edge))

    column = to_self + send(to_left, "flow", -1) + send(to_right, "flow", 1)
    from_above = send(column[:SUBS], "grad", -1)
    from_below = send(column[2 * SUBS :], "grad", 1)
    line = shape_of(3, 1, 1, slots)
    sphere_force, velocity_next = pl.pallas_call(
        finish_kernel,
        name="finish",
        in_specs=[VMEM] * 4,
        out_specs=[VMEM] * 2,
        out_shape=[line, line],
    )(*local(column[SUBS : 2 * SUBS], from_above, from_below, own_line))

    return updated, sphere_force, velocity_next


def solution(mesh):
    in_specs = (
        P(None, "flow", "grad", None),
        P(),
        P(None, "flow", "grad", None),
        P("flow", "grad", None),
        P("flow", "grad", None),
        P("flow", "grad", None),
        P("flow", "grad"),
        P("flow", "grad", None),
        P("flow", "grad", None),
        P("flow", "grad"),
        P("flow", "grad", None),
        P(None, "flow", "grad", None),
    )
    out_specs = (
        P(None, "flow", "grad", None),
        P(None, "flow", "grad", None),
        P(None, "flow", "grad", None),
    )
    return jax.shard_map(
        per_device, mesh=mesh, in_specs=in_specs, out_specs=out_specs, check_vma=False
    )
```

```python
import functools

import jax
import jax.numpy as jnp
from jax import lax
from jax.experimental import pallas as pl
from jax.experimental.pallas import tpu as pltpu
from jax.sharding import PartitionSpec as P

VELOCITIES = [
    (0, 0, 0),
    (1, 0, 0),
    (-1, 0, 0),
    (0, 1, 0),
    (0, -1, 0),
    (0, 0, 1),
    (0, 0, -1),
    (1, 1, 0),
    (-1, -1, 0),
    (1, -1, 0),
    (-1, 1, 0),
    (1, 0, 1),
    (-1, 0, -1),
    (1, 0, -1),
    (-1, 0, 1),
    (0, 1, 1),
    (0, -1, -1),
    (0, 1, -1),
    (0, -1, 1),
]
WEIGHTS = [1.0 / 3.0] + [1.0 / 18.0] * 6 + [1.0 / 36.0] * 12
UPWARD = [3, 7, 10, 15, 17]
DOWNWARD = [4, 8, 9, 16, 18]
RIGHTWARD = [1, 7, 9, 11, 13]
LEFTWARD = [2, 8, 10, 12, 14]
RELAX_TIME = 0.8
SHEAR_SPEED = 0.1
LUB_COEF = 0.5
GAP_FLOOR = 0.1
GAP_CUTOFF = 1.0
INV_MASS = 1.0 / 523.6
LANES = 128
SUBS = 8
NEAR = 9
NO_LINK = 1e30
BF16 = jnp.bfloat16
F32 = jnp.float32
NT = (((1,), (1,)), ((), ()))

VMEM = pl.BlockSpec(memory_space=pltpu.VMEM)


def collide_kernel(pops, speed, relaxed, density, right_msg, left_msg, own_line):
    width_x, width_y = pops.shape[1], pops.shape[2]
    slots = speed.shape[3]
    for x in range(width_x):
        current = [pops[d, x] for d in range(19)]
        total = functools.reduce(lambda p, q: p + q, current)
        density[x] = total
        inverse = 1.0 / total
        speeds = []
        for axis_id in range(3):
            running = None
            for direction, vector in enumerate(VELOCITIES):
                if vector[axis_id] == 0:
                    continue
                if running is None:
                    running = current[direction]
                elif vector[axis_id] > 0:
                    running = running + current[direction]
                else:
                    running = running - current[direction]
            speeds.append(running * inverse)
        base = 1.0 - 1.5 * (
            speeds[0] * speeds[0] + speeds[1] * speeds[1] + speeds[2] * speeds[2]
        )
        for direction, vector in enumerate(VELOCITIES):
            c_dot = None
            for axis_id in range(3):
                if vector[axis_id] != 0:
                    addend = vector[axis_id] * speeds[axis_id]
                    c_dot = addend if c_dot is None else c_dot + addend
            shape = base if c_dot is None else base + c_dot * (3.0 + 4.5 * c_dot)
            equil = WEIGHTS[direction] * total * shape
            value = current[direction] - (current[direction] - equil) * (1.0 / RELAX_TIME)
            relaxed[direction, x] = value
            if x == width_x - 1 and direction in RIGHTWARD:
                right_msg[RIGHTWARD.index(direction)] = value
            if x == 0 and direction in LEFTWARD:
                left_msg[LEFTWARD.index(direction)] = value
            if direction in UPWARD:
                left_msg[5 + UPWARD.index(direction), x : x + 1, :] = value[width_y - 1 :, :]
            if direction in DOWNWARD:
                right_msg[5 + DOWNWARD.index(direction), x : x + 1, :] = value[:1, :]
    right_msg[10] = jnp.zeros((SUBS, LANES), F32)
    left_msg[10] = jnp.zeros((SUBS, LANES), F32)
    for k in range(3):
        row = speed[k, 0]
        twice = jnp.concatenate([row] * (LANES // slots), axis=1)
        right_msg[10, k : k + 1, :] = twice
        left_msg[10, k : k + 1, :] = twice
        own_line[k : k + 1, :] = twice


def prepare_kernel(
    offset, own_right, own_left, from_left, from_right, msg_pair, msg_cross, own_speed, rows
):
    width_x = own_right.shape[1]
    grad_index = lax.axis_index("grad")
    at_top = grad_index == lax.axis_size("grad") - 1
    at_bottom = grad_index == 0
    even = lax.rem(grad_index, 2) == 0
    rest = jnp.broadcast_to(lax.rem(offset[...], width_x), (width_x, LANES))
    up_rest = jnp.where(at_top, rest, 0)
    down_rest = jnp.where(at_bottom, rest, 0)
    top_boost = jnp.where(at_top, 1.0, 0.0)
    bottom_boost = jnp.where(at_bottom, 1.0, 0.0)

    def window(j, start, sign, amount):
        moved = rows[j, start : start + width_x, :]
        for r in range(1, width_x):
            first = start + sign * r
            moved = jnp.where(amount == r, rows[j, first : first + width_x, :], moved)
        return moved

    ups = []
    for j, direction in enumerate(UPWARD):
        step = VELOCITIES[direction][0]
        boost = 6.0 * WEIGHTS[direction] * step * SHEAR_SPEED
        rows[j, SUBS : 2 * SUBS] = own_left[5 + j]
        rows[j, 2 * SUBS : 3 * SUBS] = from_right[5 + j]
        if step > 0:
            slab = from_left[RIGHTWARD.index(direction)]
            rows[j, SUBS - 1 : SUBS] = slab[SUBS - 1 :, :]
        moved = window(j, SUBS - step, 1, up_rest)
        if step != 0:
            moved = moved - boost * top_boost
        ups.append(moved)
    for j, direction in enumerate(DOWNWARD):
        step = VELOCITIES[direction][0]
        boost = 6.0 * WEIGHTS[direction] * step * SHEAR_SPEED
        rows[5 + j, :SUBS] = from_left[5 + j]
        rows[5 + j, SUBS : 2 * SUBS] = own_right[5 + j]
        if step < 0:
            slab = from_right[LEFTWARD.index(direction)]
            rows[5 + j, 2 * SUBS : 2 * SUBS + 1] = slab[:1, :]
        moved = window(5 + j, SUBS - step, -1, down_rest)
        if step != 0:
            moved = moved + boost * bottom_boost
        msg_pair[j] = jnp.where(even, ups[j], moved)
        msg_cross[j] = jnp.where(even, moved, ups[j])
    three = [from_left[10], own_right[10], from_right[10]]
    for out, first in ((msg_pair, 5), (msg_cross, 5), (own_speed, 0)):
        for f in range(3):
            for k in range(3):
                row = 3 * f + k
                out[first + row // SUBS, row % SUBS : row % SUBS + 1, :] = three[f][k : k + 1, :]


def to_bf16(value):
    return value.astype(F32).astype(BF16)


def mark_kernel(first_step, count, cell, direction, sphere, *refs):
    marks = refs[-1]
    step = pl.program_id(0)
    width = cell.shape[2]
    half_rows = marks.shape[0]
    q = cell[0]
    ref = sphere[0]
    row = (direction[0] - 1) * (2 * half_rows // 18) + q // LANES
    z = q % LANES
    half = (row >= half_rows).astype(jnp.int32)
    row = row - half * half_rows
    number = (first_step + step) * width + lax.broadcasted_iota(jnp.int32, (1, width), 1)
    level = ref // LANES
    scale = jnp.where(level == 0, 1.0, 0.0)
    for t in range(1, 5):
        scale = jnp.where(level == t, 2.0 ** (8 * t), scale)
    code = jnp.where(number < count[...], (LANES + ref % LANES).astype(F32) * scale, 0.0)
    block = half_rows // 3
    parts = []
    for first in range(0, half_rows, block):
        local = row - first
        local = to_bf16(jnp.where((local >= 0) & (local < block), local, 255))
        index = to_bf16(lax.broadcasted_iota(jnp.int32, (block, width), 0))
        parts.append(
            jnp.where(
                index == jnp.broadcast_to(local, (block, width)), jnp.ones((), BF16), jnp.zeros((), BF16)
            )
        )
    rows_hot = jnp.concatenate(parts, axis=0)
    column = to_bf16(z + LANES * half)
    index = to_bf16(lax.broadcasted_iota(jnp.int32, (2 * LANES, width), 0))
    columns = jnp.where(
        index == jnp.broadcast_to(column, (2 * LANES, width)),
        jnp.broadcast_to(code.astype(BF16), (2 * LANES, width)),
        jnp.zeros((), BF16),
    )
    part = lax.dot_general(rows_hot, columns, NT, preferred_element_type=F32)

    @pl.when(step == 0)
    def _():
        marks[...] = refs[0][...] + part if len(refs) == 2 else part

    @pl.when(step > 0)
    def _():
        marks[...] += part


def split(value):
    high = value.astype(BF16)
    return high, (value - high.astype(F32)).astype(BF16)


def force_kernel(
    pair_count,
    relaxed,
    density,
    marks,
    own_speed,
    from_pair,
    from_cross,
    from_wrap,
    pair_first,
    pair_second,
    pair_gap,
    pair_normal,
    bounced,
    to_left,
    to_self,
    to_right,
    link_table,
    *scratch,
):
    width_x = relaxed.shape[1]
    slots = LANES // 2
    even_buffers, odd_buffers, sums = scratch[:4], scratch[4:8], scratch[8]
    first_of = odd_buffers[0]
    half_rows = marks.shape[0]
    lane = lax.broadcasted_iota(jnp.int32, (1, LANES), 1)
    grad_index = lax.axis_index("grad")
    even = lax.rem(grad_index, 2) == 0
    at_edge = (grad_index == 0) | (grad_index == lax.axis_size("grad") - 1)
    sources = [[], [], []]
    for tile in range(2):
        near = from_pair[5 + tile]
        far = jnp.where(at_edge, from_wrap[tile], from_cross[5 + tile])
        sources[0].append(jnp.where(even, far, near))
        sources[1].append(own_speed[tile])
        sources[2].append(jnp.where(even, near, far))

    def speed_row(code, k):
        row = 3 * (code // 3) + k
        return sources[code % 3][row // SUBS][row % SUBS : row % SUBS + 1, :]

    tables = []
    for k in range(3):
        rows = []
        for t in range(5):
            low = speed_row(2 * t, k)
            high = speed_row(min(2 * t + 1, NEAR - 1), k)
            rows.append(jnp.where(lane < slots, low, high))
        tables.append(rows)
    for direction in range(1, 19):
        for t in range(5):
            total = None
            for k in range(3):
                if VELOCITIES[direction][k] != 0:
                    addend = VELOCITIES[direction][k] * tables[k][t]
                    total = addend if total is None else total + addend
            link_table[direction - 1, t : t + 1, :] = total

    index_a = to_bf16(lax.broadcasted_iota(jnp.int32, (48, LANES), 0))
    index_b = to_bf16(lax.broadcasted_iota(jnp.int32, (16, LANES), 0))
    one = jnp.ones((), BF16)
    zero = jnp.zeros((), BF16)

    def spread(ref, r):
        row = ref[pl.ds(r, SUBS, stride=0), :]
        return jnp.concatenate([row, row], axis=0).astype(BF16)

    def slot_rows(buffers, r):
        first_of, second_of, value_of, rest_of = buffers
        a = spread(first_of, r)
        b = spread(second_of, r)
        high = spread(value_of, r)
        low = spread(rest_of, r)
        left = [jnp.where(index_a[16 * i : 16 * i + 16] == a, one, zero) for i in range(3)]
        mask = index_b == b
        right = [jnp.where(mask, high, zero), jnp.where(mask, low, zero)]
        return jnp.concatenate(left, axis=0), jnp.concatenate(right, axis=0)

    def hot_rows(first_row, second_row, values):
        a = jnp.broadcast_to(to_bf16(first_row), (48, LANES))
        b = jnp.broadcast_to(to_bf16(second_row), (16, LANES))
        left = jnp.where(index_a == a, one, zero)
        mask = index_b == b
        right = []
        for value in values:
            high, low = split(value)
            right.append(
                jnp.concatenate(
                    [
                        jnp.where(mask, jnp.broadcast_to(high, (16, LANES)), zero),
                        jnp.where(mask, jnp.broadcast_to(low, (16, LANES)), zero),
                    ],
                    axis=0,
                )
            )
        return left, right

    def look_up(g, buffers):
        first_of, second_of, value_of, rest_of = buffers
        for side in range(2):
            index = 2 * g + side
            half = index // 9
            first_row = (index - 9 * half) * (2 * half_rows // 18)
            weight6 = jnp.where(index < 6, 6.0 * WEIGHTS[1], 6.0 * WEIGHTS[7]).astype(F32)
            lookup = [
                jnp.broadcast_to(link_table[index, t : t + 1, :], (SUBS, LANES)) for t in range(5)
            ]
            for x in range(width_x):
                mark = marks[
                    pl.ds(pl.multiple_of(first_row + SUBS * x, SUBS), SUBS),
                    pl.ds(pl.multiple_of(half * LANES, LANES), LANES),
                ]
                live = mark > 0.0
                scaled = mark
                level = jnp.zeros((SUBS, LANES), F32)
                for t in range(1, 5):
                    above = mark > 2.0 ** (8 * t + 6)
                    scaled = jnp.where(above, mark * 2.0 ** (-8 * t), scaled)
                    level = jnp.where(above, float(t), level)
                place = jnp.where(live, scaled - float(LANES), 0.0).astype(jnp.int32)
                speed = jnp.take_along_axis(lookup[0], place, axis=1)
                for t in range(1, 5):
                    found = jnp.take_along_axis(lookup[t], place, axis=1)
                    speed = jnp.where(level == float(t), found, speed)
                leaving = relaxed[index + 1, x]
                back = leaving - weight6 * density[x] * speed
                bounced[index, x] = jnp.where(live, back, NO_LINK)
                force = leaving + back
                if side == 1:
                    force = -force
                high_part = place // 16
                first = jnp.where(live, level * 8.0 + high_part.astype(F32), -1.0)
                second = (place - 16 * high_part).astype(F32)
                where = side * width_x * SUBS + SUBS * x
                first_of[where : where + SUBS] = first
                second_of[where : where + SUBS] = second
                force = jnp.where(live, force, 0.0)
                high = force.astype(BF16).astype(F32)
                value_of[where : where + SUBS] = high
                rest_of[where : where + SUBS] = force - high

    def add_up(g, buffers):
        lefts, rights = [], []
        for r in range(2 * width_x * SUBS):
            left, right = slot_rows(buffers, r)
            lefts.append(left)
            rights.append(right)
        sums[g] = lax.dot_general(
            jnp.concatenate(lefts, axis=1),
            jnp.concatenate(rights, axis=1),
            NT,
            preferred_element_type=F32,
        )

    look_up(0, even_buffers)

    def two_groups(i, carry):
        look_up(2 * i + 1, odd_buffers)
        add_up(2 * i, even_buffers)
        look_up(2 * i + 2, even_buffers)
        add_up(2 * i + 1, odd_buffers)
        return carry

    lax.fori_loop(0, 4, two_groups, 0)
    add_up(8, even_buffers)

    for out in (to_left, to_self, to_right):
        out[...] = jnp.zeros(out.shape, F32)
    totals = []
    for k in range(3):
        total = None
        for g in range(9):
            c = VELOCITIES[2 * g + 1][k]
            if c == 0:
                continue
            if total is None:
                total = sums[g] if c > 0 else -sums[g]
            else:
                total = total + sums[g] if c > 0 else total - sums[g]
        totals.append(total)

    pairs = pair_first.shape[2]
    lefts = []
    rights = [[], [], []]
    for start in range(0, pairs, LANES):
        here = slice(start, start + LANES)
        first = pair_first[0, :, here]
        second = pair_second[0, :, here]
        first_wide = jnp.broadcast_to(first, (SUBS, LANES))
        place = jnp.broadcast_to(second % LANES, (SUBS, LANES))
        level = second // LANES
        gap = pair_gap[0, :, here]
        rate = None
        for k in range(3):
            table = jnp.broadcast_to(tables[k][2], (SUBS, LANES))
            first_speed = jnp.take_along_axis(table, first_wide, axis=1)[:1]
            second_speed = None
            for t in range(5):
                table = jnp.broadcast_to(tables[k][t], (SUBS, LANES))
                found = jnp.take_along_axis(table, place, axis=1)[:1]
                second_speed = found if t == 0 else jnp.where(level == t, found, second_speed)
            addend = (first_speed - second_speed) * pair_normal[k, 0, :, here]
            rate = addend if rate is None else rate + addend
        resist = LUB_COEF * (1.0 / jnp.maximum(gap, GAP_FLOOR) - 1.0 / GAP_CUTOFF)
        number = start + lane
        factor = jnp.where(number < pair_count[...], -resist * rate, 0.0)
        values = [factor * pair_normal[k, 0, :, here] for k in range(3)]
        first = first + 4 * slots
        for ref, these in ((first, values), (second, [-v for v in values])):
            left, right = hot_rows(ref // 16, ref % 16, these)
            lefts.append(left)
            for k in range(3):
                rights[k].append(right[k])
    left = jnp.concatenate(lefts, axis=1)
    for k in range(3):
        total = totals[k] + lax.dot_general(
            left, jnp.concatenate(rights[k], axis=1), NT, preferred_element_type=F32
        )
        value = total[:, :16] + total[:, 16:32]
        first_of[0:48] = jnp.concatenate([value, jnp.zeros((48, LANES - 16), F32)], axis=1)
        line = None
        for s in range(4):
            piece = first_of[pl.ds(s, NEAR, stride=4), :]
            if s:
                piece = pltpu.roll(piece, 16 * s, axis=1)
            line = piece if line is None else line + piece
        for code in range(NEAR):
            row = SUBS * (code % 3) + k
            [to_left, to_self, to_right][code // 3][row : row + 1, :] = line[code : code + 1]


def stream_kernel(relaxed, bounced, from_left, from_right, from_pair, from_cross, out):
    even = lax.rem(lax.axis_index("grad"), 2) == 0
    low_rows = [jnp.where(even, from_cross[j], from_pair[j]) for j in range(5)]
    high_rows = [jnp.where(even, from_pair[j], from_cross[j]) for j in range(5)]
    width_x, width_y = relaxed.shape[1], relaxed.shape[2]
    for direction, (cx, cy, cz) in enumerate(VELOCITIES):
        for x in range(width_x):
            source = x - cx
            if source < 0:
                tile = from_left[RIGHTWARD.index(direction)]
            elif source >= width_x:
                tile = from_right[LEFTWARD.index(direction)]
            else:
                tile = relaxed[direction, source]
            if cy != 0:
                tile = pltpu.roll(tile, cy % width_y, axis=0)
                row = lax.broadcasted_iota(jnp.int32, tile.shape, 0)
                if cy > 0:
                    ghost = low_rows[UPWARD.index(direction)][x : x + 1, :]
                    tile = jnp.where(row == 0, jnp.broadcast_to(ghost, tile.shape), tile)
                else:
                    ghost = high_rows[DOWNWARD.index(direction)][x : x + 1, :]
                    tile = jnp.where(row == width_y - 1, jnp.broadcast_to(ghost, tile.shape), tile)
            if cz != 0:
                tile = pltpu.roll(tile, cz % LANES, axis=1)
            if direction > 0:
                opposite = direction + 1 if direction % 2 == 1 else direction - 1
                back = bounced[opposite - 1, x]
                tile = jnp.where(back < 0.5 * NO_LINK, back, tile)
            out[direction, x] = tile


def finish_kernel(own, one, other, speed, force, moved):
    slots = force.shape[3]
    total = own[...] + one[...] + other[...]
    for k in range(3):
        line = total[k : k + 1, :slots]
        force[k, 0] = line
        moved[k, 0] = speed[k : k + 1, :slots] + INV_MASS * line


def send(block, axis, distance):
    count = lax.axis_size(axis)
    return lax.ppermute(block, axis, [(i, (i + distance) % count) for i in range(count)])


def shape_of(*dims):
    return jax.ShapeDtypeStruct(dims, F32)


def local_of(*dims):
    return pltpu.VMEM(dims, F32)


def local(*arrays):
    return [pltpu.with_memory_space_constraint(array, pltpu.VMEM) for array in arrays]


def mark_links(first, steps, half_rows, count, link_arrays, *before):
    links = link_arrays[0].shape[2]
    width = links // 2
    link_spec = pl.BlockSpec((1, 1, width), lambda i: (0, 0, i + first))
    whole = pl.BlockSpec((half_rows, 2 * LANES), lambda i: (0, 0))
    one = pl.BlockSpec((1, 1), lambda i: (0, 0))
    return pl.pallas_call(
        functools.partial(mark_kernel, first),
        name="mark",
        grid=(steps,),
        in_specs=[one, link_spec, link_spec, link_spec] + [whole] * len(before),
        out_specs=whole,
        out_shape=local_of(half_rows, 2 * LANES),
    )(count, *link_arrays, *local(*before))


def per_device(
    populations,
    le_offset,
    sphere_velocity,
    link_cell,
    link_dir,
    link_sphere,
    link_count,
    pair_first,
    pair_second,
    pair_count,
    pair_gap,
    pair_normal,
):
    width_x, width_y, depth = populations.shape[1:]
    slots = sphere_velocity.shape[3]
    flow_count = lax.axis_size("flow")
    grad_count = lax.axis_size("grad")
    assert depth == LANES and width_y == SUBS and width_x == SUBS and 2 * slots == LANES
    assert grad_count % 2 == 0

    relaxed, density, right_msg, left_msg, own_line = pl.pallas_call(
        collide_kernel,
        name="collide",
        in_specs=[VMEM, VMEM],
        out_specs=[VMEM] * 5,
        out_shape=[
            local_of(19, width_x, width_y, depth),
            local_of(width_x, width_y, depth),
            local_of(11, SUBS, LANES),
            local_of(11, SUBS, LANES),
            local_of(3, LANES),
        ],
    )(populations, sphere_velocity)

    from_right = send(left_msg, "flow", -1)
    from_left = send(right_msg, "flow", 1)

    half_rows = 9 * width_x * width_y
    link_arrays = [link_cell, link_dir, link_sphere]
    marks = mark_links(0, 1, half_rows, link_count, link_arrays)

    msg_pair, msg_cross, own_speed = pl.pallas_call(
        prepare_kernel,
        name="prepare",
        in_specs=[VMEM] * 5,
        out_specs=[VMEM] * 3,
        out_shape=[
            local_of(7, SUBS, LANES),
            local_of(7, SUBS, LANES),
            local_of(2, SUBS, LANES),
        ],
        scratch_shapes=[pltpu.VMEM((10, 3 * SUBS, LANES), F32)],
    )(le_offset.reshape(1, 1), *local(right_msg, left_msg, from_left, from_right))

    def exchange(hops, msg_pair, msg_cross, own_speed, marks, link_count, *link_arrays):
        top = grad_count - 1
        pairs, cross, wrap = [], [], []
        for a in range(flow_count):
            line = a * grad_count
            for b in range(grad_count):
                pairs.append((line + b, line + (b ^ 1)))
                if 0 < b < top:
                    cross.append((line + b, line + b + (1 if b % 2 else -1)))
            cross.append(((a + hops) % flow_count * grad_count + top, line))
            cross.append(((a - hops) % flow_count * grad_count, line + top))
            wrap += [(line, line + top), (line + top, line)]
        axes = ("flow", "grad")
        from_pair = lax.ppermute(msg_pair, axes, pairs)
        from_wrap = lax.ppermute(own_speed, axes, wrap)
        from_cross = lax.ppermute(msg_cross, axes, cross)
        marks = mark_links(1, 1, half_rows, link_count, link_arrays, marks)
        return from_pair, from_cross, from_wrap, marks

    from_pair, from_cross, from_wrap, marks = lax.switch(
        lax.div(le_offset[0], width_x),
        [functools.partial(exchange, hops) for hops in range(flow_count)],
        msg_pair,
        msg_cross,
        own_speed,
        marks,
        link_count,
        *link_arrays,
    )

    bounced, to_left, to_self, to_right = pl.pallas_call(
        force_kernel,
        name="force",
        in_specs=[VMEM] * 12,
        out_specs=[VMEM] * 4,
        out_shape=[local_of(18, width_x, width_y, depth)] + [local_of(3 * SUBS, LANES)] * 3,
        scratch_shapes=[
            pltpu.VMEM((18, SUBS, LANES), F32),
            *[pltpu.VMEM((2 * width_x * SUBS, LANES), F32)] * 8,
            pltpu.VMEM((9, 48, 32), F32),
        ],
    )(
        pair_count,
        *local(relaxed, density, marks, own_speed, from_pair, from_cross, from_wrap),
        pair_first,
        pair_second,
        pair_gap,
        pair_normal,
    )

    updated = pl.pallas_call(
        stream_kernel,
        name="stream",
        in_specs=[VMEM] * 6,
        out_specs=VMEM,
        out_shape=shape_of(19, width_x, width_y, depth),
    )(*local(relaxed, bounced, from_left, from_right, from_pair, from_cross))

    column = to_self + send(to_left, "flow", -1) + send(to_right, "flow", 1)
    from_above = send(column[:SUBS], "grad", -1)
    from_below = send(column[2 * SUBS :], "grad", 1)
    line = shape_of(3, 1, 1, slots)
    sphere_force, velocity_next = pl.pallas_call(
        finish_kernel,
        name="finish",
        in_specs=[VMEM] * 4,
        out_specs=[VMEM] * 2,
        out_shape=[line, line],
    )(*local(column[SUBS : 2 * SUBS], from_above, from_below, own_line))

    return updated, sphere_force, velocity_next


def solution(mesh):
    in_specs = (
        P(None, "flow", "grad", None),
        P(),
        P(None, "flow", "grad", None),
        P("flow", "grad", None),
        P("flow", "grad", None),
        P("flow", "grad", None),
        P("flow", "grad"),
        P("flow", "grad", None),
        P("flow", "grad", None),
        P("flow", "grad"),
        P("flow", "grad", None),
        P(None, "flow", "grad", None),
    )
    out_specs = (
        P(None, "flow", "grad", None),
        P(None, "flow", "grad", None),
        P(None, "flow", "grad", None),
    )
    return jax.shard_map(
        per_device, mesh=mesh, in_specs=in_specs, out_specs=out_specs, check_vma=False
    )
```

```python
import functools

import jax
import jax.numpy as jnp
from jax import lax
from jax.experimental import pallas as pl
from jax.experimental.pallas import tpu as pltpu
from jax.sharding import PartitionSpec as P


VELOCITIES = [
    (0, 0, 0),
    (1, 0, 0),
    (-1, 0, 0),
    (0, 1, 0),
    (0, -1, 0),
    (0, 0, 1),
    (0, 0, -1),
    (1, 1, 0),
    (-1, -1, 0),
    (1, -1, 0),
    (-1, 1, 0),
    (1, 0, 1),
    (-1, 0, -1),
    (1, 0, -1),
    (-1, 0, 1),
    (0, 1, 1),
    (0, -1, -1),
    (0, 1, -1),
    (0, -1, 1),
]
WEIGHTS = [1.0 / 3.0] + [1.0 / 18.0] * 6 + [1.0 / 36.0] * 12
UPWARD = [3, 7, 10, 15, 17]
DOWNWARD = [4, 8, 9, 16, 18]
RIGHTWARD = [1, 7, 9, 11, 13]
LEFTWARD = [2, 8, 10, 12, 14]
RELAX_TIME = 0.8
SHEAR_SPEED = 0.1
LUB_COEF = 0.5
GAP_FLOOR = 0.1
GAP_CUTOFF = 1.0
INV_MASS = 1.0 / 523.6
LANES = 128
SUBS = 8
NEAR = 9
NO_LINK = 1e30
BF16 = jnp.bfloat16
F32 = jnp.float32
NT = (((1,), (1,)), ((), ()))

VMEM = pl.BlockSpec(memory_space=pltpu.VMEM)


def collide_kernel(
    pops, speed, relaxed, density, right_msg, left_msg, near_msg, far_msg, own_line
):
    width_x, width_y = pops.shape[1], pops.shape[2]
    slots = speed.shape[3]
    for x in range(width_x):
        current = [pops[d, x] for d in range(19)]
        total = functools.reduce(lambda p, q: p + q, current)
        density[x] = total
        inverse = 1.0 / total
        speeds = []
        for axis_id in range(3):
            running = None
            for direction, vector in enumerate(VELOCITIES):
                if vector[axis_id] == 0:
                    continue
                if running is None:
                    running = current[direction]
                elif vector[axis_id] > 0:
                    running = running + current[direction]
                else:
                    running = running - current[direction]
            speeds.append(running * inverse)
        base = 1.0 - 1.5 * (
            speeds[0] * speeds[0] + speeds[1] * speeds[1] + speeds[2] * speeds[2]
        )
        for direction, vector in enumerate(VELOCITIES):
            c_dot = None
            for axis_id in range(3):
                if vector[axis_id] != 0:
                    addend = vector[axis_id] * speeds[axis_id]
                    c_dot = addend if c_dot is None else c_dot + addend
            shape = base if c_dot is None else base + c_dot * (3.0 + 4.5 * c_dot)
            equil = WEIGHTS[direction] * total * shape
            value = current[direction] - (current[direction] - equil) * (1.0 / RELAX_TIME)
            relaxed[direction, x] = value
            if x == width_x - 1 and direction in RIGHTWARD:
                right_msg[RIGHTWARD.index(direction)] = value
            if x == 0 and direction in LEFTWARD:
                left_msg[LEFTWARD.index(direction)] = value
            if direction in UPWARD:
                left_msg[5 + UPWARD.index(direction), x : x + 1, :] = value[width_y - 1 :, :]
            if direction in DOWNWARD:
                right_msg[5 + DOWNWARD.index(direction), x : x + 1, :] = value[:1, :]
    right_msg[10] = jnp.zeros((SUBS, LANES), F32)
    left_msg[10] = jnp.zeros((SUBS, LANES), F32)
    for k in range(3):
        row = speed[k, 0]
        twice = jnp.concatenate([row] * (LANES // slots), axis=1)
        right_msg[10, k : k + 1, :] = twice
        left_msg[10, k : k + 1, :] = twice
        own_line[k : k + 1, :] = twice
    even = lax.rem(lax.axis_index("flow"), 2) == 0
    for i in range(11):
        near_msg[i] = jnp.where(even, right_msg[i], left_msg[i])
        far_msg[i] = jnp.where(even, left_msg[i], right_msg[i])


def sort_sides(axis, near, far):
    even = lax.rem(lax.axis_index(axis), 2) == 0
    near = [near[i] for i in range(near.shape[0])]
    far = [far[i] for i in range(far.shape[0])]
    lower = [jnp.where(even, q, p) for p, q in zip(near, far)]
    higher = [jnp.where(even, p, q) for p, q in zip(near, far)]
    return lower, higher


def prepare_kernel(
    offset, own_right, own_left, from_near, from_far, msg_pair, msg_cross, own_speed, rows
):
    width_x = own_right.shape[1]
    from_left, from_right = sort_sides("flow", from_near, from_far)
    grad_index = lax.axis_index("grad")
    at_top = grad_index == lax.axis_size("grad") - 1
    at_bottom = grad_index == 0
    even = lax.rem(grad_index, 2) == 0
    rest = jnp.broadcast_to(lax.rem(offset[...], width_x), (width_x, LANES))
    up_rest = jnp.where(at_top, rest, 0)
    down_rest = jnp.where(at_bottom, rest, 0)
    top_boost = jnp.where(at_top, 1.0, 0.0)
    bottom_boost = jnp.where(at_bottom, 1.0, 0.0)

    def window(j, start, sign, amount):
        moved = rows[j, start : start + width_x, :]
        for r in range(1, width_x):
            first = start + sign * r
            moved = jnp.where(amount == r, rows[j, first : first + width_x, :], moved)
        return moved

    ups = []
    for j, direction in enumerate(UPWARD):
        step = VELOCITIES[direction][0]
        boost = 6.0 * WEIGHTS[direction] * step * SHEAR_SPEED
        rows[j, SUBS : 2 * SUBS] = own_left[5 + j]
        rows[j, 2 * SUBS : 3 * SUBS] = from_right[5 + j]
        if step > 0:
            slab = from_left[RIGHTWARD.index(direction)]
            rows[j, SUBS - 1 : SUBS] = slab[SUBS - 1 :, :]
        moved = window(j, SUBS - step, 1, up_rest)
        if step != 0:
            moved = moved - boost * top_boost
        ups.append(moved)
    for j, direction in enumerate(DOWNWARD):
        step = VELOCITIES[direction][0]
        boost = 6.0 * WEIGHTS[direction] * step * SHEAR_SPEED
        rows[5 + j, :SUBS] = from_left[5 + j]
        rows[5 + j, SUBS : 2 * SUBS] = own_right[5 + j]
        if step < 0:
            slab = from_right[LEFTWARD.index(direction)]
            rows[5 + j, 2 * SUBS : 2 * SUBS + 1] = slab[:1, :]
        moved = window(5 + j, SUBS - step, -1, down_rest)
        if step != 0:
            moved = moved + boost * bottom_boost
        msg_pair[j] = jnp.where(even, ups[j], moved)
        msg_cross[j] = jnp.where(even, moved, ups[j])
    three = [from_left[10], own_right[10], from_right[10]]
    for out, first in ((msg_pair, 5), (msg_cross, 5), (own_speed, 0)):
        for f in range(3):
            for k in range(3):
                row = 3 * f + k
                out[first + row // SUBS, row % SUBS : row % SUBS + 1, :] = three[f][k : k + 1, :]


def to_bf16(value):
    return value.astype(F32).astype(BF16)


def mark_kernel(first_step, count, cell, direction, sphere, *refs):
    marks = refs[-1]
    step = pl.program_id(0)
    width = cell.shape[2]
    half_rows = marks.shape[0]
    q = cell[0]
    ref = sphere[0]
    row = (direction[0] - 1) * (2 * half_rows // 18) + q // LANES
    z = q % LANES
    half = (row >= half_rows).astype(jnp.int32)
    row = row - half * half_rows
    number = (first_step + step) * width + lax.broadcasted_iota(jnp.int32, (1, width), 1)
    level = ref // LANES
    scale = jnp.where(level == 0, 1.0, 0.0)
    for t in range(1, 5):
        scale = jnp.where(level == t, 2.0 ** (8 * t), scale)
    code = jnp.where(number < count[...], (LANES + ref % LANES).astype(F32) * scale, 0.0)
    block = half_rows // 3
    parts = []
    for first in range(0, half_rows, block):
        local = row - first
        local = to_bf16(jnp.where((local >= 0) & (local < block), local, 255))
        index = to_bf16(lax.broadcasted_iota(jnp.int32, (block, width), 0))
        parts.append(
            jnp.where(
                index == jnp.broadcast_to(local, (block, width)), jnp.ones((), BF16), jnp.zeros((), BF16)
            )
        )
    rows_hot = jnp.concatenate(parts, axis=0)
    column = to_bf16(z + LANES * half)
    index = to_bf16(lax.broadcasted_iota(jnp.int32, (2 * LANES, width), 0))
    columns = jnp.where(
        index == jnp.broadcast_to(column, (2 * LANES, width)),
        jnp.broadcast_to(code.astype(BF16), (2 * LANES, width)),
        jnp.zeros((), BF16),
    )
    part = lax.dot_general(rows_hot, columns, NT, preferred_element_type=F32)

    @pl.when(step == 0)
    def _():
        marks[...] = refs[0][...] + part if len(refs) == 2 else part

    @pl.when(step > 0)
    def _():
        marks[...] += part


def split(value):
    high = value.astype(BF16)
    return high, (value - high.astype(F32)).astype(BF16)


def force_kernel(
    pair_count,
    relaxed,
    density,
    marks,
    own_speed,
    from_pair,
    from_cross,
    from_wrap,
    pair_first,
    pair_second,
    pair_gap,
    pair_normal,
    bounced,
    to_near,
    to_self,
    to_far,
    link_table,
    *scratch,
):
    width_x = relaxed.shape[1]
    slots = LANES // 2
    even_buffers, odd_buffers, sums = scratch[:4], scratch[4:8], scratch[8]
    first_of = odd_buffers[0]
    half_rows = marks.shape[0]
    lane = lax.broadcasted_iota(jnp.int32, (1, LANES), 1)
    grad_index = lax.axis_index("grad")
    even = lax.rem(grad_index, 2) == 0
    even_flow = lax.rem(lax.axis_index("flow"), 2) == 0
    at_edge = (grad_index == 0) | (grad_index == lax.axis_size("grad") - 1)
    sources = [[], [], []]
    for tile in range(2):
        near = from_pair[5 + tile]
        far = jnp.where(at_edge, from_wrap[tile], from_cross[5 + tile])
        sources[0].append(jnp.where(even, far, near))
        sources[1].append(own_speed[tile])
        sources[2].append(jnp.where(even, near, far))

    def speed_row(code, k):
        row = 3 * (code // 3) + k
        return sources[code % 3][row // SUBS][row % SUBS : row % SUBS + 1, :]

    tables = []
    for k in range(3):
        rows = []
        for t in range(5):
            low = speed_row(2 * t, k)
            high = speed_row(min(2 * t + 1, NEAR - 1), k)
            rows.append(jnp.where(lane < slots, low, high))
        tables.append(rows)
    for direction in range(1, 19):
        for t in range(5):
            total = None
            for k in range(3):
                if VELOCITIES[direction][k] != 0:
                    addend = VELOCITIES[direction][k] * tables[k][t]
                    total = addend if total is None else total + addend
            link_table[direction - 1, t : t + 1, :] = total

    index_a = to_bf16(lax.broadcasted_iota(jnp.int32, (48, LANES), 0))
    index_b = to_bf16(lax.broadcasted_iota(jnp.int32, (16, LANES), 0))
    one = jnp.ones((), BF16)
    zero = jnp.zeros((), BF16)

    def spread(ref, r):
        row = ref[pl.ds(r, SUBS, stride=0), :]
        return jnp.concatenate([row, row], axis=0).astype(BF16)

    def slot_rows(buffers, r):
        first_of, second_of, value_of, rest_of = buffers
        a = spread(first_of, r)
        b = spread(second_of, r)
        high = spread(value_of, r)
        low = spread(rest_of, r)
        left = [jnp.where(index_a[16 * i : 16 * i + 16] == a, one, zero) for i in range(3)]
        mask = index_b == b
        right = [jnp.where(mask, high, zero), jnp.where(mask, low, zero)]
        return jnp.concatenate(left, axis=0), jnp.concatenate(right, axis=0)

    def hot_rows(first_row, second_row, values):
        a = jnp.broadcast_to(to_bf16(first_row), (48, LANES))
        b = jnp.broadcast_to(to_bf16(second_row), (16, LANES))
        left = jnp.where(index_a == a, one, zero)
        mask = index_b == b
        right = []
        for value in values:
            high, low = split(value)
            right.append(
                jnp.concatenate(
                    [
                        jnp.where(mask, jnp.broadcast_to(high, (16, LANES)), zero),
                        jnp.where(mask, jnp.broadcast_to(low, (16, LANES)), zero),
                    ],
                    axis=0,
                )
            )
        return left, right

    def look_up(g, buffers):
        first_of, second_of, value_of, rest_of = buffers
        for side in range(2):
            index = 2 * g + side
            half = index // 9
            first_row = (index - 9 * half) * (2 * half_rows // 18)
            weight6 = jnp.where(index < 6, 6.0 * WEIGHTS[1], 6.0 * WEIGHTS[7]).astype(F32)
            lookup = [
                jnp.broadcast_to(link_table[index, t : t + 1, :], (SUBS, LANES)) for t in range(5)
            ]
            for x in range(width_x):
                mark = marks[
                    pl.ds(pl.multiple_of(first_row + SUBS * x, SUBS), SUBS),
                    pl.ds(pl.multiple_of(half * LANES, LANES), LANES),
                ]
                live = mark > 0.0
                scaled = mark
                level = jnp.zeros((SUBS, LANES), F32)
                for t in range(1, 5):
                    above = mark > 2.0 ** (8 * t + 6)
                    scaled = jnp.where(above, mark * 2.0 ** (-8 * t), scaled)
                    level = jnp.where(above, float(t), level)
                place = jnp.where(live, scaled - float(LANES), 0.0).astype(jnp.int32)
                speed = jnp.take_along_axis(lookup[0], place, axis=1)
                for t in range(1, 5):
                    found = jnp.take_along_axis(lookup[t], place, axis=1)
                    speed = jnp.where(level == float(t), found, speed)
                leaving = relaxed[index + 1, x]
                back = leaving - weight6 * density[x] * speed
                bounced[index, x] = jnp.where(live, back, NO_LINK)
                force = leaving + back
                if side == 1:
                    force = -force
                high_part = place // 16
                first = jnp.where(live, level * 8.0 + high_part.astype(F32), -1.0)
                second = (place - 16 * high_part).astype(F32)
                where = side * width_x * SUBS + SUBS * x
                first_of[where : where + SUBS] = first
                second_of[where : where + SUBS] = second
                force = jnp.where(live, force, 0.0)
                high = force.astype(BF16).astype(F32)
                value_of[where : where + SUBS] = high
                rest_of[where : where + SUBS] = force - high

    def add_up(g, buffers):
        lefts, rights = [], []
        for r in range(2 * width_x * SUBS):
            left, right = slot_rows(buffers, r)
            lefts.append(left)
            rights.append(right)
        sums[g] = lax.dot_general(
            jnp.concatenate(lefts, axis=1),
            jnp.concatenate(rights, axis=1),
            NT,
            preferred_element_type=F32,
        )

    look_up(0, even_buffers)

    def two_groups(i, carry):
        look_up(2 * i + 1, odd_buffers)
        add_up(2 * i, even_buffers)
        look_up(2 * i + 2, even_buffers)
        add_up(2 * i + 1, odd_buffers)
        return carry

    lax.fori_loop(0, 4, two_groups, 0)
    add_up(8, even_buffers)

    for out in (to_near, to_self, to_far):
        out[...] = jnp.zeros(out.shape, F32)
    totals = []
    for k in range(3):
        total = None
        for g in range(9):
            c = VELOCITIES[2 * g + 1][k]
            if c == 0:
                continue
            if total is None:
                total = sums[g] if c > 0 else -sums[g]
            else:
                total = total + sums[g] if c > 0 else total - sums[g]
        totals.append(total)

    pairs = pair_first.shape[2]
    lefts = []
    rights = [[], [], []]
    for start in range(0, pairs, LANES):
        here = slice(start, start + LANES)
        first = pair_first[0, :, here]
        second = pair_second[0, :, here]
        first_wide = jnp.broadcast_to(first, (SUBS, LANES))
        place = jnp.broadcast_to(second % LANES, (SUBS, LANES))
        level = second // LANES
        gap = pair_gap[0, :, here]
        rate = None
        for k in range(3):
            table = jnp.broadcast_to(tables[k][2], (SUBS, LANES))
            first_speed = jnp.take_along_axis(table, first_wide, axis=1)[:1]
            second_speed = None
            for t in range(5):
                table = jnp.broadcast_to(tables[k][t], (SUBS, LANES))
                found = jnp.take_along_axis(table, place, axis=1)[:1]
                second_speed = found if t == 0 else jnp.where(level == t, found, second_speed)
            addend = (first_speed - second_speed) * pair_normal[k, 0, :, here]
            rate = addend if rate is None else rate + addend
        resist = LUB_COEF * (1.0 / jnp.maximum(gap, GAP_FLOOR) - 1.0 / GAP_CUTOFF)
        number = start + lane
        factor = jnp.where(number < pair_count[...], -resist * rate, 0.0)
        values = [factor * pair_normal[k, 0, :, here] for k in range(3)]
        first = first + 4 * slots
        for ref, these in ((first, values), (second, [-v for v in values])):
            left, right = hot_rows(ref // 16, ref % 16, these)
            lefts.append(left)
            for k in range(3):
                rights[k].append(right[k])
    left = jnp.concatenate(lefts, axis=1)
    for k in range(3):
        total = totals[k] + lax.dot_general(
            left, jnp.concatenate(rights[k], axis=1), NT, preferred_element_type=F32
        )
        value = total[:, :16] + total[:, 16:32]
        first_of[0:48] = jnp.concatenate([value, jnp.zeros((48, LANES - 16), F32)], axis=1)
        line = None
        for s in range(4):
            piece = first_of[pl.ds(s, NEAR, stride=4), :]
            if s:
                piece = pltpu.roll(piece, 16 * s, axis=1)
            line = piece if line is None else line + piece
        for g in range(3):
            row = SUBS * g + k
            low, own, high = [line[3 * f + g : 3 * f + g + 1] for f in range(3)]
            to_near[row : row + 1, :] = jnp.where(even_flow, high, low)
            to_self[row : row + 1, :] = own
            to_far[row : row + 1, :] = jnp.where(even_flow, low, high)


def stream_kernel(relaxed, bounced, from_near, from_far, from_pair, from_cross, out):
    from_left, from_right = sort_sides("flow", from_near, from_far)
    low_rows, high_rows = sort_sides("grad", from_pair, from_cross)
    width_x, width_y = relaxed.shape[1], relaxed.shape[2]
    for direction, (cx, cy, cz) in enumerate(VELOCITIES):
        for x in range(width_x):
            source = x - cx
            if source < 0:
                tile = from_left[RIGHTWARD.index(direction)]
            elif source >= width_x:
                tile = from_right[LEFTWARD.index(direction)]
            else:
                tile = relaxed[direction, source]
            if cy != 0:
                tile = pltpu.roll(tile, cy % width_y, axis=0)
                row = lax.broadcasted_iota(jnp.int32, tile.shape, 0)
                if cy > 0:
                    ghost = low_rows[UPWARD.index(direction)][x : x + 1, :]
                    tile = jnp.where(row == 0, jnp.broadcast_to(ghost, tile.shape), tile)
                else:
                    ghost = high_rows[DOWNWARD.index(direction)][x : x + 1, :]
                    tile = jnp.where(row == width_y - 1, jnp.broadcast_to(ghost, tile.shape), tile)
            if cz != 0:
                tile = pltpu.roll(tile, cz % LANES, axis=1)
            if direction > 0:
                opposite = direction + 1 if direction % 2 == 1 else direction - 1
                back = bounced[opposite - 1, x]
                tile = jnp.where(back < 0.5 * NO_LINK, back, tile)
            out[direction, x] = tile


def finish_kernel(own, one, other, speed, force, moved):
    slots = force.shape[3]
    total = own[...] + one[...] + other[...]
    for k in range(3):
        line = total[k : k + 1, :slots]
        force[k, 0] = line
        moved[k, 0] = speed[k : k + 1, :slots] + INV_MASS * line


def swap(block, axis, far):
    count = lax.axis_size(axis)
    assert count % 2 == 0
    route = []
    for i in range(count):
        up = (i % 2 == 0) != far
        route.append((i, (i + (1 if up else -1)) % count))
    return lax.ppermute(block, axis, route)


def shape_of(*dims):
    return jax.ShapeDtypeStruct(dims, F32)


def local_of(*dims):
    return pltpu.VMEM(dims, F32)


def local(*arrays):
    return [pltpu.with_memory_space_constraint(array, pltpu.VMEM) for array in arrays]


def mark_links(first, steps, half_rows, count, link_arrays, *before):
    links = link_arrays[0].shape[2]
    width = links // 2
    link_spec = pl.BlockSpec((1, 1, width), lambda i: (0, 0, i + first))
    whole = pl.BlockSpec((half_rows, 2 * LANES), lambda i: (0, 0))
    one = pl.BlockSpec((1, 1), lambda i: (0, 0))
    return pl.pallas_call(
        functools.partial(mark_kernel, first),
        name="mark",
        grid=(steps,),
        in_specs=[one, link_spec, link_spec, link_spec] + [whole] * len(before),
        out_specs=whole,
        out_shape=local_of(half_rows, 2 * LANES),
    )(count, *link_arrays, *local(*before))


def one_step(
    populations,
    le_offset,
    sphere_velocity,
    link_cell,
    link_dir,
    link_sphere,
    link_count,
    pair_first,
    pair_second,
    pair_count,
    pair_gap,
    pair_normal,
):
    width_x, width_y, depth = populations.shape[1:]
    slots = sphere_velocity.shape[3]
    flow_count = lax.axis_size("flow")
    grad_count = lax.axis_size("grad")
    assert depth == LANES and width_y == SUBS and width_x == SUBS and 2 * slots == LANES
    assert grad_count % 2 == 0

    relaxed, density, right_msg, left_msg, near_msg, far_msg, own_line = pl.pallas_call(
        collide_kernel,
        name="collide",
        in_specs=[VMEM, VMEM],
        out_specs=[VMEM] * 7,
        out_shape=[
            local_of(19, width_x, width_y, depth),
            local_of(width_x, width_y, depth),
            local_of(11, SUBS, LANES),
            local_of(11, SUBS, LANES),
            local_of(11, SUBS, LANES),
            local_of(11, SUBS, LANES),
            local_of(3, LANES),
        ],
    )(populations, sphere_velocity)

    from_far = swap(far_msg, "flow", True)
    from_near = swap(near_msg, "flow", False)

    half_rows = 9 * width_x * width_y
    link_arrays = [link_cell, link_dir, link_sphere]
    marks = mark_links(0, 1, half_rows, link_count, link_arrays)

    msg_pair, msg_cross, own_speed = pl.pallas_call(
        prepare_kernel,
        name="prepare",
        in_specs=[VMEM] * 5,
        out_specs=[VMEM] * 3,
        out_shape=[
            local_of(7, SUBS, LANES),
            local_of(7, SUBS, LANES),
            local_of(2, SUBS, LANES),
        ],
        scratch_shapes=[pltpu.VMEM((10, 3 * SUBS, LANES), F32)],
    )(le_offset.reshape(1, 1), *local(right_msg, left_msg, from_near, from_far))

    def exchange(hops, msg_pair, msg_cross, own_speed, marks, link_count, *link_arrays):
        top = grad_count - 1
        pairs, cross, wrap = [], [], []
        for a in range(flow_count):
            line = a * grad_count
            for b in range(grad_count):
                pairs.append((line + b, line + (b ^ 1)))
                if 0 < b < top:
                    cross.append((line + b, line + b + (1 if b % 2 else -1)))
            cross.append(((a + hops) % flow_count * grad_count + top, line))
            cross.append(((a - hops) % flow_count * grad_count, line + top))
            wrap += [(line, line + top), (line + top, line)]
        axes = ("flow", "grad")
        from_pair = lax.ppermute(msg_pair, axes, pairs)
        from_wrap = lax.ppermute(own_speed, axes, wrap)
        from_cross = lax.ppermute(msg_cross, axes, cross)
        marks = mark_links(1, 1, half_rows, link_count, link_arrays, marks)
        return from_pair, from_cross, from_wrap, marks

    from_pair, from_cross, from_wrap, marks = lax.switch(
        lax.div(le_offset[0], width_x),
        [functools.partial(exchange, hops) for hops in range(flow_count)],
        msg_pair,
        msg_cross,
        own_speed,
        marks,
        link_count,
        *link_arrays,
    )

    bounced, to_near, to_self, to_far = pl.pallas_call(
        force_kernel,
        name="force",
        in_specs=[VMEM] * 12,
        out_specs=[VMEM] * 4,
        out_shape=[local_of(18, width_x, width_y, depth)] + [local_of(3 * SUBS, LANES)] * 3,
        scratch_shapes=[
            pltpu.VMEM((18, SUBS, LANES), F32),
            *[pltpu.VMEM((2 * width_x * SUBS, LANES), F32)] * 8,
            pltpu.VMEM((9, 48, 32), F32),
        ],
    )(
        pair_count,
        *local(relaxed, density, marks, own_speed, from_pair, from_cross, from_wrap),
        pair_first,
        pair_second,
        pair_gap,
        pair_normal,
    )

    updated = pl.pallas_call(
        stream_kernel,
        name="stream",
        in_specs=[VMEM] * 6,
        out_specs=VMEM,
        out_shape=shape_of(19, width_x, width_y, depth),
    )(*local(relaxed, bounced, from_near, from_far, from_pair, from_cross))

    column = to_self + swap(to_far, "flow", True) + swap(to_near, "flow", False)
    even = lax.axis_index("grad") % 2 == 0
    low, high = column[:SUBS], column[2 * SUBS :]
    from_cross_force = swap(jnp.where(even, low, high), "grad", True)
    from_pair_force = swap(jnp.where(even, high, low), "grad", False)
    line = shape_of(3, 1, 1, slots)
    sphere_force, velocity_next = pl.pallas_call(
        finish_kernel,
        name="finish",
        in_specs=[VMEM] * 4,
        out_specs=[VMEM] * 2,
        out_shape=[line, line],
    )(*local(column[SUBS : 2 * SUBS], from_pair_force, from_cross_force, own_line))

    return updated, sphere_force, velocity_next


def solution(mesh):
    in_specs = (
        P(None, "flow", "grad", None),
        P(),
        P(None, "flow", "grad", None),
        P("flow", "grad", None),
        P("flow", "grad", None),
        P("flow", "grad", None),
        P("flow", "grad"),
        P("flow", "grad", None),
        P("flow", "grad", None),
        P("flow", "grad"),
        P("flow", "grad", None),
        P(None, "flow", "grad", None),
    )
    out_specs = (
        P(None, "flow", "grad", None),
        P(None, "flow", "grad", None),
        P(None, "flow", "grad", None),
    )
    return jax.shard_map(
        one_step, mesh=mesh, in_specs=in_specs, out_specs=out_specs, check_vma=False
    )
```

```python
import functools

import jax
import jax.numpy as jnp
from jax import lax
from jax.experimental import pallas as pl
from jax.experimental.pallas import tpu as pltpu
from jax.sharding import PartitionSpec as P


VELOCITIES = [
    (0, 0, 0),
    (1, 0, 0),
    (-1, 0, 0),
    (0, 1, 0),
    (0, -1, 0),
    (0, 0, 1),
    (0, 0, -1),
    (1, 1, 0),
    (-1, -1, 0),
    (1, -1, 0),
    (-1, 1, 0),
    (1, 0, 1),
    (-1, 0, -1),
    (1, 0, -1),
    (-1, 0, 1),
    (0, 1, 1),
    (0, -1, -1),
    (0, 1, -1),
    (0, -1, 1),
]
WEIGHTS = [1.0 / 3.0] + [1.0 / 18.0] * 6 + [1.0 / 36.0] * 12
UPWARD = [3, 7, 10, 15, 17]
DOWNWARD = [4, 8, 9, 16, 18]
RIGHTWARD = [1, 7, 9, 11, 13]
LEFTWARD = [2, 8, 10, 12, 14]
RELAX_TIME = 0.8
SHEAR_SPEED = 0.1
LUB_COEF = 0.5
GAP_FLOOR = 0.1
GAP_CUTOFF = 1.0
INV_MASS = 1.0 / 523.6
LANES = 128
SUBS = 8
NEAR = 9
NO_LINK = 1e30
BF16 = jnp.bfloat16
F32 = jnp.float32
NT = (((1,), (1,)), ((), ()))

VMEM = pl.BlockSpec(memory_space=pltpu.VMEM)


def collide_kernel(
    pops, speed, relaxed, density, right_msg, left_msg, near_msg, far_msg, own_line
):
    width_x, width_y = pops.shape[1], pops.shape[2]
    slots = speed.shape[3]
    for x in range(width_x):
        current = [pops[d, x] for d in range(19)]
        total = functools.reduce(lambda p, q: p + q, current)
        density[x] = total
        inverse = 1.0 / total
        speeds = []
        for axis_id in range(3):
            running = None
            for direction, vector in enumerate(VELOCITIES):
                if vector[axis_id] == 0:
                    continue
                if running is None:
                    running = current[direction]
                elif vector[axis_id] > 0:
                    running = running + current[direction]
                else:
                    running = running - current[direction]
            speeds.append(running * inverse)
        base = 1.0 - 1.5 * (
            speeds[0] * speeds[0] + speeds[1] * speeds[1] + speeds[2] * speeds[2]
        )
        for direction, vector in enumerate(VELOCITIES):
            c_dot = None
            for axis_id in range(3):
                if vector[axis_id] != 0:
                    addend = vector[axis_id] * speeds[axis_id]
                    c_dot = addend if c_dot is None else c_dot + addend
            shape = base if c_dot is None else base + c_dot * (3.0 + 4.5 * c_dot)
            equil = WEIGHTS[direction] * total * shape
            value = current[direction] - (current[direction] - equil) * (1.0 / RELAX_TIME)
            relaxed[direction, x] = value
            if x == width_x - 1 and direction in RIGHTWARD:
                right_msg[RIGHTWARD.index(direction)] = value
            if x == 0 and direction in LEFTWARD:
                left_msg[LEFTWARD.index(direction)] = value
            if direction in UPWARD:
                left_msg[5 + UPWARD.index(direction), x : x + 1, :] = value[width_y - 1 :, :]
            if direction in DOWNWARD:
                right_msg[5 + DOWNWARD.index(direction), x : x + 1, :] = value[:1, :]
    right_msg[10] = jnp.zeros((SUBS, LANES), F32)
    left_msg[10] = jnp.zeros((SUBS, LANES), F32)
    for k in range(3):
        row = speed[k, 0]
        twice = jnp.concatenate([row] * (LANES // slots), axis=1)
        right_msg[10, k : k + 1, :] = twice
        left_msg[10, k : k + 1, :] = twice
        own_line[k : k + 1, :] = twice
    even = lax.rem(lax.axis_index("flow"), 2) == 0
    for i in range(11):
        near_msg[i] = jnp.where(even, right_msg[i], left_msg[i])
        far_msg[i] = jnp.where(even, left_msg[i], right_msg[i])


def sort_sides(axis, near, far):
    even = lax.rem(lax.axis_index(axis), 2) == 0
    near = [near[i] for i in range(near.shape[0])]
    far = [far[i] for i in range(far.shape[0])]
    lower = [jnp.where(even, q, p) for p, q in zip(near, far)]
    higher = [jnp.where(even, p, q) for p, q in zip(near, far)]
    return lower, higher


def prepare_kernel(
    offset, own_right, own_left, from_near, from_far, msg_pair, msg_cross, own_speed, rows
):
    width_x = own_right.shape[1]
    from_left, from_right = sort_sides("flow", from_near, from_far)
    grad_index = lax.axis_index("grad")
    at_top = grad_index == lax.axis_size("grad") - 1
    at_bottom = grad_index == 0
    even = lax.rem(grad_index, 2) == 0
    rest = jnp.broadcast_to(lax.rem(offset[...], width_x), (width_x, LANES))
    up_rest = jnp.where(at_top, rest, 0)
    down_rest = jnp.where(at_bottom, rest, 0)
    top_boost = jnp.where(at_top, 1.0, 0.0)
    bottom_boost = jnp.where(at_bottom, 1.0, 0.0)

    def window(j, start, sign, amount):
        moved = rows[j, start : start + width_x, :]
        for r in range(1, width_x):
            first = start + sign * r
            moved = jnp.where(amount == r, rows[j, first : first + width_x, :], moved)
        return moved

    ups = []
    for j, direction in enumerate(UPWARD):
        step = VELOCITIES[direction][0]
        boost = 6.0 * WEIGHTS[direction] * step * SHEAR_SPEED
        rows[j, SUBS : 2 * SUBS] = own_left[5 + j]
        rows[j, 2 * SUBS : 3 * SUBS] = from_right[5 + j]
        if step > 0:
            slab = from_left[RIGHTWARD.index(direction)]
            rows[j, SUBS - 1 : SUBS] = slab[SUBS - 1 :, :]
        moved = window(j, SUBS - step, 1, up_rest)
        if step != 0:
            moved = moved - boost * top_boost
        ups.append(moved)
    for j, direction in enumerate(DOWNWARD):
        step = VELOCITIES[direction][0]
        boost = 6.0 * WEIGHTS[direction] * step * SHEAR_SPEED
        rows[5 + j, :SUBS] = from_left[5 + j]
        rows[5 + j, SUBS : 2 * SUBS] = own_right[5 + j]
        if step < 0:
            slab = from_right[LEFTWARD.index(direction)]
            rows[5 + j, 2 * SUBS : 2 * SUBS + 1] = slab[:1, :]
        moved = window(5 + j, SUBS - step, -1, down_rest)
        if step != 0:
            moved = moved + boost * bottom_boost
        msg_pair[j] = jnp.where(even, ups[j], moved)
        msg_cross[j] = jnp.where(even, moved, ups[j])
    three = [from_left[10], own_right[10], from_right[10]]
    for out, first in ((msg_pair, 5), (msg_cross, 5), (own_speed, 0)):
        for f in range(3):
            for k in range(3):
                row = 3 * f + k
                out[first + row // SUBS, row % SUBS : row % SUBS + 1, :] = three[f][k : k + 1, :]


def to_bf16(value):
    return value.astype(F32).astype(BF16)


def mark_kernel(first_step, count, cell, direction, sphere, *refs):
    marks = refs[-1]
    step = pl.program_id(0)
    width = cell.shape[2]
    half_rows = marks.shape[0]
    q = cell[0]
    ref = sphere[0]
    row = (direction[0] - 1) * (2 * half_rows // 18) + q // LANES
    z = q % LANES
    half = (row >= half_rows).astype(jnp.int32)
    row = row - half * half_rows
    number = (first_step + step) * width + lax.broadcasted_iota(jnp.int32, (1, width), 1)
    level = ref // LANES
    scale = jnp.where(level == 0, 1.0, 0.0)
    for t in range(1, 5):
        scale = jnp.where(level == t, 2.0 ** (8 * t), scale)
    code = jnp.where(number < count[...], (LANES + ref % LANES).astype(F32) * scale, 0.0)
    block = half_rows // 3
    parts = []
    for first in range(0, half_rows, block):
        local = row - first
        local = to_bf16(jnp.where((local >= 0) & (local < block), local, 255))
        index = to_bf16(lax.broadcasted_iota(jnp.int32, (block, width), 0))
        parts.append(
            jnp.where(
                index == jnp.broadcast_to(local, (block, width)), jnp.ones((), BF16), jnp.zeros((), BF16)
            )
        )
    rows_hot = jnp.concatenate(parts, axis=0)
    column = to_bf16(z + LANES * half)
    index = to_bf16(lax.broadcasted_iota(jnp.int32, (2 * LANES, width), 0))
    columns = jnp.where(
        index == jnp.broadcast_to(column, (2 * LANES, width)),
        jnp.broadcast_to(code.astype(BF16), (2 * LANES, width)),
        jnp.zeros((), BF16),
    )
    part = lax.dot_general(rows_hot, columns, NT, preferred_element_type=F32)

    @pl.when(step == 0)
    def _():
        marks[...] = refs[0][...] + part if len(refs) == 2 else part

    @pl.when(step > 0)
    def _():
        marks[...] += part


def split(value):
    high = value.astype(BF16)
    return high, (value - high.astype(F32)).astype(BF16)


def force_kernel(
    pair_count,
    relaxed,
    density,
    marks,
    own_speed,
    from_pair,
    from_cross,
    from_wrap,
    pair_first,
    pair_second,
    pair_gap,
    pair_normal,
    bounced,
    to_near,
    to_self,
    to_far,
    link_table,
    *scratch,
):
    width_x = relaxed.shape[1]
    slots = LANES // 2
    even_buffers, odd_buffers, sums = scratch[:4], scratch[4:8], scratch[8]
    first_of, second_of = odd_buffers[:2]
    half_rows = marks.shape[0]
    lane = lax.broadcasted_iota(jnp.int32, (1, LANES), 1)
    grad_index = lax.axis_index("grad")
    even = lax.rem(grad_index, 2) == 0
    even_flow = lax.rem(lax.axis_index("flow"), 2) == 0
    at_edge = (grad_index == 0) | (grad_index == lax.axis_size("grad") - 1)
    sources = [[], [], []]
    for tile in range(2):
        near = from_pair[5 + tile]
        far = jnp.where(at_edge, from_wrap[tile], from_cross[5 + tile])
        sources[0].append(jnp.where(even, far, near))
        sources[1].append(own_speed[tile])
        sources[2].append(jnp.where(even, near, far))

    def speed_row(code, k):
        row = 3 * (code // 3) + k
        return sources[code % 3][row // SUBS][row % SUBS : row % SUBS + 1, :]

    tables = []
    for k in range(3):
        rows = []
        for t in range(5):
            low = speed_row(2 * t, k)
            high = speed_row(min(2 * t + 1, NEAR - 1), k)
            rows.append(jnp.where(lane < slots, low, high))
        tables.append(rows)
    for direction in range(1, 19):
        for t in range(5):
            total = None
            for k in range(3):
                if VELOCITIES[direction][k] != 0:
                    addend = VELOCITIES[direction][k] * tables[k][t]
                    total = addend if total is None else total + addend
            link_table[direction - 1, t : t + 1, :] = total

    index_a = to_bf16(lax.broadcasted_iota(jnp.int32, (48, LANES), 0))
    index_b = to_bf16(lax.broadcasted_iota(jnp.int32, (16, LANES), 0))
    one = jnp.ones((), BF16)
    zero = jnp.zeros((), BF16)

    def spread(ref, r):
        row = ref[pl.ds(r, SUBS, stride=0), :]
        return jnp.concatenate([row, row], axis=0).astype(BF16)

    def slot_rows(buffers, r):
        first_of, second_of, value_of, rest_of = buffers
        a = spread(first_of, r)
        b = spread(second_of, r)
        high = spread(value_of, r)
        low = spread(rest_of, r)
        left = [jnp.where(index_a[16 * i : 16 * i + 16] == a, one, zero) for i in range(3)]
        mask = index_b == b
        right = [jnp.where(mask, high, zero), jnp.where(mask, low, zero)]
        return jnp.concatenate(left, axis=0), jnp.concatenate(right, axis=0)

    def hot_rows(first_row, second_row, values):
        a = jnp.broadcast_to(to_bf16(first_row), (48, LANES))
        b = jnp.broadcast_to(to_bf16(second_row), (16, LANES))
        left = jnp.where(index_a == a, one, zero)
        mask = index_b == b
        right = []
        for value in values:
            high, low = split(value)
            right.append(
                jnp.concatenate(
                    [
                        jnp.where(mask, jnp.broadcast_to(high, (16, LANES)), zero),
                        jnp.where(mask, jnp.broadcast_to(low, (16, LANES)), zero),
                    ],
                    axis=0,
                )
            )
        return left, right

    def look_up(g, buffers):
        first_of, second_of, value_of, rest_of = buffers
        for side in range(2):
            index = 2 * g + side
            half = index // 9
            first_row = (index - 9 * half) * (2 * half_rows // 18)
            weight6 = jnp.where(index < 6, 6.0 * WEIGHTS[1], 6.0 * WEIGHTS[7]).astype(F32)
            lookup = [
                jnp.broadcast_to(link_table[index, t : t + 1, :], (SUBS, LANES)) for t in range(5)
            ]
            for x in range(width_x):
                mark = marks[
                    pl.ds(pl.multiple_of(first_row + SUBS * x, SUBS), SUBS),
                    pl.ds(pl.multiple_of(half * LANES, LANES), LANES),
                ]
                live = mark > 0.0
                scale = jnp.ones((SUBS, LANES), F32)
                first = jnp.zeros((SUBS, LANES), F32)
                levels = [mark > 2.0 ** (8 * t + 6) for t in range(1, 5)]
                for t, above in enumerate(levels, 1):
                    scale = jnp.where(above, 2.0 ** (-8 * t), scale)
                    first = jnp.where(above, 8.0 * t, first)
                place = (mark * scale).astype(jnp.int32) & (LANES - 1)
                speed = jnp.take_along_axis(lookup[0], place, axis=1)
                for t, above in enumerate(levels, 1):
                    found = jnp.take_along_axis(lookup[t], place, axis=1)
                    speed = jnp.where(above, found, speed)
                leaving = relaxed[index + 1, x]
                back = leaving - weight6 * density[x] * speed
                bounced[index, x] = jnp.where(live, back, NO_LINK)
                force = leaving + back
                first = first + (place >> 4).astype(F32)
                second = (place & 15).astype(F32)
                where = side * width_x * SUBS + SUBS * x
                first_of[where : where + SUBS] = first
                second_of[where : where + SUBS] = second
                force = jnp.where(live, force, 0.0)
                high = force.astype(BF16).astype(F32)
                value_of[where : where + SUBS] = high
                rest_of[where : where + SUBS] = force - high

    def add_up(g, buffers):
        for part in range(2):
            lefts, rights = [], []
            for r in range(part * 2 * width_x * SUBS // 2, (part + 1) * 2 * width_x * SUBS // 2):
                left, right = slot_rows(buffers, r)
                lefts.append(left)
                rights.append(right)
            sums[2 * g + part] = lax.dot_general(
                jnp.concatenate(rights, axis=1),
                jnp.concatenate(lefts, axis=1),
                NT,
                preferred_element_type=F32,
            )

    look_up(0, even_buffers)

    def two_groups(i, carry):
        look_up(2 * i + 1, odd_buffers)
        add_up(2 * i, even_buffers)
        look_up(2 * i + 2, even_buffers)
        add_up(2 * i + 1, odd_buffers)
        return carry

    lax.fori_loop(0, 4, two_groups, 0)
    add_up(8, even_buffers)

    for out in (to_near, to_self, to_far):
        out[...] = jnp.zeros(out.shape, F32)
    totals = []
    for k in range(3):
        total = None
        for direction in range(1, 19):
            c = VELOCITIES[direction][k]
            if c == 0:
                continue
            addend = sums[direction - 1]
            if total is None:
                total = addend if c > 0 else -addend
            else:
                total = total + addend if c > 0 else total - addend
        totals.append(total)

    pairs = pair_first.shape[2]
    lefts = []
    rights = [[], [], []]
    for start in range(0, pairs, LANES):
        here = slice(start, start + LANES)
        first = pair_first[0, :, here]
        second = pair_second[0, :, here]
        first_wide = jnp.broadcast_to(first, (SUBS, LANES))
        place = jnp.broadcast_to(second % LANES, (SUBS, LANES))
        level = second // LANES
        gap = pair_gap[0, :, here]
        rate = None
        for k in range(3):
            table = jnp.broadcast_to(tables[k][2], (SUBS, LANES))
            first_speed = jnp.take_along_axis(table, first_wide, axis=1)[:1]
            second_speed = None
            for t in range(5):
                table = jnp.broadcast_to(tables[k][t], (SUBS, LANES))
                found = jnp.take_along_axis(table, place, axis=1)[:1]
                second_speed = found if t == 0 else jnp.where(level == t, found, second_speed)
            addend = (first_speed - second_speed) * pair_normal[k, 0, :, here]
            rate = addend if rate is None else rate + addend
        resist = LUB_COEF * (1.0 / jnp.maximum(gap, GAP_FLOOR) - 1.0 / GAP_CUTOFF)
        number = start + lane
        factor = jnp.where(number < pair_count[...], -resist * rate, 0.0)
        values = [factor * pair_normal[k, 0, :, here] for k in range(3)]
        first = first + 4 * slots
        for ref, these in ((first, values), (second, [-v for v in values])):
            left, right = hot_rows(ref // 16, ref % 16, these)
            lefts.append(left)
            for k in range(3):
                rights[k].append(right[k])
    left = jnp.concatenate(lefts, axis=1)
    for k in range(3):
        total = totals[k] + lax.dot_general(
            jnp.concatenate(rights[k], axis=1), left, NT, preferred_element_type=F32
        )
        first_of[16 * k : 16 * k + 16, 0:48] = total[:16] + total[16:]
    second_of[...] = first_of[...].T
    for k in range(3):
        line = None
        for s in range(4):
            piece = second_of[pl.ds(s, NEAR, stride=4), :]
            shift = 16 * (s - k) % LANES
            if shift:
                piece = pltpu.roll(piece, shift, axis=1)
            line = piece if line is None else jnp.where(lane >= 16 * s, piece, line)
        for g in range(3):
            row = SUBS * g + k
            low, own, high = [line[3 * f + g : 3 * f + g + 1] for f in range(3)]
            to_near[row : row + 1, :] = jnp.where(even_flow, high, low)
            to_self[row : row + 1, :] = own
            to_far[row : row + 1, :] = jnp.where(even_flow, low, high)


def stream_kernel(relaxed, bounced, from_near, from_far, from_pair, from_cross, out):
    from_left, from_right = sort_sides("flow", from_near, from_far)
    low_rows, high_rows = sort_sides("grad", from_pair, from_cross)
    width_x, width_y = relaxed.shape[1], relaxed.shape[2]
    for direction, (cx, cy, cz) in enumerate(VELOCITIES):
        for x in range(width_x):
            source = x - cx
            if source < 0:
                tile = from_left[RIGHTWARD.index(direction)]
            elif source >= width_x:
                tile = from_right[LEFTWARD.index(direction)]
            else:
                tile = relaxed[direction, source]
            if cy != 0:
                tile = pltpu.roll(tile, cy % width_y, axis=0)
                row = lax.broadcasted_iota(jnp.int32, tile.shape, 0)
                if cy > 0:
                    ghost = low_rows[UPWARD.index(direction)][x : x + 1, :]
                    tile = jnp.where(row == 0, jnp.broadcast_to(ghost, tile.shape), tile)
                else:
                    ghost = high_rows[DOWNWARD.index(direction)][x : x + 1, :]
                    tile = jnp.where(row == width_y - 1, jnp.broadcast_to(ghost, tile.shape), tile)
            if cz != 0:
                tile = pltpu.roll(tile, cz % LANES, axis=1)
            if direction > 0:
                opposite = direction + 1 if direction % 2 == 1 else direction - 1
                back = bounced[opposite - 1, x]
                tile = jnp.where(back < 0.5 * NO_LINK, back, tile)
            out[direction, x] = tile


def finish_kernel(own, one, other, speed, force, moved):
    slots = force.shape[3]
    total = own[...] + one[...] + other[...]
    for k in range(3):
        line = total[k : k + 1, :slots]
        force[k, 0] = line
        moved[k, 0] = speed[k : k + 1, :slots] + INV_MASS * line


def swap(block, axis, far):
    count = lax.axis_size(axis)
    assert count % 2 == 0
    route = []
    for i in range(count):
        up = (i % 2 == 0) != far
        route.append((i, (i + (1 if up else -1)) % count))
    return lax.ppermute(block, axis, route)


def shape_of(*dims):
    return jax.ShapeDtypeStruct(dims, F32)


def local_of(*dims):
    return pltpu.VMEM(dims, F32)


def local(*arrays):
    return [pltpu.with_memory_space_constraint(array, pltpu.VMEM) for array in arrays]


def mark_links(first, steps, half_rows, count, link_arrays, *before):
    links = link_arrays[0].shape[2]
    width = links // 2
    link_spec = pl.BlockSpec((1, 1, width), lambda i: (0, 0, i + first))
    whole = pl.BlockSpec((half_rows, 2 * LANES), lambda i: (0, 0))
    one = pl.BlockSpec((1, 1), lambda i: (0, 0))
    return pl.pallas_call(
        functools.partial(mark_kernel, first),
        name="mark",
        grid=(steps,),
        in_specs=[one, link_spec, link_spec, link_spec] + [whole] * len(before),
        out_specs=whole,
        out_shape=local_of(half_rows, 2 * LANES),
    )(count, *link_arrays, *local(*before))


def one_step(
    populations,
    le_offset,
    sphere_velocity,
    link_cell,
    link_dir,
    link_sphere,
    link_count,
    pair_first,
    pair_second,
    pair_count,
    pair_gap,
    pair_normal,
):
    width_x, width_y, depth = populations.shape[1:]
    slots = sphere_velocity.shape[3]
    flow_count = lax.axis_size("flow")
    grad_count = lax.axis_size("grad")
    assert depth == LANES and width_y == SUBS and width_x == SUBS and 2 * slots == LANES
    assert grad_count % 2 == 0

    relaxed, density, right_msg, left_msg, near_msg, far_msg, own_line = pl.pallas_call(
        collide_kernel,
        name="collide",
        in_specs=[VMEM, VMEM],
        out_specs=[VMEM] * 7,
        out_shape=[
            local_of(19, width_x, width_y, depth),
            local_of(width_x, width_y, depth),
            local_of(11, SUBS, LANES),
            local_of(11, SUBS, LANES),
            local_of(11, SUBS, LANES),
            local_of(11, SUBS, LANES),
            local_of(3, LANES),
        ],
    )(populations, sphere_velocity)

    from_far = swap(far_msg, "flow", True)
    from_near = swap(near_msg, "flow", False)

    half_rows = 9 * width_x * width_y
    link_arrays = [link_cell, link_dir, link_sphere]
    marks = mark_links(0, 1, half_rows, link_count, link_arrays)

    msg_pair, msg_cross, own_speed = pl.pallas_call(
        prepare_kernel,
        name="prepare",
        in_specs=[VMEM] * 5,
        out_specs=[VMEM] * 3,
        out_shape=[
            local_of(7, SUBS, LANES),
            local_of(7, SUBS, LANES),
            local_of(2, SUBS, LANES),
        ],
        scratch_shapes=[pltpu.VMEM((10, 3 * SUBS, LANES), F32)],
    )(le_offset.reshape(1, 1), *local(right_msg, left_msg, from_near, from_far))

    def exchange(hops, msg_pair, msg_cross, own_speed, marks, link_count, *link_arrays):
        top = grad_count - 1
        pairs, cross, wrap = [], [], []
        for a in range(flow_count):
            line = a * grad_count
            for b in range(grad_count):
                pairs.append((line + b, line + (b ^ 1)))
                if 0 < b < top:
                    cross.append((line + b, line + b + (1 if b % 2 else -1)))
            cross.append(((a + hops) % flow_count * grad_count + top, line))
            cross.append(((a - hops) % flow_count * grad_count, line + top))
            wrap += [(line, line + top), (line + top, line)]
        axes = ("flow", "grad")
        from_pair = lax.ppermute(msg_pair, axes, pairs)
        from_wrap = lax.ppermute(own_speed, axes, wrap)
        from_cross = lax.ppermute(msg_cross, axes, cross)
        marks = mark_links(1, 1, half_rows, link_count, link_arrays, marks)
        return from_pair, from_cross, from_wrap, marks

    from_pair, from_cross, from_wrap, marks = lax.switch(
        lax.div(le_offset[0], width_x),
        [functools.partial(exchange, hops) for hops in range(flow_count)],
        msg_pair,
        msg_cross,
        own_speed,
        marks,
        link_count,
        *link_arrays,
    )

    bounced, to_near, to_self, to_far = pl.pallas_call(
        force_kernel,
        name="force",
        in_specs=[VMEM] * 12,
        out_specs=[VMEM] * 4,
        out_shape=[local_of(18, width_x, width_y, depth)] + [local_of(3 * SUBS, LANES)] * 3,
        scratch_shapes=[
            pltpu.VMEM((18, SUBS, LANES), F32),
            *[pltpu.VMEM((2 * width_x * SUBS, LANES), F32)] * 8,
            pltpu.VMEM((18, 32, 48), F32),
        ],
    )(
        pair_count,
        *local(relaxed, density, marks, own_speed, from_pair, from_cross, from_wrap),
        pair_first,
        pair_second,
        pair_gap,
        pair_normal,
    )

    updated = pl.pallas_call(
        stream_kernel,
        name="stream",
        in_specs=[VMEM] * 6,
        out_specs=VMEM,
        out_shape=shape_of(19, width_x, width_y, depth),
    )(*local(relaxed, bounced, from_near, from_far, from_pair, from_cross))

    column = to_self + swap(to_far, "flow", True) + swap(to_near, "flow", False)
    even = lax.axis_index("grad") % 2 == 0
    low, high = column[:SUBS], column[2 * SUBS :]
    from_cross_force = swap(jnp.where(even, low, high), "grad", True)
    from_pair_force = swap(jnp.where(even, high, low), "grad", False)
    line = shape_of(3, 1, 1, slots)
    sphere_force, velocity_next = pl.pallas_call(
        finish_kernel,
        name="finish",
        in_specs=[VMEM] * 4,
        out_specs=[VMEM] * 2,
        out_shape=[line, line],
    )(*local(column[SUBS : 2 * SUBS], from_pair_force, from_cross_force, own_line))

    return updated, sphere_force, velocity_next


def solution(mesh):
    in_specs = (
        P(None, "flow", "grad", None),
        P(),
        P(None, "flow", "grad", None),
        P("flow", "grad", None),
        P("flow", "grad", None),
        P("flow", "grad", None),
        P("flow", "grad"),
        P("flow", "grad", None),
        P("flow", "grad", None),
        P("flow", "grad"),
        P("flow", "grad", None),
        P(None, "flow", "grad", None),
    )
    out_specs = (
        P(None, "flow", "grad", None),
        P(None, "flow", "grad", None),
        P(None, "flow", "grad", None),
    )
    return jax.shard_map(
        one_step, mesh=mesh, in_specs=in_specs, out_specs=out_specs, check_vma=False
    )
```

```python
import functools

import jax
import jax.numpy as jnp
from jax import lax
from jax.experimental import pallas as pl
from jax.experimental.pallas import tpu as pltpu
from jax.sharding import PartitionSpec as P


VELOCITIES = [
    (0, 0, 0),
    (1, 0, 0),
    (-1, 0, 0),
    (0, 1, 0),
    (0, -1, 0),
    (0, 0, 1),
    (0, 0, -1),
    (1, 1, 0),
    (-1, -1, 0),
    (1, -1, 0),
    (-1, 1, 0),
    (1, 0, 1),
    (-1, 0, -1),
    (1, 0, -1),
    (-1, 0, 1),
    (0, 1, 1),
    (0, -1, -1),
    (0, 1, -1),
    (0, -1, 1),
]
WEIGHTS = [1.0 / 3.0] + [1.0 / 18.0] * 6 + [1.0 / 36.0] * 12
UPWARD = [3, 7, 10, 15, 17]
DOWNWARD = [4, 8, 9, 16, 18]
RIGHTWARD = [1, 7, 9, 11, 13]
LEFTWARD = [2, 8, 10, 12, 14]
RELAX_TIME = 0.8
SHEAR_SPEED = 0.1
LUB_COEF = 0.5
GAP_FLOOR = 0.1
GAP_CUTOFF = 1.0
INV_MASS = 1.0 / 523.6
LANES = 128
SUBS = 8
NEAR = 9
NO_LINK = 1e30
BF16 = jnp.bfloat16
F32 = jnp.float32
NT = (((1,), (1,)), ((), ()))

VMEM = pl.BlockSpec(memory_space=pltpu.VMEM)


def collide_kernel(
    pops, speed, relaxed, density, right_msg, left_msg, near_msg, far_msg, own_line
):
    width_x, width_y = pops.shape[1], pops.shape[2]
    slots = speed.shape[3]
    for x in range(width_x):
        current = [pops[d, x] for d in range(19)]
        total = functools.reduce(lambda p, q: p + q, current)
        density[x] = total
        inverse = 1.0 / total
        speeds = []
        for axis_id in range(3):
            running = None
            for direction, vector in enumerate(VELOCITIES):
                if vector[axis_id] == 0:
                    continue
                if running is None:
                    running = current[direction]
                elif vector[axis_id] > 0:
                    running = running + current[direction]
                else:
                    running = running - current[direction]
            speeds.append(running * inverse)
        base = 1.0 - 1.5 * (
            speeds[0] * speeds[0] + speeds[1] * speeds[1] + speeds[2] * speeds[2]
        )
        for direction, vector in enumerate(VELOCITIES):
            c_dot = None
            for axis_id in range(3):
                if vector[axis_id] != 0:
                    addend = vector[axis_id] * speeds[axis_id]
                    c_dot = addend if c_dot is None else c_dot + addend
            shape = base if c_dot is None else base + c_dot * (3.0 + 4.5 * c_dot)
            equil = WEIGHTS[direction] * total * shape
            value = current[direction] - (current[direction] - equil) * (1.0 / RELAX_TIME)
            relaxed[direction, x] = value
            if x == width_x - 1 and direction in RIGHTWARD:
                right_msg[RIGHTWARD.index(direction)] = value
            if x == 0 and direction in LEFTWARD:
                left_msg[LEFTWARD.index(direction)] = value
            if direction in UPWARD:
                left_msg[5 + UPWARD.index(direction), x : x + 1, :] = value[width_y - 1 :, :]
            if direction in DOWNWARD:
                right_msg[5 + DOWNWARD.index(direction), x : x + 1, :] = value[:1, :]
    right_msg[10] = jnp.zeros((SUBS, LANES), F32)
    left_msg[10] = jnp.zeros((SUBS, LANES), F32)
    for k in range(3):
        row = speed[k, 0]
        twice = jnp.concatenate([row] * (LANES // slots), axis=1)
        right_msg[10, k : k + 1, :] = twice
        left_msg[10, k : k + 1, :] = twice
        own_line[k : k + 1, :] = twice
    even = lax.rem(lax.axis_index("flow"), 2) == 0
    for i in range(11):
        near_msg[i] = jnp.where(even, right_msg[i], left_msg[i])
        far_msg[i] = jnp.where(even, left_msg[i], right_msg[i])


def sort_sides(axis, near, far):
    even = lax.rem(lax.axis_index(axis), 2) == 0
    near = [near[i] for i in range(near.shape[0])]
    far = [far[i] for i in range(far.shape[0])]
    lower = [jnp.where(even, q, p) for p, q in zip(near, far)]
    higher = [jnp.where(even, p, q) for p, q in zip(near, far)]
    return lower, higher


def prepare_kernel(
    offset, own_right, own_left, from_near, from_far, msg_pair, msg_cross, own_speed, rows
):
    width_x = own_right.shape[1]
    from_left, from_right = sort_sides("flow", from_near, from_far)
    grad_index = lax.axis_index("grad")
    at_top = grad_index == lax.axis_size("grad") - 1
    at_bottom = grad_index == 0
    even = lax.rem(grad_index, 2) == 0
    rest = jnp.broadcast_to(lax.rem(offset[...], width_x), (width_x, LANES))
    up_rest = jnp.where(at_top, rest, 0)
    down_rest = jnp.where(at_bottom, rest, 0)
    top_boost = jnp.where(at_top, 1.0, 0.0)
    bottom_boost = jnp.where(at_bottom, 1.0, 0.0)

    def window(j, start, sign, amount):
        moved = rows[j, start : start + width_x, :]
        for r in range(1, width_x):
            first = start + sign * r
            moved = jnp.where(amount == r, rows[j, first : first + width_x, :], moved)
        return moved

    ups = []
    for j, direction in enumerate(UPWARD):
        step = VELOCITIES[direction][0]
        boost = 6.0 * WEIGHTS[direction] * step * SHEAR_SPEED
        rows[j, SUBS : 2 * SUBS] = own_left[5 + j]
        rows[j, 2 * SUBS : 3 * SUBS] = from_right[5 + j]
        if step > 0:
            slab = from_left[RIGHTWARD.index(direction)]
            rows[j, SUBS - 1 : SUBS] = slab[SUBS - 1 :, :]
        moved = window(j, SUBS - step, 1, up_rest)
        if step != 0:
            moved = moved - boost * top_boost
        ups.append(moved)
    for j, direction in enumerate(DOWNWARD):
        step = VELOCITIES[direction][0]
        boost = 6.0 * WEIGHTS[direction] * step * SHEAR_SPEED
        rows[5 + j, :SUBS] = from_left[5 + j]
        rows[5 + j, SUBS : 2 * SUBS] = own_right[5 + j]
        if step < 0:
            slab = from_right[LEFTWARD.index(direction)]
            rows[5 + j, 2 * SUBS : 2 * SUBS + 1] = slab[:1, :]
        moved = window(5 + j, SUBS - step, -1, down_rest)
        if step != 0:
            moved = moved + boost * bottom_boost
        msg_pair[j] = jnp.where(even, ups[j], moved)
        msg_cross[j] = jnp.where(even, moved, ups[j])
    three = [from_left[10], own_right[10], from_right[10]]
    for out, first in ((msg_pair, 5), (msg_cross, 5), (own_speed, 0)):
        for f in range(3):
            for k in range(3):
                row = 3 * f + k
                out[first + row // SUBS, row % SUBS : row % SUBS + 1, :] = three[f][k : k + 1, :]


def to_bf16(value):
    return value.astype(F32).astype(BF16)


def mark_kernel(count, cell, direction, sphere, marks):
    step = pl.program_id(0)
    width = cell.shape[2]
    half_rows = marks.shape[0]
    q = cell[0]
    ref = sphere[0]
    row = (direction[0] - 1) * (2 * half_rows // 18) + q // LANES
    z = q % LANES
    half = (row >= half_rows).astype(jnp.int32)
    row = row - half * half_rows
    number = step * width + lax.broadcasted_iota(jnp.int32, (1, width), 1)
    level = ref // LANES
    scale = jnp.where(level == 0, 1.0, 0.0)
    for t in range(1, 5):
        scale = jnp.where(level == t, 2.0 ** (8 * t), scale)
    code = jnp.where(number < count[...], (LANES + ref % LANES).astype(F32) * scale, 0.0)
    block = half_rows // 3
    parts = []
    for first in range(0, half_rows, block):
        local = row - first
        local = to_bf16(jnp.where((local >= 0) & (local < block), local, 255))
        index = to_bf16(lax.broadcasted_iota(jnp.int32, (block, width), 0))
        parts.append(
            jnp.where(
                index == jnp.broadcast_to(local, (block, width)), jnp.ones((), BF16), jnp.zeros((), BF16)
            )
        )
    rows_hot = jnp.concatenate(parts, axis=0)
    column = to_bf16(z + LANES * half)
    index = to_bf16(lax.broadcasted_iota(jnp.int32, (2 * LANES, width), 0))
    columns = jnp.where(
        index == jnp.broadcast_to(column, (2 * LANES, width)),
        jnp.broadcast_to(code.astype(BF16), (2 * LANES, width)),
        jnp.zeros((), BF16),
    )
    part = lax.dot_general(rows_hot, columns, NT, preferred_element_type=F32)

    @pl.when(step == 0)
    def _():
        marks[...] = part

    @pl.when(step > 0)
    def _():
        marks[...] += part


def split(value):
    high = value.astype(BF16)
    return high, (value - high.astype(F32)).astype(BF16)


def force_kernel(
    pair_count,
    relaxed,
    density,
    marks,
    own_speed,
    from_pair,
    from_cross,
    from_wrap,
    pair_first,
    pair_second,
    pair_gap,
    pair_normal,
    bounced,
    to_near,
    to_self,
    to_far,
    link_table,
    *scratch,
):
    width_x = relaxed.shape[1]
    slots = LANES // 2
    even_buffers, odd_buffers, sums = scratch[:4], scratch[4:8], scratch[8]
    first_of, second_of = odd_buffers[:2]
    half_rows = marks.shape[0]
    lane = lax.broadcasted_iota(jnp.int32, (1, LANES), 1)
    grad_index = lax.axis_index("grad")
    even = lax.rem(grad_index, 2) == 0
    even_flow = lax.rem(lax.axis_index("flow"), 2) == 0
    at_edge = (grad_index == 0) | (grad_index == lax.axis_size("grad") - 1)
    sources = [[], [], []]
    for tile in range(2):
        near = from_pair[5 + tile]
        far = jnp.where(at_edge, from_wrap[tile], from_cross[5 + tile])
        sources[0].append(jnp.where(even, far, near))
        sources[1].append(own_speed[tile])
        sources[2].append(jnp.where(even, near, far))

    def speed_row(code, k):
        row = 3 * (code // 3) + k
        return sources[code % 3][row // SUBS][row % SUBS : row % SUBS + 1, :]

    tables = []
    for k in range(3):
        rows = []
        for t in range(5):
            low = speed_row(2 * t, k)
            high = speed_row(min(2 * t + 1, NEAR - 1), k)
            rows.append(jnp.where(lane < slots, low, high))
        tables.append(rows)
    for direction in range(1, 19):
        for t in range(5):
            total = None
            for k in range(3):
                if VELOCITIES[direction][k] != 0:
                    addend = VELOCITIES[direction][k] * tables[k][t]
                    total = addend if total is None else total + addend
            link_table[direction - 1, t : t + 1, :] = total

    index_a = to_bf16(lax.broadcasted_iota(jnp.int32, (48, LANES), 0))
    index_b = to_bf16(lax.broadcasted_iota(jnp.int32, (16, LANES), 0))
    one = jnp.ones((), BF16)
    zero = jnp.zeros((), BF16)

    def spread(ref, r):
        row = ref[pl.ds(r, SUBS, stride=0), :]
        return jnp.concatenate([row, row], axis=0).astype(BF16)

    def slot_rows(buffers, r):
        first_of, second_of, value_of, rest_of = buffers
        a = spread(first_of, r)
        b = spread(second_of, r)
        high = spread(value_of, r)
        low = spread(rest_of, r)
        left = [jnp.where(index_a[16 * i : 16 * i + 16] == a, one, zero) for i in range(3)]
        mask = index_b == b
        right = [jnp.where(mask, high, zero), jnp.where(mask, low, zero)]
        return jnp.concatenate(left, axis=0), jnp.concatenate(right, axis=0)

    def hot_rows(first_row, second_row, values):
        a = jnp.broadcast_to(to_bf16(first_row), (48, LANES))
        b = jnp.broadcast_to(to_bf16(second_row), (16, LANES))
        left = jnp.where(index_a == a, one, zero)
        mask = index_b == b
        right = []
        for value in values:
            high, low = split(value)
            right.append(
                jnp.concatenate(
                    [
                        jnp.where(mask, jnp.broadcast_to(high, (16, LANES)), zero),
                        jnp.where(mask, jnp.broadcast_to(low, (16, LANES)), zero),
                    ],
                    axis=0,
                )
            )
        return left, right

    def look_up(g, buffers):
        first_of, second_of, value_of, rest_of = buffers
        for side in range(2):
            index = 2 * g + side
            half = index // 9
            first_row = (index - 9 * half) * (2 * half_rows // 18)
            weight6 = jnp.where(index < 6, 6.0 * WEIGHTS[1], 6.0 * WEIGHTS[7]).astype(F32)
            lookup = [
                jnp.broadcast_to(link_table[index, t : t + 1, :], (SUBS, LANES)) for t in range(5)
            ]
            for x in range(width_x):
                mark = marks[
                    pl.ds(pl.multiple_of(first_row + SUBS * x, SUBS), SUBS),
                    pl.ds(pl.multiple_of(half * LANES, LANES), LANES),
                ]
                live = mark > 0.0
                scale = jnp.ones((SUBS, LANES), F32)
                first = jnp.zeros((SUBS, LANES), F32)
                levels = [mark > 2.0 ** (8 * t + 6) for t in range(1, 5)]
                for t, above in enumerate(levels, 1):
                    scale = jnp.where(above, 2.0 ** (-8 * t), scale)
                    first = jnp.where(above, 8.0 * t, first)
                place = (mark * scale).astype(jnp.int32) & (LANES - 1)
                speed = jnp.take_along_axis(lookup[0], place, axis=1)
                for t, above in enumerate(levels, 1):
                    found = jnp.take_along_axis(lookup[t], place, axis=1)
                    speed = jnp.where(above, found, speed)
                leaving = relaxed[index + 1, x]
                back = leaving - weight6 * density[x] * speed
                bounced[index, x] = jnp.where(live, back, NO_LINK)
                force = leaving + back
                first = first + (place >> 4).astype(F32)
                second = (place & 15).astype(F32)
                where = side * width_x * SUBS + SUBS * x
                first_of[where : where + SUBS] = first
                second_of[where : where + SUBS] = second
                force = jnp.where(live, force, 0.0)
                high = force.astype(BF16).astype(F32)
                value_of[where : where + SUBS] = high
                rest_of[where : where + SUBS] = force - high

    def add_up(g, buffers):
        for part in range(2):
            lefts, rights = [], []
            for r in range(part * 2 * width_x * SUBS // 2, (part + 1) * 2 * width_x * SUBS // 2):
                left, right = slot_rows(buffers, r)
                lefts.append(left)
                rights.append(right)
            sums[2 * g + part] = lax.dot_general(
                jnp.concatenate(rights, axis=1),
                jnp.concatenate(lefts, axis=1),
                NT,
                preferred_element_type=F32,
            )

    look_up(0, even_buffers)

    def two_groups(i, carry):
        look_up(2 * i + 1, odd_buffers)
        add_up(2 * i, even_buffers)
        look_up(2 * i + 2, even_buffers)
        add_up(2 * i + 1, odd_buffers)
        return carry

    lax.fori_loop(0, 4, two_groups, 0)
    add_up(8, even_buffers)

    for out in (to_near, to_self, to_far):
        out[...] = jnp.zeros(out.shape, F32)
    totals = []
    for k in range(3):
        total = None
        for direction in range(1, 19):
            c = VELOCITIES[direction][k]
            if c == 0:
                continue
            addend = sums[direction - 1]
            if total is None:
                total = addend if c > 0 else -addend
            else:
                total = total + addend if c > 0 else total - addend
        totals.append(total)

    pairs = pair_first.shape[2]
    lefts = []
    rights = [[], [], []]
    for start in range(0, pairs, LANES):
        here = slice(start, start + LANES)
        first = pair_first[0, :, here]
        second = pair_second[0, :, here]
        first_wide = jnp.broadcast_to(first, (SUBS, LANES))
        place = jnp.broadcast_to(second % LANES, (SUBS, LANES))
        level = second // LANES
        gap = pair_gap[0, :, here]
        rate = None
        for k in range(3):
            table = jnp.broadcast_to(tables[k][2], (SUBS, LANES))
            first_speed = jnp.take_along_axis(table, first_wide, axis=1)[:1]
            second_speed = None
            for t in range(5):
                table = jnp.broadcast_to(tables[k][t], (SUBS, LANES))
                found = jnp.take_along_axis(table, place, axis=1)[:1]
                second_speed = found if t == 0 else jnp.where(level == t, found, second_speed)
            addend = (first_speed - second_speed) * pair_normal[k, 0, :, here]
            rate = addend if rate is None else rate + addend
        resist = LUB_COEF * (1.0 / jnp.maximum(gap, GAP_FLOOR) - 1.0 / GAP_CUTOFF)
        number = start + lane
        factor = jnp.where(number < pair_count[...], -resist * rate, 0.0)
        values = [factor * pair_normal[k, 0, :, here] for k in range(3)]
        first = first + 4 * slots
        for ref, these in ((first, values), (second, [-v for v in values])):
            left, right = hot_rows(ref // 16, ref % 16, these)
            lefts.append(left)
            for k in range(3):
                rights[k].append(right[k])
    left = jnp.concatenate(lefts, axis=1)
    for k in range(3):
        total = totals[k] + lax.dot_general(
            jnp.concatenate(rights[k], axis=1), left, NT, preferred_element_type=F32
        )
        first_of[16 * k : 16 * k + 16, 0:48] = total[:16] + total[16:]
    second_of[...] = first_of[...].T
    for k in range(3):
        line = None
        for s in range(4):
            piece = second_of[pl.ds(s, NEAR, stride=4), :]
            shift = 16 * (s - k) % LANES
            if shift:
                piece = pltpu.roll(piece, shift, axis=1)
            line = piece if line is None else jnp.where(lane >= 16 * s, piece, line)
        for g in range(3):
            row = SUBS * g + k
            low, own, high = [line[3 * f + g : 3 * f + g + 1] for f in range(3)]
            to_near[row : row + 1, :] = jnp.where(even_flow, high, low)
            to_self[row : row + 1, :] = own
            to_far[row : row + 1, :] = jnp.where(even_flow, low, high)


def stream_kernel(relaxed, bounced, from_near, from_far, from_pair, from_cross, out):
    from_left, from_right = sort_sides("flow", from_near, from_far)
    low_rows, high_rows = sort_sides("grad", from_pair, from_cross)
    width_x, width_y = relaxed.shape[1], relaxed.shape[2]
    for direction, (cx, cy, cz) in enumerate(VELOCITIES):
        for x in range(width_x):
            source = x - cx
            if source < 0:
                tile = from_left[RIGHTWARD.index(direction)]
            elif source >= width_x:
                tile = from_right[LEFTWARD.index(direction)]
            else:
                tile = relaxed[direction, source]
            if cy != 0:
                tile = pltpu.roll(tile, cy % width_y, axis=0)
                row = lax.broadcasted_iota(jnp.int32, tile.shape, 0)
                if cy > 0:
                    ghost = low_rows[UPWARD.index(direction)][x : x + 1, :]
                    tile = jnp.where(row == 0, jnp.broadcast_to(ghost, tile.shape), tile)
                else:
                    ghost = high_rows[DOWNWARD.index(direction)][x : x + 1, :]
                    tile = jnp.where(row == width_y - 1, jnp.broadcast_to(ghost, tile.shape), tile)
            if cz != 0:
                tile = pltpu.roll(tile, cz % LANES, axis=1)
            if direction > 0:
                opposite = direction + 1 if direction % 2 == 1 else direction - 1
                back = bounced[opposite - 1, x]
                tile = jnp.where(back < 0.5 * NO_LINK, back, tile)
            out[direction, x] = tile


def finish_kernel(own, one, other, speed, force, moved):
    slots = force.shape[3]
    total = own[...] + one[...] + other[...]
    for k in range(3):
        line = total[k : k + 1, :slots]
        force[k, 0] = line
        moved[k, 0] = speed[k : k + 1, :slots] + INV_MASS * line


def swap(block, axis, far):
    count = lax.axis_size(axis)
    assert count % 2 == 0
    route = []
    for i in range(count):
        up = (i % 2 == 0) != far
        route.append((i, (i + (1 if up else -1)) % count))
    return lax.ppermute(block, axis, route)


def shape_of(*dims):
    return jax.ShapeDtypeStruct(dims, F32)


def local_of(*dims):
    return pltpu.VMEM(dims, F32)


def local(*arrays):
    return [pltpu.with_memory_space_constraint(array, pltpu.VMEM) for array in arrays]


def mark_links(half_rows, count, link_arrays):
    links = link_arrays[0].shape[2]
    width = links // 2
    link_spec = pl.BlockSpec((1, 1, width), lambda i: (0, 0, i))
    return pl.pallas_call(
        mark_kernel,
        name="mark",
        grid=(links // width,),
        in_specs=[pl.BlockSpec((1, 1), lambda i: (0, 0)), link_spec, link_spec, link_spec],
        out_specs=pl.BlockSpec((half_rows, 2 * LANES), lambda i: (0, 0)),
        out_shape=local_of(half_rows, 2 * LANES),
    )(count, *link_arrays)


def one_step(
    populations,
    le_offset,
    sphere_velocity,
    link_cell,
    link_dir,
    link_sphere,
    link_count,
    pair_first,
    pair_second,
    pair_count,
    pair_gap,
    pair_normal,
):
    width_x, width_y, depth = populations.shape[1:]
    slots = sphere_velocity.shape[3]
    flow_count = lax.axis_size("flow")
    grad_count = lax.axis_size("grad")
    assert depth == LANES and width_y == SUBS and width_x == SUBS and 2 * slots == LANES
    assert grad_count % 2 == 0

    relaxed, density, right_msg, left_msg, near_msg, far_msg, own_line = pl.pallas_call(
        collide_kernel,
        name="collide",
        in_specs=[VMEM, VMEM],
        out_specs=[VMEM] * 7,
        out_shape=[
            local_of(19, width_x, width_y, depth),
            local_of(width_x, width_y, depth),
            local_of(11, SUBS, LANES),
            local_of(11, SUBS, LANES),
            local_of(11, SUBS, LANES),
            local_of(11, SUBS, LANES),
            local_of(3, LANES),
        ],
    )(populations, sphere_velocity)

    from_far = swap(far_msg, "flow", True)
    from_near = swap(near_msg, "flow", False)

    half_rows = 9 * width_x * width_y
    link_arrays = [link_cell, link_dir, link_sphere]
    msg_pair, msg_cross, own_speed = pl.pallas_call(
        prepare_kernel,
        name="prepare",
        in_specs=[VMEM] * 5,
        out_specs=[VMEM] * 3,
        out_shape=[
            local_of(7, SUBS, LANES),
            local_of(7, SUBS, LANES),
            local_of(2, SUBS, LANES),
        ],
        scratch_shapes=[pltpu.VMEM((10, 3 * SUBS, LANES), F32)],
    )(le_offset.reshape(1, 1), *local(right_msg, left_msg, from_near, from_far))

    def exchange(hops, msg_pair, msg_cross, own_speed, link_count, *link_arrays):
        top = grad_count - 1
        pairs, cross, wrap = [], [], []
        for a in range(flow_count):
            line = a * grad_count
            for b in range(grad_count):
                pairs.append((line + b, line + (b ^ 1)))
                if 0 < b < top:
                    cross.append((line + b, line + b + (1 if b % 2 else -1)))
            cross.append(((a + hops) % flow_count * grad_count + top, line))
            cross.append(((a - hops) % flow_count * grad_count, line + top))
            wrap += [(line, line + top), (line + top, line)]
        axes = ("flow", "grad")
        from_pair = lax.ppermute(msg_pair, axes, pairs)
        from_wrap = lax.ppermute(own_speed, axes, wrap)
        from_cross = lax.ppermute(msg_cross, axes, cross)
        marks = mark_links(half_rows, link_count, link_arrays)
        return from_pair, from_cross, from_wrap, marks

    from_pair, from_cross, from_wrap, marks = lax.switch(
        lax.div(le_offset[0], width_x),
        [functools.partial(exchange, hops) for hops in range(flow_count)],
        msg_pair,
        msg_cross,
        own_speed,
        link_count,
        *link_arrays,
    )

    bounced, to_near, to_self, to_far = pl.pallas_call(
        force_kernel,
        name="force",
        in_specs=[VMEM] * 12,
        out_specs=[VMEM] * 4,
        out_shape=[local_of(18, width_x, width_y, depth)] + [local_of(3 * SUBS, LANES)] * 3,
        scratch_shapes=[
            pltpu.VMEM((18, SUBS, LANES), F32),
            *[pltpu.VMEM((2 * width_x * SUBS, LANES), F32)] * 8,
            pltpu.VMEM((18, 32, 48), F32),
        ],
    )(
        pair_count,
        *local(relaxed, density, marks, own_speed, from_pair, from_cross, from_wrap),
        pair_first,
        pair_second,
        pair_gap,
        pair_normal,
    )

    updated = pl.pallas_call(
        stream_kernel,
        name="stream",
        in_specs=[VMEM] * 6,
        out_specs=VMEM,
        out_shape=shape_of(19, width_x, width_y, depth),
    )(*local(relaxed, bounced, from_near, from_far, from_pair, from_cross))

    column = to_self + swap(to_far, "flow", True) + swap(to_near, "flow", False)
    even = lax.axis_index("grad") % 2 == 0
    low, high = column[:SUBS], column[2 * SUBS :]
    from_cross_force = swap(jnp.where(even, low, high), "grad", True)
    from_pair_force = swap(jnp.where(even, high, low), "grad", False)
    line = shape_of(3, 1, 1, slots)
    sphere_force, velocity_next = pl.pallas_call(
        finish_kernel,
        name="finish",
        in_specs=[VMEM] * 4,
        out_specs=[VMEM] * 2,
        out_shape=[line, line],
    )(*local(column[SUBS : 2 * SUBS], from_pair_force, from_cross_force, own_line))

    return updated, sphere_force, velocity_next


def solution(mesh):
    in_specs = (
        P(None, "flow", "grad", None),
        P(),
        P(None, "flow", "grad", None),
        P("flow", "grad", None),
        P("flow", "grad", None),
        P("flow", "grad", None),
        P("flow", "grad"),
        P("flow", "grad", None),
        P("flow", "grad", None),
        P("flow", "grad"),
        P("flow", "grad", None),
        P(None, "flow", "grad", None),
    )
    out_specs = (
        P(None, "flow", "grad", None),
        P(None, "flow", "grad", None),
        P(None, "flow", "grad", None),
    )
    return jax.shard_map(
        one_step, mesh=mesh, in_specs=in_specs, out_specs=out_specs, check_vma=False
    )
```

```python
import functools

import jax
import jax.numpy as jnp
from jax import lax
from jax.experimental import pallas as pl
from jax.experimental.pallas import tpu as pltpu
from jax.sharding import PartitionSpec as P


VELOCITIES = [
    (0, 0, 0),
    (1, 0, 0),
    (-1, 0, 0),
    (0, 1, 0),
    (0, -1, 0),
    (0, 0, 1),
    (0, 0, -1),
    (1, 1, 0),
    (-1, -1, 0),
    (1, -1, 0),
    (-1, 1, 0),
    (1, 0, 1),
    (-1, 0, -1),
    (1, 0, -1),
    (-1, 0, 1),
    (0, 1, 1),
    (0, -1, -1),
    (0, 1, -1),
    (0, -1, 1),
]
WEIGHTS = [1.0 / 3.0] + [1.0 / 18.0] * 6 + [1.0 / 36.0] * 12
UPWARD = [3, 7, 10, 15, 17]
DOWNWARD = [4, 8, 9, 16, 18]
RIGHTWARD = [1, 7, 9, 11, 13]
LEFTWARD = [2, 8, 10, 12, 14]
RELAX_TIME = 0.8
SHEAR_SPEED = 0.1
LUB_COEF = 0.5
GAP_FLOOR = 0.1
GAP_CUTOFF = 1.0
INV_MASS = 1.0 / 523.6
LANES = 128
SUBS = 8
NEAR = 9
NO_LINK = 1e30
BF16 = jnp.bfloat16
F32 = jnp.float32
NT = (((1,), (1,)), ((), ()))

VMEM = pl.BlockSpec(memory_space=pltpu.VMEM)


def collide_kernel(
    pops, speed, relaxed, density, right_msg, left_msg, near_msg, far_msg, own_line
):
    width_x, width_y = pops.shape[1], pops.shape[2]
    slots = speed.shape[3]
    for x in range(width_x):
        current = [pops[d, x] for d in range(19)]
        total = functools.reduce(lambda p, q: p + q, current)
        density[x] = total
        inverse = 1.0 / total
        speeds = []
        for axis_id in range(3):
            running = None
            for direction, vector in enumerate(VELOCITIES):
                if vector[axis_id] == 0:
                    continue
                if running is None:
                    running = current[direction]
                elif vector[axis_id] > 0:
                    running = running + current[direction]
                else:
                    running = running - current[direction]
            speeds.append(running * inverse)
        base = 1.0 - 1.5 * (
            speeds[0] * speeds[0] + speeds[1] * speeds[1] + speeds[2] * speeds[2]
        )
        for direction, vector in enumerate(VELOCITIES):
            c_dot = None
            for axis_id in range(3):
                if vector[axis_id] != 0:
                    addend = vector[axis_id] * speeds[axis_id]
                    c_dot = addend if c_dot is None else c_dot + addend
            shape = base if c_dot is None else base + c_dot * (3.0 + 4.5 * c_dot)
            equil = WEIGHTS[direction] * total * shape
            value = current[direction] - (current[direction] - equil) * (1.0 / RELAX_TIME)
            relaxed[direction, x] = value
            if x == width_x - 1 and direction in RIGHTWARD:
                right_msg[RIGHTWARD.index(direction)] = value
            if x == 0 and direction in LEFTWARD:
                left_msg[LEFTWARD.index(direction)] = value
            if direction in UPWARD:
                left_msg[5 + UPWARD.index(direction), x : x + 1, :] = value[width_y - 1 :, :]
            if direction in DOWNWARD:
                right_msg[5 + DOWNWARD.index(direction), x : x + 1, :] = value[:1, :]
    right_msg[10] = jnp.zeros((SUBS, LANES), F32)
    left_msg[10] = jnp.zeros((SUBS, LANES), F32)
    for k in range(3):
        row = speed[k, 0]
        twice = jnp.concatenate([row] * (LANES // slots), axis=1)
        right_msg[10, k : k + 1, :] = twice
        left_msg[10, k : k + 1, :] = twice
        own_line[k : k + 1, :] = twice
    even = lax.rem(lax.axis_index("flow"), 2) == 0
    for i in range(11):
        near_msg[i] = jnp.where(even, right_msg[i], left_msg[i])
        far_msg[i] = jnp.where(even, left_msg[i], right_msg[i])


def sort_sides(axis, near, far):
    even = lax.rem(lax.axis_index(axis), 2) == 0
    count = len(far) if isinstance(far, list) else far.shape[0]
    near = [near[i] for i in range(count)]
    far = [far[i] for i in range(count)]
    lower = [jnp.where(even, q, p) for p, q in zip(near, far)]
    higher = [jnp.where(even, p, q) for p, q in zip(near, far)]
    return lower, higher


def prepare_kernel(
    offset, own_right, own_left, from_near, from_far, msg_pair, msg_cross, own_speed, rows
):
    width_x = own_right.shape[1]
    from_left, from_right = sort_sides("flow", from_near, from_far)
    grad_index = lax.axis_index("grad")
    at_top = grad_index == lax.axis_size("grad") - 1
    at_bottom = grad_index == 0
    even = lax.rem(grad_index, 2) == 0
    rest = jnp.broadcast_to(lax.rem(offset[...], width_x), (width_x, LANES))
    up_rest = jnp.where(at_top, rest, 0)
    down_rest = jnp.where(at_bottom, rest, 0)
    top_boost = jnp.where(at_top, 1.0, 0.0)
    bottom_boost = jnp.where(at_bottom, 1.0, 0.0)

    def window(j, start, sign, amount):
        moved = rows[j, start : start + width_x, :]
        for r in range(1, width_x):
            first = start + sign * r
            moved = jnp.where(amount == r, rows[j, first : first + width_x, :], moved)
        return moved

    ups = []
    for j, direction in enumerate(UPWARD):
        step = VELOCITIES[direction][0]
        boost = 6.0 * WEIGHTS[direction] * step * SHEAR_SPEED
        rows[j, SUBS : 2 * SUBS] = own_left[5 + j]
        rows[j, 2 * SUBS : 3 * SUBS] = from_right[5 + j]
        if step > 0:
            slab = from_left[RIGHTWARD.index(direction)]
            rows[j, SUBS - 1 : SUBS] = slab[SUBS - 1 :, :]
        moved = window(j, SUBS - step, 1, up_rest)
        if step != 0:
            moved = moved - boost * top_boost
        ups.append(moved)
    for j, direction in enumerate(DOWNWARD):
        step = VELOCITIES[direction][0]
        boost = 6.0 * WEIGHTS[direction] * step * SHEAR_SPEED
        rows[5 + j, :SUBS] = from_left[5 + j]
        rows[5 + j, SUBS : 2 * SUBS] = own_right[5 + j]
        if step < 0:
            slab = from_right[LEFTWARD.index(direction)]
            rows[5 + j, 2 * SUBS : 2 * SUBS + 1] = slab[:1, :]
        moved = window(5 + j, SUBS - step, -1, down_rest)
        if step != 0:
            moved = moved + boost * bottom_boost
        msg_pair[j] = jnp.where(even, ups[j], moved)
        msg_cross[j] = jnp.where(even, moved, ups[j])
    three = [from_left[10], own_right[10], from_right[10]]
    for out, first in ((msg_pair, 5), (msg_cross, 5), (own_speed, 0)):
        for f in range(3):
            for k in range(3):
                row = 3 * f + k
                out[first + row // SUBS, row % SUBS : row % SUBS + 1, :] = three[f][k : k + 1, :]


def to_bf16(value):
    return value.astype(F32).astype(BF16)


def mark_kernel(first_step, count, cell, direction, sphere, *refs):
    marks = refs[-1]
    step = pl.program_id(0)
    width = cell.shape[2]
    half_rows = marks.shape[0]
    q = cell[0]
    ref = sphere[0]
    row = (direction[0] - 1) * (2 * half_rows // 18) + q // LANES
    z = q % LANES
    half = (row >= half_rows).astype(jnp.int32)
    row = row - half * half_rows
    number = (first_step + step) * width + lax.broadcasted_iota(jnp.int32, (1, width), 1)
    level = ref // LANES
    scale = jnp.where(level == 0, 1.0, 0.0)
    for t in range(1, 5):
        scale = jnp.where(level == t, 2.0 ** (8 * t), scale)
    code = jnp.where(number < count[...], (LANES + ref % LANES).astype(F32) * scale, 0.0)
    block = half_rows // 3
    parts = []
    for first in range(0, half_rows, block):
        local = row - first
        local = to_bf16(jnp.where((local >= 0) & (local < block), local, 255))
        index = to_bf16(lax.broadcasted_iota(jnp.int32, (block, width), 0))
        parts.append(
            jnp.where(
                index == jnp.broadcast_to(local, (block, width)), jnp.ones((), BF16), jnp.zeros((), BF16)
            )
        )
    rows_hot = jnp.concatenate(parts, axis=0)
    column = to_bf16(z + LANES * half)
    index = to_bf16(lax.broadcasted_iota(jnp.int32, (2 * LANES, width), 0))
    columns = jnp.where(
        index == jnp.broadcast_to(column, (2 * LANES, width)),
        jnp.broadcast_to(code.astype(BF16), (2 * LANES, width)),
        jnp.zeros((), BF16),
    )
    part = lax.dot_general(rows_hot, columns, NT, preferred_element_type=F32)

    @pl.when(step == 0)
    def _():
        marks[...] = refs[0][...] + part if len(refs) == 2 else part

    @pl.when(step > 0)
    def _():
        marks[...] += part


def split(value):
    high = value.astype(BF16)
    return high, (value - high.astype(F32)).astype(BF16)


def force_kernel(
    pair_count,
    relaxed,
    density,
    marks,
    own_speed,
    from_pair,
    from_cross,
    pair_first,
    pair_second,
    pair_gap,
    pair_normal,
    bounced,
    to_near,
    to_self,
    to_far,
    link_table,
    *scratch,
):
    width_x = relaxed.shape[1]
    slots = LANES // 2
    even_buffers, odd_buffers, sums = scratch[:4], scratch[4:8], scratch[8]
    first_of, second_of = odd_buffers[:2]
    half_rows = marks.shape[0]
    lane = lax.broadcasted_iota(jnp.int32, (1, LANES), 1)
    grad_index = lax.axis_index("grad")
    even = lax.rem(grad_index, 2) == 0
    even_flow = lax.rem(lax.axis_index("flow"), 2) == 0
    sources = [[], [], []]
    for tile in range(2):
        near = from_pair[5 + tile]
        far = from_cross[5 + tile]
        sources[0].append(jnp.where(even, far, near))
        sources[1].append(own_speed[tile])
        sources[2].append(jnp.where(even, near, far))

    def speed_row(code, k):
        row = 3 * (code // 3) + k
        return sources[code % 3][row // SUBS][row % SUBS : row % SUBS + 1, :]

    tables = []
    for k in range(3):
        rows = []
        for t in range(5):
            low = speed_row(2 * t, k)
            high = speed_row(min(2 * t + 1, NEAR - 1), k)
            rows.append(jnp.where(lane < slots, low, high))
        tables.append(rows)
    for direction in range(1, 19):
        for t in range(5):
            total = None
            for k in range(3):
                if VELOCITIES[direction][k] != 0:
                    addend = VELOCITIES[direction][k] * tables[k][t]
                    total = addend if total is None else total + addend
            link_table[direction - 1, t : t + 1, :] = total

    index_a = to_bf16(lax.broadcasted_iota(jnp.int32, (48, LANES), 0))
    index_b = to_bf16(lax.broadcasted_iota(jnp.int32, (16, LANES), 0))
    one = jnp.ones((), BF16)
    zero = jnp.zeros((), BF16)

    def spread(ref, r):
        row = ref[pl.ds(r, SUBS, stride=0), :]
        return jnp.concatenate([row, row], axis=0).astype(BF16)

    def slot_rows(buffers, r):
        first_of, second_of, value_of, rest_of = buffers
        a = spread(first_of, r)
        b = spread(second_of, r)
        high = spread(value_of, r)
        low = spread(rest_of, r)
        left = [jnp.where(index_a[16 * i : 16 * i + 16] == a, one, zero) for i in range(3)]
        mask = index_b == b
        right = [jnp.where(mask, high, zero), jnp.where(mask, low, zero)]
        return jnp.concatenate(left, axis=0), jnp.concatenate(right, axis=0)

    def hot_rows(first_row, second_row, values):
        a = jnp.broadcast_to(to_bf16(first_row), (48, LANES))
        b = jnp.broadcast_to(to_bf16(second_row), (16, LANES))
        left = jnp.where(index_a == a, one, zero)
        mask = index_b == b
        right = []
        for value in values:
            high, low = split(value)
            right.append(
                jnp.concatenate(
                    [
                        jnp.where(mask, jnp.broadcast_to(high, (16, LANES)), zero),
                        jnp.where(mask, jnp.broadcast_to(low, (16, LANES)), zero),
                    ],
                    axis=0,
                )
            )
        return left, right

    def look_up(g, buffers):
        first_of, second_of, value_of, rest_of = buffers
        for side in range(2):
            index = 2 * g + side
            half = index // 9
            first_row = (index - 9 * half) * (2 * half_rows // 18)
            weight6 = jnp.where(index < 6, 6.0 * WEIGHTS[1], 6.0 * WEIGHTS[7]).astype(F32)
            lookup = [
                jnp.broadcast_to(link_table[index, t : t + 1, :], (SUBS, LANES)) for t in range(5)
            ]
            for x in range(width_x):
                mark = marks[
                    pl.ds(pl.multiple_of(first_row + SUBS * x, SUBS), SUBS),
                    pl.ds(pl.multiple_of(half * LANES, LANES), LANES),
                ]
                live = mark > 0.0
                scale = jnp.ones((SUBS, LANES), F32)
                first = jnp.zeros((SUBS, LANES), F32)
                levels = [mark > 2.0 ** (8 * t + 6) for t in range(1, 5)]
                for t, above in enumerate(levels, 1):
                    scale = jnp.where(above, 2.0 ** (-8 * t), scale)
                    first = jnp.where(above, 8.0 * t, first)
                place = (mark * scale).astype(jnp.int32) & (LANES - 1)
                speed = jnp.take_along_axis(lookup[0], place, axis=1)
                for t, above in enumerate(levels, 1):
                    found = jnp.take_along_axis(lookup[t], place, axis=1)
                    speed = jnp.where(above, found, speed)
                leaving = relaxed[index + 1, x]
                back = leaving - weight6 * density[x] * speed
                bounced[index, x] = jnp.where(live, back, NO_LINK)
                force = leaving + back
                first = first + (place >> 4).astype(F32)
                second = (place & 15).astype(F32)
                where = side * width_x * SUBS + SUBS * x
                first_of[where : where + SUBS] = first
                second_of[where : where + SUBS] = second
                force = jnp.where(live, force, 0.0)
                high = force.astype(BF16).astype(F32)
                value_of[where : where + SUBS] = high
                rest_of[where : where + SUBS] = force - high

    def add_up(g, buffers):
        for part in range(2):
            lefts, rights = [], []
            for r in range(part * 2 * width_x * SUBS // 2, (part + 1) * 2 * width_x * SUBS // 2):
                left, right = slot_rows(buffers, r)
                lefts.append(left)
                rights.append(right)
            sums[2 * g + part] = lax.dot_general(
                jnp.concatenate(rights, axis=1),
                jnp.concatenate(lefts, axis=1),
                NT,
                preferred_element_type=F32,
            )

    look_up(0, even_buffers)

    def two_groups(i, carry):
        look_up(2 * i + 1, odd_buffers)
        add_up(2 * i, even_buffers)
        look_up(2 * i + 2, even_buffers)
        add_up(2 * i + 1, odd_buffers)
        return carry

    lax.fori_loop(0, 4, two_groups, 0)
    add_up(8, even_buffers)

    for out in (to_near, to_self, to_far):
        out[...] = jnp.zeros(out.shape, F32)
    totals = []
    for k in range(3):
        total = None
        for direction in range(1, 19):
            c = VELOCITIES[direction][k]
            if c == 0:
                continue
            addend = sums[direction - 1]
            if total is None:
                total = addend if c > 0 else -addend
            else:
                total = total + addend if c > 0 else total - addend
        totals.append(total)

    pairs = pair_first.shape[2]
    lefts = []
    rights = [[], [], []]
    for start in range(0, pairs, LANES):
        here = slice(start, start + LANES)
        first = pair_first[0, :, here]
        second = pair_second[0, :, here]
        first_wide = jnp.broadcast_to(first, (SUBS, LANES))
        place = jnp.broadcast_to(second % LANES, (SUBS, LANES))
        level = second // LANES
        gap = pair_gap[0, :, here]
        rate = None
        for k in range(3):
            table = jnp.broadcast_to(tables[k][2], (SUBS, LANES))
            first_speed = jnp.take_along_axis(table, first_wide, axis=1)[:1]
            second_speed = None
            for t in range(5):
                table = jnp.broadcast_to(tables[k][t], (SUBS, LANES))
                found = jnp.take_along_axis(table, place, axis=1)[:1]
                second_speed = found if t == 0 else jnp.where(level == t, found, second_speed)
            addend = (first_speed - second_speed) * pair_normal[k, 0, :, here]
            rate = addend if rate is None else rate + addend
        resist = LUB_COEF * (1.0 / jnp.maximum(gap, GAP_FLOOR) - 1.0 / GAP_CUTOFF)
        number = start + lane
        factor = jnp.where(number < pair_count[...], -resist * rate, 0.0)
        values = [factor * pair_normal[k, 0, :, here] for k in range(3)]
        first = first + 4 * slots
        for ref, these in ((first, values), (second, [-v for v in values])):
            left, right = hot_rows(ref // 16, ref % 16, these)
            lefts.append(left)
            for k in range(3):
                rights[k].append(right[k])
    left = jnp.concatenate(lefts, axis=1)
    for k in range(3):
        total = totals[k] + lax.dot_general(
            jnp.concatenate(rights[k], axis=1), left, NT, preferred_element_type=F32
        )
        first_of[16 * k : 16 * k + 16, 0:48] = total[:16] + total[16:]
    second_of[...] = first_of[...].T
    for k in range(3):
        line = None
        for s in range(4):
            piece = second_of[pl.ds(s, NEAR, stride=4), :]
            shift = 16 * (s - k) % LANES
            if shift:
                piece = pltpu.roll(piece, shift, axis=1)
            line = piece if line is None else jnp.where(lane >= 16 * s, piece, line)
        for g in range(3):
            row = SUBS * g + k
            low, own, high = [line[3 * f + g : 3 * f + g + 1] for f in range(3)]
            to_near[row : row + 1, :] = jnp.where(even_flow, high, low)
            to_self[row : row + 1, :] = own
            to_far[row : row + 1, :] = jnp.where(even_flow, low, high)


def stream_kernel(relaxed, bounced, from_near, from_far, from_pair, from_cross, displaced, out):
    from_left, from_right = sort_sides("flow", from_near, from_far)
    grad_index = lax.axis_index("grad")
    at_edge = (grad_index == 0) | (grad_index == lax.axis_size("grad") - 1)
    low_rows, high_rows = sort_sides(
        "grad", from_pair, [jnp.where(at_edge, displaced[i], from_cross[i]) for i in range(5)]
    )
    width_x, width_y = relaxed.shape[1], relaxed.shape[2]
    for direction, (cx, cy, cz) in enumerate(VELOCITIES):
        for x in range(width_x):
            source = x - cx
            if source < 0:
                tile = from_left[RIGHTWARD.index(direction)]
            elif source >= width_x:
                tile = from_right[LEFTWARD.index(direction)]
            else:
                tile = relaxed[direction, source]
            if cy != 0:
                tile = pltpu.roll(tile, cy % width_y, axis=0)
                row = lax.broadcasted_iota(jnp.int32, tile.shape, 0)
                if cy > 0:
                    ghost = low_rows[UPWARD.index(direction)][x : x + 1, :]
                    tile = jnp.where(row == 0, jnp.broadcast_to(ghost, tile.shape), tile)
                else:
                    ghost = high_rows[DOWNWARD.index(direction)][x : x + 1, :]
                    tile = jnp.where(row == width_y - 1, jnp.broadcast_to(ghost, tile.shape), tile)
            if cz != 0:
                tile = pltpu.roll(tile, cz % LANES, axis=1)
            if direction > 0:
                opposite = direction + 1 if direction % 2 == 1 else direction - 1
                back = bounced[opposite - 1, x]
                tile = jnp.where(back < 0.5 * NO_LINK, back, tile)
            out[direction, x] = tile


def finish_kernel(own, one, other, speed, force, moved):
    slots = force.shape[3]
    total = own[...] + one[...] + other[...]
    for k in range(3):
        line = total[k : k + 1, :slots]
        force[k, 0] = line
        moved[k, 0] = speed[k : k + 1, :slots] + INV_MASS * line


def swap(block, axis, far):
    count = lax.axis_size(axis)
    assert count % 2 == 0
    route = []
    for i in range(count):
        up = (i % 2 == 0) != far
        route.append((i, (i + (1 if up else -1)) % count))
    return lax.ppermute(block, axis, route)


def displaced_route(flow_count, grad_count, hops):
    top = grad_count - 1
    route = []
    for a in range(flow_count):
        line = a * grad_count
        route.append(((a + hops) % flow_count * grad_count + top, line))
        route.append(((a - hops) % flow_count * grad_count, line + top))
    return route


def shape_of(*dims):
    return jax.ShapeDtypeStruct(dims, F32)


def local_of(*dims):
    return pltpu.VMEM(dims, F32)


def local(*arrays):
    return [pltpu.with_memory_space_constraint(array, pltpu.VMEM) for array in arrays]


def mark_links(first, steps, half_rows, count, link_arrays, *before):
    links = link_arrays[0].shape[2]
    width = links // 2
    link_spec = pl.BlockSpec((1, 1, width), lambda i: (0, 0, i + first))
    whole = pl.BlockSpec((half_rows, 2 * LANES), lambda i: (0, 0))
    one = pl.BlockSpec((1, 1), lambda i: (0, 0))
    return pl.pallas_call(
        functools.partial(mark_kernel, first),
        name="mark",
        grid=(steps,),
        in_specs=[one, link_spec, link_spec, link_spec] + [whole] * len(before),
        out_specs=whole,
        out_shape=local_of(half_rows, 2 * LANES),
    )(count, *link_arrays, *local(*before))


def one_step(
    populations,
    le_offset,
    sphere_velocity,
    link_cell,
    link_dir,
    link_sphere,
    link_count,
    pair_first,
    pair_second,
    pair_count,
    pair_gap,
    pair_normal,
):
    width_x, width_y, depth = populations.shape[1:]
    slots = sphere_velocity.shape[3]
    flow_count = lax.axis_size("flow")
    grad_count = lax.axis_size("grad")
    assert depth == LANES and width_y == SUBS and width_x == SUBS and 2 * slots == LANES
    assert grad_count % 2 == 0

    relaxed, density, right_msg, left_msg, near_msg, far_msg, own_line = pl.pallas_call(
        collide_kernel,
        name="collide",
        in_specs=[VMEM, VMEM],
        out_specs=[VMEM] * 7,
        out_shape=[
            local_of(19, width_x, width_y, depth),
            local_of(width_x, width_y, depth),
            local_of(11, SUBS, LANES),
            local_of(11, SUBS, LANES),
            local_of(11, SUBS, LANES),
            local_of(11, SUBS, LANES),
            local_of(3, LANES),
        ],
    )(populations, sphere_velocity)

    from_far = swap(far_msg, "flow", True)
    from_near = swap(near_msg, "flow", False)

    half_rows = 9 * width_x * width_y
    link_arrays = [link_cell, link_dir, link_sphere]
    marks = mark_links(0, 1, half_rows, link_count, link_arrays)

    msg_pair, msg_cross, own_speed = pl.pallas_call(
        prepare_kernel,
        name="prepare",
        in_specs=[VMEM] * 5,
        out_specs=[VMEM] * 3,
        out_shape=[
            local_of(7, SUBS, LANES),
            local_of(7, SUBS, LANES),
            local_of(2, SUBS, LANES),
        ],
        scratch_shapes=[pltpu.VMEM((10, 3 * SUBS, LANES), F32)],
    )(le_offset.reshape(1, 1), *local(right_msg, left_msg, from_near, from_far))

    from_pair = swap(msg_pair, "grad", False)
    from_cross = swap(msg_cross, "grad", True)
    marks = mark_links(1, 1, half_rows, link_count, link_arrays, marks)

    bounced, to_near, to_self, to_far = pl.pallas_call(
        force_kernel,
        name="force",
        in_specs=[VMEM] * 11,
        out_specs=[VMEM] * 4,
        out_shape=[local_of(18, width_x, width_y, depth)] + [local_of(3 * SUBS, LANES)] * 3,
        scratch_shapes=[
            pltpu.VMEM((18, SUBS, LANES), F32),
            *[pltpu.VMEM((2 * width_x * SUBS, LANES), F32)] * 8,
            pltpu.VMEM((18, 32, 48), F32),
        ],
    )(
        pair_count,
        *local(relaxed, density, marks, own_speed, from_pair, from_cross),
        pair_first,
        pair_second,
        pair_gap,
        pair_normal,
    )

    def displace(hops, block):
        return lax.ppermute(block, ("flow", "grad"), displaced_route(flow_count, grad_count, hops))

    late_cross, _ = lax.optimization_barrier((msg_cross, to_self))
    displaced = lax.switch(
        lax.div(le_offset[0], width_x),
        [functools.partial(displace, hops) for hops in range(flow_count)],
        late_cross,
    )

    column = to_self + swap(to_far, "flow", True) + swap(to_near, "flow", False)
    even = lax.axis_index("grad") % 2 == 0
    low, high = column[:SUBS], column[2 * SUBS :]
    from_cross_force = swap(jnp.where(even, low, high), "grad", True)
    from_pair_force = swap(jnp.where(even, high, low), "grad", False)
    line = shape_of(3, 1, 1, slots)
    sphere_force, velocity_next = pl.pallas_call(
        finish_kernel,
        name="finish",
        in_specs=[VMEM] * 4,
        out_specs=[VMEM] * 2,
        out_shape=[line, line],
    )(*local(column[SUBS : 2 * SUBS], from_pair_force, from_cross_force, own_line))

    updated = pl.pallas_call(
        stream_kernel,
        name="stream",
        in_specs=[VMEM] * 7,
        out_specs=VMEM,
        out_shape=shape_of(19, width_x, width_y, depth),
    )(*local(relaxed, bounced, from_near, from_far, from_pair, from_cross, displaced))

    return updated, sphere_force, velocity_next


def solution(mesh):
    in_specs = (
        P(None, "flow", "grad", None),
        P(),
        P(None, "flow", "grad", None),
        P("flow", "grad", None),
        P("flow", "grad", None),
        P("flow", "grad", None),
        P("flow", "grad"),
        P("flow", "grad", None),
        P("flow", "grad", None),
        P("flow", "grad"),
        P("flow", "grad", None),
        P(None, "flow", "grad", None),
    )
    out_specs = (
        P(None, "flow", "grad", None),
        P(None, "flow", "grad", None),
        P(None, "flow", "grad", None),
    )
    return jax.shard_map(
        one_step, mesh=mesh, in_specs=in_specs, out_specs=out_specs, check_vma=False
    )
```

```python
import functools

import jax
import jax.numpy as jnp
from jax import lax
from jax.experimental import pallas as pl
from jax.experimental.pallas import tpu as pltpu
from jax.sharding import PartitionSpec as P


VELOCITIES = [
    (0, 0, 0),
    (1, 0, 0),
    (-1, 0, 0),
    (0, 1, 0),
    (0, -1, 0),
    (0, 0, 1),
    (0, 0, -1),
    (1, 1, 0),
    (-1, -1, 0),
    (1, -1, 0),
    (-1, 1, 0),
    (1, 0, 1),
    (-1, 0, -1),
    (1, 0, -1),
    (-1, 0, 1),
    (0, 1, 1),
    (0, -1, -1),
    (0, 1, -1),
    (0, -1, 1),
]
WEIGHTS = [1.0 / 3.0] + [1.0 / 18.0] * 6 + [1.0 / 36.0] * 12
UPWARD = [3, 7, 10, 15, 17]
DOWNWARD = [4, 8, 9, 16, 18]
RIGHTWARD = [1, 7, 9, 11, 13]
LEFTWARD = [2, 8, 10, 12, 14]
RELAX_TIME = 0.8
SHEAR_SPEED = 0.1
LUB_COEF = 0.5
GAP_FLOOR = 0.1
GAP_CUTOFF = 1.0
INV_MASS = 1.0 / 523.6
LANES = 128
SUBS = 8
NEAR = 9
NO_LINK = 1e30
BF16 = jnp.bfloat16
F32 = jnp.float32
NT = (((1,), (1,)), ((), ()))

VMEM = pl.BlockSpec(memory_space=pltpu.VMEM)


def collide_kernel(
    pops, speed, relaxed, density, right_msg, left_msg, near_msg, far_msg, own_line
):
    width_x, width_y = pops.shape[1], pops.shape[2]
    slots = speed.shape[3]
    for x in range(width_x):
        current = [pops[d, x] for d in range(19)]
        total = functools.reduce(lambda p, q: p + q, current)
        density[x] = total
        inverse = 1.0 / total
        speeds = []
        for axis_id in range(3):
            running = None
            for direction, vector in enumerate(VELOCITIES):
                if vector[axis_id] == 0:
                    continue
                if running is None:
                    running = current[direction]
                elif vector[axis_id] > 0:
                    running = running + current[direction]
                else:
                    running = running - current[direction]
            speeds.append(running * inverse)
        base = 1.0 - 1.5 * (
            speeds[0] * speeds[0] + speeds[1] * speeds[1] + speeds[2] * speeds[2]
        )
        for direction, vector in enumerate(VELOCITIES):
            c_dot = None
            for axis_id in range(3):
                if vector[axis_id] != 0:
                    addend = vector[axis_id] * speeds[axis_id]
                    c_dot = addend if c_dot is None else c_dot + addend
            shape = base if c_dot is None else base + c_dot * (3.0 + 4.5 * c_dot)
            equil = WEIGHTS[direction] * total * shape
            value = current[direction] - (current[direction] - equil) * (1.0 / RELAX_TIME)
            relaxed[direction, x] = value
            if x == width_x - 1 and direction in RIGHTWARD:
                right_msg[RIGHTWARD.index(direction)] = value
            if x == 0 and direction in LEFTWARD:
                left_msg[LEFTWARD.index(direction)] = value
            if direction in UPWARD:
                left_msg[5 + UPWARD.index(direction), x : x + 1, :] = value[width_y - 1 :, :]
            if direction in DOWNWARD:
                right_msg[5 + DOWNWARD.index(direction), x : x + 1, :] = value[:1, :]
    right_msg[10] = jnp.zeros((SUBS, LANES), F32)
    left_msg[10] = jnp.zeros((SUBS, LANES), F32)
    for k in range(3):
        row = speed[k, 0]
        twice = jnp.concatenate([row] * (LANES // slots), axis=1)
        right_msg[10, k : k + 1, :] = twice
        left_msg[10, k : k + 1, :] = twice
        own_line[k : k + 1, :] = twice
    even = lax.rem(lax.axis_index("flow"), 2) == 0
    for i in range(11):
        near_msg[i] = jnp.where(even, right_msg[i], left_msg[i])
        far_msg[i] = jnp.where(even, left_msg[i], right_msg[i])


def sort_sides(axis, near, far):
    even = lax.rem(lax.axis_index(axis), 2) == 0
    count = len(far) if isinstance(far, list) else far.shape[0]
    near = [near[i] for i in range(count)]
    far = [far[i] for i in range(count)]
    lower = [jnp.where(even, q, p) for p, q in zip(near, far)]
    higher = [jnp.where(even, p, q) for p, q in zip(near, far)]
    return lower, higher


def prepare_kernel(
    offset, own_right, own_left, from_near, from_far, msg_pair, msg_cross, own_speed, rows
):
    width_x = own_right.shape[1]
    from_left, from_right = sort_sides("flow", from_near, from_far)
    grad_index = lax.axis_index("grad")
    at_top = grad_index == lax.axis_size("grad") - 1
    at_bottom = grad_index == 0
    even = lax.rem(grad_index, 2) == 0
    rest = jnp.broadcast_to(lax.rem(offset[...], width_x), (width_x, LANES))
    up_rest = jnp.where(at_top, rest, 0)
    down_rest = jnp.where(at_bottom, rest, 0)
    top_boost = jnp.where(at_top, 1.0, 0.0)
    bottom_boost = jnp.where(at_bottom, 1.0, 0.0)

    def window(j, start, sign, amount):
        moved = rows[j, start : start + width_x, :]
        for r in range(1, width_x):
            first = start + sign * r
            moved = jnp.where(amount == r, rows[j, first : first + width_x, :], moved)
        return moved

    ups = []
    for j, direction in enumerate(UPWARD):
        step = VELOCITIES[direction][0]
        boost = 6.0 * WEIGHTS[direction] * step * SHEAR_SPEED
        rows[j, SUBS : 2 * SUBS] = own_left[5 + j]
        rows[j, 2 * SUBS : 3 * SUBS] = from_right[5 + j]
        if step > 0:
            slab = from_left[RIGHTWARD.index(direction)]
            rows[j, SUBS - 1 : SUBS] = slab[SUBS - 1 :, :]
        moved = window(j, SUBS - step, 1, up_rest)
        if step != 0:
            moved = moved - boost * top_boost
        ups.append(moved)
    for j, direction in enumerate(DOWNWARD):
        step = VELOCITIES[direction][0]
        boost = 6.0 * WEIGHTS[direction] * step * SHEAR_SPEED
        rows[5 + j, :SUBS] = from_left[5 + j]
        rows[5 + j, SUBS : 2 * SUBS] = own_right[5 + j]
        if step < 0:
            slab = from_right[LEFTWARD.index(direction)]
            rows[5 + j, 2 * SUBS : 2 * SUBS + 1] = slab[:1, :]
        moved = window(5 + j, SUBS - step, -1, down_rest)
        if step != 0:
            moved = moved + boost * bottom_boost
        msg_pair[j] = jnp.where(even, ups[j], moved)
        msg_cross[j] = jnp.where(even, moved, ups[j])
    three = [from_left[10], own_right[10], from_right[10]]
    for out, first in ((msg_pair, 5), (msg_cross, 5), (own_speed, 0)):
        for f in range(3):
            for k in range(3):
                row = 3 * f + k
                out[first + row // SUBS, row % SUBS : row % SUBS + 1, :] = three[f][k : k + 1, :]


def to_bf16(value):
    return value.astype(F32).astype(BF16)


def mark_kernel(first_step, count, cell, direction, sphere, *refs):
    marks = refs[-1]
    step = pl.program_id(0)
    width = cell.shape[2]
    half_rows = marks.shape[0]
    q = cell[0]
    ref = sphere[0]
    row = (direction[0] - 1) * (2 * half_rows // 18) + q // LANES
    z = q % LANES
    half = (row >= half_rows).astype(jnp.int32)
    row = row - half * half_rows
    number = (first_step + step) * width + lax.broadcasted_iota(jnp.int32, (1, width), 1)
    level = ref // LANES
    scale = jnp.where(level == 0, 1.0, 0.0)
    for t in range(1, 5):
        scale = jnp.where(level == t, 2.0 ** (8 * t), scale)
    code = jnp.where(number < count[...], (LANES + ref % LANES).astype(F32) * scale, 0.0)
    block = half_rows // 3
    parts = []
    for first in range(0, half_rows, block):
        local = row - first
        local = to_bf16(jnp.where((local >= 0) & (local < block), local, 255))
        index = to_bf16(lax.broadcasted_iota(jnp.int32, (block, width), 0))
        parts.append(
            jnp.where(
                index == jnp.broadcast_to(local, (block, width)), jnp.ones((), BF16), jnp.zeros((), BF16)
            )
        )
    rows_hot = jnp.concatenate(parts, axis=0)
    column = to_bf16(z + LANES * half)
    index = to_bf16(lax.broadcasted_iota(jnp.int32, (2 * LANES, width), 0))
    columns = jnp.where(
        index == jnp.broadcast_to(column, (2 * LANES, width)),
        jnp.broadcast_to(code.astype(BF16), (2 * LANES, width)),
        jnp.zeros((), BF16),
    )
    part = lax.dot_general(rows_hot, columns, NT, preferred_element_type=F32)

    @pl.when(step == 0)
    def _():
        marks[...] = refs[0][...] + part if len(refs) == 2 else part

    @pl.when(step > 0)
    def _():
        marks[...] += part


def split(value):
    high = value.astype(BF16)
    return high, (value - high.astype(F32)).astype(BF16)


def force_kernel(
    pair_count,
    relaxed,
    density,
    marks,
    own_speed,
    from_pair,
    from_cross,
    pair_first,
    pair_second,
    pair_gap,
    pair_normal,
    bounced,
    to_near,
    to_self,
    to_far,
    link_table,
    *scratch,
):
    width_x = relaxed.shape[1]
    slots = LANES // 2
    even_buffers, odd_buffers, sums = scratch[:4], scratch[4:8], scratch[8]
    first_of, second_of = odd_buffers[:2]
    half_rows = marks.shape[0]
    lane = lax.broadcasted_iota(jnp.int32, (1, LANES), 1)
    grad_index = lax.axis_index("grad")
    even = lax.rem(grad_index, 2) == 0
    even_flow = lax.rem(lax.axis_index("flow"), 2) == 0
    sources = [[], [], []]
    for tile in range(2):
        near = from_pair[5 + tile]
        far = from_cross[5 + tile]
        sources[0].append(jnp.where(even, far, near))
        sources[1].append(own_speed[tile])
        sources[2].append(jnp.where(even, near, far))

    def speed_row(code, k):
        row = 3 * (code // 3) + k
        return sources[code % 3][row // SUBS][row % SUBS : row % SUBS + 1, :]

    tables = []
    for k in range(3):
        rows = []
        for t in range(5):
            low = speed_row(2 * t, k)
            high = speed_row(min(2 * t + 1, NEAR - 1), k)
            rows.append(jnp.where(lane < slots, low, high))
        tables.append(rows)
    for direction in range(1, 19):
        for t in range(5):
            total = None
            for k in range(3):
                if VELOCITIES[direction][k] != 0:
                    addend = VELOCITIES[direction][k] * tables[k][t]
                    total = addend if total is None else total + addend
            link_table[direction - 1, t : t + 1, :] = total

    index_a = to_bf16(lax.broadcasted_iota(jnp.int32, (48, LANES), 0))
    index_b = to_bf16(lax.broadcasted_iota(jnp.int32, (16, LANES), 0))
    one = jnp.ones((), BF16)
    zero = jnp.zeros((), BF16)

    def spread(ref, r):
        row = ref[pl.ds(r, SUBS, stride=0), :]
        return jnp.concatenate([row, row], axis=0).astype(BF16)

    def slot_rows(buffers, r):
        first_of, second_of, value_of, rest_of = buffers
        a = spread(first_of, r)
        b = spread(second_of, r)
        high = spread(value_of, r)
        low = spread(rest_of, r)
        left = [jnp.where(index_a[16 * i : 16 * i + 16] == a, one, zero) for i in range(3)]
        mask = index_b == b
        right = [jnp.where(mask, high, zero), jnp.where(mask, low, zero)]
        return jnp.concatenate(left, axis=0), jnp.concatenate(right, axis=0)

    def hot_rows(first_row, second_row, values):
        a = jnp.broadcast_to(to_bf16(first_row), (48, LANES))
        b = jnp.broadcast_to(to_bf16(second_row), (16, LANES))
        left = jnp.where(index_a == a, one, zero)
        mask = index_b == b
        right = []
        for value in values:
            high, low = split(value)
            right.append(
                jnp.concatenate(
                    [
                        jnp.where(mask, jnp.broadcast_to(high, (16, LANES)), zero),
                        jnp.where(mask, jnp.broadcast_to(low, (16, LANES)), zero),
                    ],
                    axis=0,
                )
            )
        return left, right

    def look_up(g, buffers):
        first_of, second_of, value_of, rest_of = buffers
        for side in range(2):
            index = 2 * g + side
            half = index // 9
            first_row = (index - 9 * half) * (2 * half_rows // 18)
            weight6 = jnp.where(index < 6, 6.0 * WEIGHTS[1], 6.0 * WEIGHTS[7]).astype(F32)
            lookup = [
                jnp.broadcast_to(link_table[index, t : t + 1, :], (SUBS, LANES)) for t in range(5)
            ]
            for x in range(width_x):
                mark = marks[
                    pl.ds(pl.multiple_of(first_row + SUBS * x, SUBS), SUBS),
                    pl.ds(pl.multiple_of(half * LANES, LANES), LANES),
                ]
                live = mark > 0.0
                scale = jnp.ones((SUBS, LANES), F32)
                first = jnp.zeros((SUBS, LANES), F32)
                levels = [mark > 2.0 ** (8 * t + 6) for t in range(1, 5)]
                for t, above in enumerate(levels, 1):
                    scale = jnp.where(above, 2.0 ** (-8 * t), scale)
                    first = jnp.where(above, 8.0 * t, first)
                place = (mark * scale).astype(jnp.int32) & (LANES - 1)
                speed = jnp.take_along_axis(lookup[0], place, axis=1)
                for t, above in enumerate(levels, 1):
                    found = jnp.take_along_axis(lookup[t], place, axis=1)
                    speed = jnp.where(above, found, speed)
                leaving = relaxed[index + 1, x]
                back = leaving - weight6 * density[x] * speed
                bounced[index, x] = jnp.where(live, back, NO_LINK)
                force = leaving + back
                first = first + (place >> 4).astype(F32)
                second = (place & 15).astype(F32)
                where = side * width_x * SUBS + SUBS * x
                first_of[where : where + SUBS] = first
                second_of[where : where + SUBS] = second
                force = jnp.where(live, force, 0.0)
                high = force.astype(BF16).astype(F32)
                value_of[where : where + SUBS] = high
                rest_of[where : where + SUBS] = force - high

    def add_up(g, buffers):
        for part in range(2):
            lefts, rights = [], []
            for r in range(part * 2 * width_x * SUBS // 2, (part + 1) * 2 * width_x * SUBS // 2):
                left, right = slot_rows(buffers, r)
                lefts.append(left)
                rights.append(right)
            sums[2 * g + part] = lax.dot_general(
                jnp.concatenate(rights, axis=1),
                jnp.concatenate(lefts, axis=1),
                NT,
                preferred_element_type=F32,
            )

    look_up(0, even_buffers)

    def two_groups(i, carry):
        look_up(2 * i + 1, odd_buffers)
        add_up(2 * i, even_buffers)
        look_up(2 * i + 2, even_buffers)
        add_up(2 * i + 1, odd_buffers)
        return carry

    lax.fori_loop(0, 4, two_groups, 0)
    add_up(8, even_buffers)

    for out in (to_near, to_self, to_far):
        out[...] = jnp.zeros(out.shape, F32)
    totals = []
    for k in range(3):
        total = None
        for direction in range(1, 19):
            c = VELOCITIES[direction][k]
            if c == 0:
                continue
            addend = sums[direction - 1]
            if total is None:
                total = addend if c > 0 else -addend
            else:
                total = total + addend if c > 0 else total - addend
        totals.append(total)

    pairs = pair_first.shape[2]
    lefts = []
    rights = [[], [], []]
    for start in range(0, pairs, LANES):
        here = slice(start, start + LANES)
        first = pair_first[0, :, here]
        second = pair_second[0, :, here]
        first_wide = jnp.broadcast_to(first, (SUBS, LANES))
        place = jnp.broadcast_to(second % LANES, (SUBS, LANES))
        level = second // LANES
        gap = pair_gap[0, :, here]
        rate = None
        for k in range(3):
            table = jnp.broadcast_to(tables[k][2], (SUBS, LANES))
            first_speed = jnp.take_along_axis(table, first_wide, axis=1)[:1]
            second_speed = None
            for t in range(5):
                table = jnp.broadcast_to(tables[k][t], (SUBS, LANES))
                found = jnp.take_along_axis(table, place, axis=1)[:1]
                second_speed = found if t == 0 else jnp.where(level == t, found, second_speed)
            addend = (first_speed - second_speed) * pair_normal[k, 0, :, here]
            rate = addend if rate is None else rate + addend
        resist = LUB_COEF * (1.0 / jnp.maximum(gap, GAP_FLOOR) - 1.0 / GAP_CUTOFF)
        number = start + lane
        factor = jnp.where(number < pair_count[...], -resist * rate, 0.0)
        values = [factor * pair_normal[k, 0, :, here] for k in range(3)]
        first = first + 4 * slots
        for ref, these in ((first, values), (second, [-v for v in values])):
            left, right = hot_rows(ref // 16, ref % 16, these)
            lefts.append(left)
            for k in range(3):
                rights[k].append(right[k])
    left = jnp.concatenate(lefts, axis=1)
    for k in range(3):
        total = totals[k] + lax.dot_general(
            jnp.concatenate(rights[k], axis=1), left, NT, preferred_element_type=F32
        )
        first_of[16 * k : 16 * k + 16, 0:48] = total[:16] + total[16:]
    second_of[...] = first_of[...].T
    for k in range(3):
        line = None
        for s in range(4):
            piece = second_of[pl.ds(s, NEAR, stride=4), :]
            shift = 16 * (s - k) % LANES
            if shift:
                piece = pltpu.roll(piece, shift, axis=1)
            line = piece if line is None else jnp.where(lane >= 16 * s, piece, line)
        for g in range(3):
            row = SUBS * g + k
            low, own, high = [line[3 * f + g : 3 * f + g + 1] for f in range(3)]
            to_near[row : row + 1, :] = jnp.where(even_flow, high, low)
            to_self[row : row + 1, :] = own
            to_far[row : row + 1, :] = jnp.where(even_flow, low, high)


def stream_kernel(relaxed, bounced, from_near, from_far, from_pair, from_cross, displaced, out):
    from_left, from_right = sort_sides("flow", from_near, from_far)
    grad_index = lax.axis_index("grad")
    at_edge = (grad_index == 0) | (grad_index == lax.axis_size("grad") - 1)
    low_rows, high_rows = sort_sides(
        "grad", from_pair, [jnp.where(at_edge, displaced[i], from_cross[i]) for i in range(5)]
    )
    width_x, width_y = relaxed.shape[1], relaxed.shape[2]
    for direction, (cx, cy, cz) in enumerate(VELOCITIES):
        for x in range(width_x):
            source = x - cx
            if source < 0:
                tile = from_left[RIGHTWARD.index(direction)]
            elif source >= width_x:
                tile = from_right[LEFTWARD.index(direction)]
            else:
                tile = relaxed[direction, source]
            if cy != 0:
                tile = pltpu.roll(tile, cy % width_y, axis=0)
                row = lax.broadcasted_iota(jnp.int32, tile.shape, 0)
                if cy > 0:
                    ghost = low_rows[UPWARD.index(direction)][x : x + 1, :]
                    tile = jnp.where(row == 0, jnp.broadcast_to(ghost, tile.shape), tile)
                else:
                    ghost = high_rows[DOWNWARD.index(direction)][x : x + 1, :]
                    tile = jnp.where(row == width_y - 1, jnp.broadcast_to(ghost, tile.shape), tile)
            if cz != 0:
                tile = pltpu.roll(tile, cz % LANES, axis=1)
            if direction > 0:
                opposite = direction + 1 if direction % 2 == 1 else direction - 1
                back = bounced[opposite - 1, x]
                tile = jnp.where(back < 0.5 * NO_LINK, back, tile)
            out[direction, x] = tile


def finish_kernel(own, one, other, speed, force, moved):
    slots = force.shape[3]
    total = own[...] + one[...] + other[...]
    for k in range(3):
        line = total[k : k + 1, :slots]
        force[k, 0] = line
        moved[k, 0] = speed[k : k + 1, :slots] + INV_MASS * line


def swap(block, axis, far):
    count = lax.axis_size(axis)
    assert count % 2 == 0
    route = []
    for i in range(count):
        up = (i % 2 == 0) != far
        route.append((i, (i + (1 if up else -1)) % count))
    return lax.ppermute(block, axis, route)


def displaced_route(flow_count, grad_count, hops):
    top = grad_count - 1
    route = []
    for a in range(flow_count):
        line = a * grad_count
        route.append(((a + hops) % flow_count * grad_count + top, line))
        route.append(((a - hops) % flow_count * grad_count, line + top))
    return route


def shape_of(*dims):
    return jax.ShapeDtypeStruct(dims, F32)


def local_of(*dims):
    return pltpu.VMEM(dims, F32)


def local(*arrays):
    return [pltpu.with_memory_space_constraint(array, pltpu.VMEM) for array in arrays]


def mark_links(first, steps, half_rows, count, link_arrays, *before):
    links = link_arrays[0].shape[2]
    width = links // 2
    link_spec = pl.BlockSpec((1, 1, width), lambda i: (0, 0, i + first))
    whole = pl.BlockSpec((half_rows, 2 * LANES), lambda i: (0, 0))
    one = pl.BlockSpec((1, 1), lambda i: (0, 0))
    return pl.pallas_call(
        functools.partial(mark_kernel, first),
        name="mark",
        grid=(steps,),
        in_specs=[one, link_spec, link_spec, link_spec] + [whole] * len(before),
        out_specs=whole,
        out_shape=local_of(half_rows, 2 * LANES),
    )(count, *link_arrays, *local(*before))


def one_step(
    populations,
    le_offset,
    sphere_velocity,
    link_cell,
    link_dir,
    link_sphere,
    link_count,
    pair_first,
    pair_second,
    pair_count,
    pair_gap,
    pair_normal,
):
    width_x, width_y, depth = populations.shape[1:]
    slots = sphere_velocity.shape[3]
    flow_count = lax.axis_size("flow")
    grad_count = lax.axis_size("grad")
    assert depth == LANES and width_y == SUBS and width_x == SUBS and 2 * slots == LANES
    assert grad_count % 2 == 0

    relaxed, density, right_msg, left_msg, near_msg, far_msg, own_line = pl.pallas_call(
        collide_kernel,
        name="collide",
        in_specs=[VMEM, VMEM],
        out_specs=[VMEM] * 7,
        out_shape=[
            local_of(19, width_x, width_y, depth),
            local_of(width_x, width_y, depth),
            local_of(11, SUBS, LANES),
            local_of(11, SUBS, LANES),
            local_of(11, SUBS, LANES),
            local_of(11, SUBS, LANES),
            local_of(3, LANES),
        ],
    )(populations, sphere_velocity)

    from_far = swap(far_msg, "flow", True)
    from_near = swap(near_msg, "flow", False)

    half_rows = 9 * width_x * width_y
    link_arrays = [link_cell, link_dir, link_sphere]
    marks = mark_links(0, 1, half_rows, link_count, link_arrays)

    msg_pair, msg_cross, own_speed = pl.pallas_call(
        prepare_kernel,
        name="prepare",
        in_specs=[VMEM] * 5,
        out_specs=[VMEM] * 3,
        out_shape=[
            local_of(7, SUBS, LANES),
            local_of(7, SUBS, LANES),
            local_of(2, SUBS, LANES),
        ],
        scratch_shapes=[pltpu.VMEM((10, 3 * SUBS, LANES), F32)],
    )(le_offset.reshape(1, 1), *local(right_msg, left_msg, from_near, from_far))

    from_pair = swap(msg_pair, "grad", False)
    from_cross = swap(msg_cross, "grad", True)
    marks = mark_links(1, 1, half_rows, link_count, link_arrays, marks)

    bounced, to_near, to_self, to_far = pl.pallas_call(
        force_kernel,
        name="force",
        in_specs=[VMEM] * 11,
        out_specs=[VMEM] * 4,
        out_shape=[local_of(18, width_x, width_y, depth)] + [local_of(3 * SUBS, LANES)] * 3,
        scratch_shapes=[
            pltpu.VMEM((18, SUBS, LANES), F32),
            *[pltpu.VMEM((2 * width_x * SUBS, LANES), F32)] * 8,
            pltpu.VMEM((18, 32, 48), F32),
        ],
    )(
        pair_count,
        *local(relaxed, density, marks, own_speed, from_pair, from_cross),
        pair_first,
        pair_second,
        pair_gap,
        pair_normal,
    )

    def tail(hops, to_near, to_self, to_far, msg_cross, own_line, *fields):
        far = swap(to_far, "flow", True)
        near = swap(to_near, "flow", False)
        route = displaced_route(flow_count, grad_count, hops)
        displaced = lax.ppermute(msg_cross, ("flow", "grad"), route)
        column = to_self + far + near
        even = lax.axis_index("grad") % 2 == 0
        low, high = column[:SUBS], column[2 * SUBS :]
        to_cross = jnp.where(even, low, high)
        to_pair = jnp.where(even, high, low)
        from_pair_force = swap(to_pair, "grad", False)
        from_cross_force = swap(to_cross, "grad", True)
        updated = pl.pallas_call(
            stream_kernel,
            name="stream",
            in_specs=[VMEM] * 7,
            out_specs=VMEM,
            out_shape=shape_of(19, width_x, width_y, depth),
        )(*local(*fields, displaced))
        line = shape_of(3, 1, 1, slots)
        sphere_force, velocity_next = pl.pallas_call(
            finish_kernel,
            name="finish",
            in_specs=[VMEM] * 4,
            out_specs=[VMEM] * 2,
            out_shape=[line, line],
        )(*local(column[SUBS : 2 * SUBS], from_pair_force, from_cross_force, own_line))
        return updated, sphere_force, velocity_next

    return lax.switch(
        lax.div(le_offset[0], width_x),
        [functools.partial(tail, hops) for hops in range(flow_count)],
        to_near,
        to_self,
        to_far,
        msg_cross,
        own_line,
        relaxed,
        bounced,
        from_near,
        from_far,
        from_pair,
        from_cross,
    )


def solution(mesh):
    in_specs = (
        P(None, "flow", "grad", None),
        P(),
        P(None, "flow", "grad", None),
        P("flow", "grad", None),
        P("flow", "grad", None),
        P("flow", "grad", None),
        P("flow", "grad"),
        P("flow", "grad", None),
        P("flow", "grad", None),
        P("flow", "grad"),
        P("flow", "grad", None),
        P(None, "flow", "grad", None),
    )
    out_specs = (
        P(None, "flow", "grad", None),
        P(None, "flow", "grad", None),
        P(None, "flow", "grad", None),
    )
    return jax.shard_map(
        one_step, mesh=mesh, in_specs=in_specs, out_specs=out_specs, check_vma=False
    )
```
